32 devices in a mesh: dp: 8 (over z, x), seq: 4 (over y, core).
Axes of the slice: x: 2, y: 2, z: 4, core: 2. Of those that a mesh axis runs over, the one named last changes fastest.
Arguments:
- hidden_in: bfloat16 [32, 512, 1024], P('dp', 'seq'), may hold values from -6 to 6
- lengths: int32 [32], P('dp'), may hold values from 8 to 512, as said below
- w_query: bfloat16 [1024, 1024], replicated, may hold values from -0.375 to 0.375
- w_key: bfloat16 [1024, 1024], replicated, may hold values from -0.1875 to 0.1875
- w_value: bfloat16 [1024, 1024], replicated, may hold values from -0.1875 to 0.1875
- w_output: bfloat16 [1024, 1024], replicated, may hold values from -0.75 to 0.75
- gain_attn: float32 [1024], replicated, may hold values from 0.1 to 1.9
- w_expand: bfloat16 [1024, 4096], replicated, may hold values from -0.1875 to 0.1875
- w_contract: bfloat16 [4096, 1024], replicated, may hold values from -0.09375 to 0.09375
- gain_ffn: float32 [1024], replicated, may hold values from 0.1 to 1.9
- bias_query: float32 [1024], replicated, may hold values from -3 to 3
- bias_value: float32 [1024], replicated, may hold values from -0.3 to 0.3
- bias_output: float32 [1024], replicated, may hold values from -3 to 3
- shift_attn: float32 [1024], replicated, may hold values from -3 to 3
- bias_expand: float32 [4096], replicated, may hold values from -3 to 3
- bias_contract: float32 [1024], replicated, may hold values from -3 to 3
- shift_ffn: float32 [1024], replicated, may hold values from -3 to 3
- cotangent: bfloat16 [32, 512, 1024], P('dp', 'seq')
Outputs:
- output: bfloat16 [32, 512, 1024], P('dp', 'seq')
- grad_input: bfloat16 [32, 512, 1024], P('dp', 'seq')
- grad_bias_query: float32 [1024], replicated
- grad_bias_value: float32 [1024], replicated
- grad_bias_output: float32 [1024], replicated
- grad_shift_attn: float32 [1024], replicated
- grad_bias_expand: float32 [4096], replicated
- grad_bias_contract: float32 [1024], replicated
- grad_shift_ffn: float32 [1024], replicated
The draws below stay inside these ranges and needn't reach their ends.
Inputs may be any that keep to these rules, and one draw needn't show every extreme that they name: `lengths`: keys at positions at or beyond a sequence's length are masked; some sequence has length 512 and some has length 8.
All inputs are finite; a program needn't handle non-finite values.
Results may differ from the reference program's by a relative error of at most 0.013.
Values may be sent and summed in bfloat16 or wider, within the bound.
A program may use at most 192 MiB of HBM per device.

```python
import jax
import jax.numpy as jnp
from jax import lax

D = 1024
HEADS = 16
HEAD = 64
FF = 4096
SEQ_LEN = 512
SEQ_DEV = 4
SEQS = 32
TOKENS = 16384


def draw_lengths(key, part):
    first, second = jax.random.split(jax.random.fold_in(key, 11))
    lens = jax.random.randint(first, (SEQS,), 8, SEQ_LEN + 1, dtype=jnp.int32)
    order = jax.random.permutation(second, SEQS)
    lens = lens.at[order[0]].set(SEQ_LEN).at[order[1]].set(8)
    return lens.astype(jnp.int32)


def draw_cotangent(key, part):
    first = jax.random.fold_in(jax.random.fold_in(key, 23), 0)
    rising = jnp.arange(SEQS, dtype=jnp.float32) / (SEQS - 1.0)
    base = jax.random.normal(first, (SEQS, SEQ_LEN, D), jnp.float32)
    factor = 1.0 + 2.0 * rising
    return (base * factor[:, None, None]).astype(jnp.bfloat16)


def block_scale(key, extent, pieces, least, high):
    level, own = 1.0, jax.random.fold_in(key, 6)
    for dim, blocks in pieces:
        heights = jnp.exp(jax.random.uniform(jax.random.fold_in(own, dim), (blocks,), jnp.float32, least / len(pieces), high / len(pieces)))
        level = level * jnp.repeat(heights, extent[dim] // blocks).reshape([-1 if axis == dim else 1 for axis in range(len(extent))])
    return level


def scatter_about(stream_key, dims, scale, reach, pieces=(), held_as=jnp.bfloat16):
    drawn = scale * jax.random.normal(stream_key, dims, jnp.float32)
    if pieces:
        drawn = drawn * block_scale(stream_key, dims, pieces, -0.22, 0.18)
    return jnp.clip(drawn, -reach, reach).astype(held_as)


def setup_inputs(seed: int = 0) -> dict:
    splits = jax.random.split(jax.random.key(seed), 19)
    hidden_in = scatter_about(splits[0], (SEQS, SEQ_LEN, D), 1.0, 6.0, ((0, 8), (1, 4)))
    lengths = draw_lengths(jax.random.fold_in(splits[18], 71), 0)
    w_query = scatter_about(splits[2], (D, D), (D // 4) ** -0.5, 0.375)
    w_key = scatter_about(splits[3], (D, D), D ** -0.5, 0.1875)
    w_value = scatter_about(splits[4], (D, D), D ** -0.5, 0.1875)
    w_output = scatter_about(splits[5], (D, D), (D // 16) ** -0.5, 0.75)
    gain_attn = jnp.clip(1.0 + 0.18 * jax.random.normal(splits[6], (D,), jnp.float32), 0.1, 1.9)
    w_expand = scatter_about(splits[7], (D, FF), D ** -0.5, 0.1875)
    w_contract = scatter_about(splits[8], (FF, D), FF ** -0.5, 0.09375)
    gain_ffn = jnp.clip(1.0 + 0.18 * jax.random.normal(splits[9], (D,), jnp.float32), 0.1, 1.9)
    bias_query = scatter_about(splits[10], (D,), 0.5, 3.0, (), jnp.float32)
    bias_value = scatter_about(splits[11], (D,), 0.05, 0.3, (), jnp.float32)
    bias_output = scatter_about(splits[12], (D,), 0.5, 3.0, (), jnp.float32)
    shift_attn = scatter_about(splits[13], (D,), 0.5, 3.0, (), jnp.float32)
    bias_expand = scatter_about(splits[14], (FF,), 0.5, 3.0, (), jnp.float32)
    bias_contract = scatter_about(splits[15], (D,), 0.5, 3.0, (), jnp.float32)
    shift_ffn = scatter_about(splits[16], (D,), 0.5, 3.0, (), jnp.float32)
    cotangent = draw_cotangent(jax.random.fold_in(splits[18], 71), 0)
    return {"hidden_in": hidden_in, "lengths": lengths, "w_query": w_query, "w_key": w_key, "w_value": w_value, "w_output": w_output, "gain_attn": gain_attn, "w_expand": w_expand, "w_contract": w_contract, "gain_ffn": gain_ffn, "bias_query": bias_query, "bias_value": bias_value, "bias_output": bias_output, "shift_attn": shift_attn, "bias_expand": bias_expand, "bias_contract": bias_contract, "shift_ffn": shift_ffn, "cotangent": cotangent}


@jax.custom_vjp
def low(v):
    return lax.optimization_barrier(v.astype(jnp.bfloat16)).astype(jnp.float32)

@jax.custom_vjp
def low_back(v):
    return v

def low_keep(v):
    return (low(v), None)

def low_pass(kept, grad):
    return (grad,)

def back_keep(v):
    return (v, None)

def back_low(kept, grad):
    return (low(grad),)
low.defvjp(low_keep, low_pass)
low_back.defvjp(back_keep, back_low)
NEG = -1e+30
EPSILON = 1e-12
HIGH = lax.Precision.HIGHEST

def matmul(left, right):
    return jnp.dot(left, right, precision=HIGH)

def layer_norm(resid, gain, shift):
    center = resid - lax.optimization_barrier(jnp.mean(resid, -1, keepdims=True))
    spread = lax.optimization_barrier(jnp.mean(center * center, -1, keepdims=True))
    return center * lax.rsqrt(spread + EPSILON) * gain + shift

def forward(params, inputs, lens, weights, gain_attn, gain_ffn):
    bias_query, bias_value, bias_output, shift_attn, bias_expand, bias_contract, shift_ffn = params
    w_query, w_key, w_value, w_output, w_expand, w_contract = weights
    group = inputs.shape[0]
    shape4 = (group, SEQ_LEN, HEADS, HEAD)
    query = low(low_back(matmul(inputs, w_query) + bias_query)).reshape(shape4)
    keys = low(low_back(matmul(inputs, w_key))).reshape(shape4)
    values = low(low_back(matmul(inputs, w_value) + bias_value)).reshape(shape4)
    scores = low_back(jnp.einsum('gqhd,gkhd->ghqk', query, keys, precision=HIGH) * HEAD ** (-0.5))
    position = jnp.arange(SEQ_LEN, dtype=jnp.int32)
    valid = (position[None, :] < lens[:, None])[:, None, None, :]
    scores = jnp.where(valid, scores, NEG)
    probs = low(jax.nn.softmax(scores, axis=-1))
    context = low(low_back(jnp.einsum('ghqk,gkhd->gqhd', probs, values, precision=HIGH)))
    context = context.reshape(group, SEQ_LEN, D)
    attn_out = low_back(matmul(context, w_output) + bias_output)
    normed_one = layer_norm(inputs + attn_out, gain_attn, shift_attn)
    expand = low_back(matmul(low(normed_one), w_expand) + bias_expand)
    hidden = low(jax.nn.gelu(expand, approximate=False))
    branch = low_back(matmul(hidden, w_contract) + bias_contract)
    return layer_norm(normed_one + branch, gain_ffn, shift_ffn)

def reference(hidden_in, lengths, w_query, w_key, w_value, w_output, gain_attn, w_expand, w_contract, gain_ffn, bias_query, bias_value, bias_output, shift_attn, bias_expand, bias_contract, shift_ffn, cotangent):
    weights = tuple((w.astype(jnp.float32) for w in (w_query, w_key, w_value, w_output, w_expand, w_contract)))
    params = (bias_query, bias_value, bias_output, shift_attn, bias_expand, bias_contract, shift_ffn)
    groups = SEQS // SEQ_DEV
    inputs_all = hidden_in.astype(jnp.float32).reshape(groups, SEQ_DEV, SEQ_LEN, D)
    cots_all = cotangent.astype(jnp.float32).reshape(groups, SEQ_DEV, SEQ_LEN, D)
    lens_all = lengths.reshape(groups, SEQ_DEV)

    def group_step(totals, items):
        inputs, cots, lens = items

        def run(prm, xval):
            return forward(prm, xval, lens, weights, gain_attn, gain_ffn)
        result, back = jax.vjp(run, params, inputs)
        grad_params, grad_inputs = back(cots)
        totals = tuple((a + b for a, b in zip(totals, grad_params)))
        return (totals, (result.astype(jnp.bfloat16), grad_inputs.astype(jnp.bfloat16)))
    zeros = tuple((jnp.zeros_like(p) for p in params))
    totals, (results, grads) = lax.scan(group_step, zeros, (inputs_all, cots_all, lens_all))
    factor = TOKENS ** (-0.5)
    scaled = tuple((t * factor for t in totals))
    return (results.reshape(SEQS, SEQ_LEN, D), grads.reshape(SEQS, SEQ_LEN, D), scaled[0], scaled[1], scaled[2], scaled[3], scaled[4], scaled[5], scaled[6])
```

```python
import jax
import jax.numpy as jnp
from jax import lax
from jax.sharding import PartitionSpec as P

HEADS = 16
HEAD = 64


NEG = -1e30
EPSILON = 1e-12


def layer_norm(resid, gain, shift):
    center = resid - jnp.mean(resid, -1, keepdims=True)
    spread = jnp.mean(center * center, -1, keepdims=True)
    return center * lax.rsqrt(spread + EPSILON) * gain + shift


def gelu_exact(value):
    return jax.nn.gelu(value, approximate=False)


def times_transpose(grad, weight):
    return lax.dot_general(
        grad, weight, (((1,), (1,)), ((), ())), preferred_element_type=jnp.float32
    )


def local(
    hidden_in,
    lengths,
    w_query,
    w_key,
    w_value,
    w_output,
    gain_attn,
    w_expand,
    w_contract,
    gain_ffn,
    bias_query,
    bias_value,
    bias_output,
    shift_attn,
    bias_expand,
    bias_contract,
    shift_ffn,
    cotangent,
):
    group = lax.axis_size("seq")
    seqs_here, local_len, width = hidden_in.shape
    seqs = seqs_here // group
    full_len = local_len * group
    rows = seqs * full_len
    scale = HEAD ** (-0.5)
    f32 = jnp.float32
    bf16 = jnp.bfloat16

    def gather_seqs(arr):
        return lax.all_to_all(arr, "seq", split_axis=0, concat_axis=1, tiled=True).reshape(rows, width)

    def scatter_seqs(arr):
        return lax.all_to_all(
            arr.reshape(seqs, full_len, width), "seq", split_axis=1, concat_axis=0, tiled=True
        )

    def heads(arr):
        return arr.reshape(seqs, full_len, HEADS, HEAD)

    x_rows = gather_seqs(hidden_in)
    cot_rows = gather_seqs(cotangent)
    lens = lax.dynamic_slice_in_dim(lengths, lax.axis_index("seq") * seqs, seqs)
    query = heads((jnp.dot(x_rows, w_query, preferred_element_type=f32) + bias_query).astype(bf16))
    keys = heads(jnp.dot(x_rows, w_key, preferred_element_type=f32).astype(bf16))
    values = heads((jnp.dot(x_rows, w_value, preferred_element_type=f32) + bias_value).astype(bf16))
    raw = jnp.einsum("sqhd,skhd->shqk", query, keys, preferred_element_type=f32) * scale
    position = jnp.arange(full_len, dtype=jnp.int32)
    valid = position[None, :] < lens[:, None]
    scores = jnp.where(valid[:, None, None, :], raw, NEG)
    top = jnp.max(scores, -1, keepdims=True)
    expd = jnp.exp(scores - top)
    probs_full = expd / jnp.sum(expd, -1, keepdims=True)
    probs = probs_full.astype(bf16)
    context = jnp.einsum("shqk,skhd->sqhd", probs, values, preferred_element_type=f32)
    context_rows = context.astype(bf16).reshape(rows, width)
    attn_out = jnp.dot(context_rows, w_output, preferred_element_type=f32) + bias_output
    resid_one = x_rows.astype(f32) + attn_out
    normed_one = layer_norm(resid_one, gain_attn, shift_attn)
    normed_low = normed_one.astype(bf16)
    expand = jnp.dot(normed_low, w_expand, preferred_element_type=f32) + bias_expand
    hidden = gelu_exact(expand).astype(bf16)
    resid_two = normed_one + jnp.dot(hidden, w_contract, preferred_element_type=f32) + bias_contract
    result = scatter_seqs(layer_norm(resid_two, gain_ffn, shift_ffn).astype(bf16))
    grad_out = cot_rows.astype(f32)
    g_shift_ffn = jnp.sum(grad_out, 0)
    _, norm_two_back = jax.vjp(lambda resid: layer_norm(resid, gain_ffn, shift_ffn), resid_two)
    grad_two = norm_two_back(grad_out)[0]
    grad_branch = grad_two.astype(bf16)
    g_bias_contract = jnp.sum(grad_branch.astype(f32), 0)
    grad_hidden = times_transpose(grad_branch, w_contract)
    _, gelu_back = jax.vjp(gelu_exact, expand)
    grad_expand = gelu_back(grad_hidden)[0].astype(bf16)
    g_bias_expand = jnp.sum(grad_expand.astype(f32), 0)
    grad_normed = times_transpose(grad_expand, w_expand) + grad_two
    g_shift_attn = jnp.sum(grad_normed, 0)
    _, norm_one_back = jax.vjp(lambda resid: layer_norm(resid, gain_attn, shift_attn), resid_one)
    grad_one = norm_one_back(grad_normed)[0]
    grad_attn = grad_one.astype(bf16)
    g_bias_output = jnp.sum(grad_attn.astype(f32), 0)
    grad_context = heads(times_transpose(grad_attn, w_output).astype(bf16))
    grad_probs = jnp.einsum("sqhd,skhd->shqk", grad_context, values, preferred_element_type=f32)
    inner = jnp.sum(probs_full * grad_probs, -1, keepdims=True)
    grad_scores = (probs_full * (grad_probs - inner)).astype(bf16)
    grad_query = (
        jnp.einsum("shqk,skhd->sqhd", grad_scores, keys, preferred_element_type=f32) * scale
    ).astype(bf16).reshape(rows, width)
    grad_key = (
        jnp.einsum("shqk,sqhd->skhd", grad_scores, query, preferred_element_type=f32) * scale
    ).astype(bf16).reshape(rows, width)
    grad_value = (
        jnp.einsum("shqk,sqhd->skhd", probs, grad_context, preferred_element_type=f32)
    ).astype(bf16).reshape(rows, width)
    g_bias_query = jnp.sum(grad_query.astype(f32), 0)
    g_bias_value = jnp.sum(grad_value.astype(f32), 0)
    grad_input = (
        grad_one
        + times_transpose(grad_query, w_query)
        + times_transpose(grad_key, w_key)
        + times_transpose(grad_value, w_value)
    )
    grad_input = scatter_seqs(grad_input.astype(bf16))
    summed = lax.psum(
        (
            g_shift_ffn,
            g_bias_contract,
            g_bias_expand,
            g_shift_attn,
            g_bias_output,
            g_bias_query,
            g_bias_value,
        ),
        ("dp", "seq"),
    )
    factor = (rows * lax.axis_size("dp") * group) ** (-0.5)
    return (
        result,
        grad_input,
        summed[5] * factor,
        summed[6] * factor,
        summed[4] * factor,
        summed[3] * factor,
        summed[2] * factor,
        summed[1] * factor,
        summed[0] * factor,
    )


def solution(mesh):
    placed = (
        P("dp", "seq", None),
        P("dp"),
        P(),
        P(),
        P(),
        P(),
        P(),
        P(),
        P(),
        P(),
        P(),
        P(),
        P(),
        P(),
        P(),
        P(),
        P(),
        P("dp", "seq", None),
    )
    return jax.shard_map(
        local,
        mesh=mesh,
        in_specs=placed,
        out_specs=(P("dp", "seq", None), P("dp", "seq", None), P(), P(), P(), P(), P(), P(), P()),
        check_vma=False,
    )
```

```python
import functools

import jax
import jax.numpy as jnp
from jax import lax
from jax.experimental import pallas as pl
from jax.experimental.pallas import tpu as pltpu
from jax.sharding import PartitionSpec as P

HEADS = 16
HEAD = 64
NEG = -1e30
EPSILON = 1e-12
LANES = 128
MESH = pl.DeviceIdType.MESH
F32 = jnp.float32
BF16 = jnp.bfloat16


def dot_nn(left, right):
    return jnp.dot(left, right, preferred_element_type=F32)


def dot_nt(left, right):
    return lax.dot_general(left, right, (((1,), (1,)), ((), ())), preferred_element_type=F32)


def flip(index, mask):
    bit = 1
    while bit <= mask:
        if mask & bit:
            index = index + bit - 2 * bit * ((index // bit) % 2)
        bit *= 2
    return index


def ds(start, size):
    return pl.ds(start if isinstance(start, int) else pl.multiple_of(start, size), size)


def fold8(value):
    rows, width = value.shape
    return jnp.sum(value.reshape(rows // 8, 8, width), 0)


def loop(count, body):
    def step(index, carry):
        body(index)
        return carry

    lax.fori_loop(0, count, step, 0)


def kernel(
    group,
    dp_size,
    factor,
    hidden_in,
    lengths,
    w_query,
    w_key,
    w_value,
    w_output,
    gain_attn,
    w_expand,
    w_contract,
    gain_ffn,
    bias_query,
    bias_value,
    bias_output,
    shift_attn,
    bias_expand,
    bias_contract,
    shift_ffn,
    cotangent,
    out,
    grad_in,
    g_bias_query,
    g_bias_value,
    g_bias_output,
    g_shift_attn,
    g_bias_expand,
    g_bias_contract,
    g_shift_ffn,
    wq,
    wk,
    wv,
    wo,
    we,
    wc,
    vecs,
    vec_expand,
    x_buf,
    cot_buf,
    q_t,
    k_n,
    k_t,
    v_n,
    v_t,
    probs,
    recip,
    ctx_t,
    ctx_n,
    xh1,
    rstd1,
    low,
    big_a,
    big_b,
    resid,
    sums,
    red,
    red_in,
    local_sem,
    send_sem,
    recv_sem,
    red_send,
    red_recv,
):
    me = lax.axis_index("seq")
    dp = lax.axis_index("dp")
    part = hidden_in.shape[1]
    rows, width = x_buf.shape
    ff = we.shape[1]
    peers = list(range(1, group))
    dp_bits = [1 << b for b in range(dp_size.bit_length() - 1)]

    small = (
        bias_query,
        bias_value,
        bias_output,
        gain_attn,
        shift_attn,
        bias_contract,
        gain_ffn,
        shift_ffn,
    )
    b_q, b_v, b_o, gain1, shift1, b_c, gain2, shift2 = range(8)
    fetch = {}

    def fetch_start(name, src, dst):
        fetch[name] = pltpu.make_async_copy(src, dst, local_sem.at[len(fetch)])
        fetch[name].start()

    mine = ds(me * part, part)
    fetch_start("x", hidden_in.at[me], x_buf.at[mine])
    fetch_start("wq", w_query, wq)
    fetch_start("wk", w_key, wk)
    fetch_start("wv", w_value, wv)

    barrier = pltpu.get_barrier_semaphore()
    for j in peers:
        pl.semaphore_signal(barrier, inc=1, device_id={"seq": flip(me, j)}, device_id_type=MESH)
    for b in dp_bits:
        pl.semaphore_signal(barrier, inc=1, device_id={"dp": flip(dp, b)}, device_id_type=MESH)
    pl.semaphore_wait(barrier, len(peers) + len(dp_bits))

    def exchange(kind, src_of, dst):
        copies = []
        for j in peers:
            peer = flip(me, j)
            copies.append(
                pltpu.make_async_remote_copy(
                    src_ref=src_of(peer),
                    dst_ref=dst,
                    send_sem=send_sem.at[kind, j - 1],
                    recv_sem=recv_sem.at[kind, j - 1],
                    device_id={"seq": peer},
                    device_id_type=MESH,
                )
            )
        return copies

    x_copies = exchange(0, lambda peer: hidden_in.at[peer], x_buf.at[mine])
    for copy in x_copies:
        copy.start()
    for i, vec in enumerate(small):
        fetch_start(("v", i), vec, vecs.at[i])
    fetch_start("be", bias_expand, vec_expand)
    fetch_start("wo", w_output, wo)
    fetch_start("we", w_expand, we)
    cot_copies = exchange(1, lambda peer: cotangent.at[peer], cot_buf.at[mine])
    for copy in cot_copies:
        copy.start()
    fetch_start("cot", cotangent.at[me], cot_buf.at[mine])
    fetch_start("wc", w_contract, wc)

    sums[...] = jnp.zeros_like(sums)
    s_ffn, s_contract, s_attn, s_output, s_query, s_value, s_expand = range(7)

    fetch["x"].wait()
    for copy in x_copies:
        copy.wait()
    for i in range(len(small)):
        fetch["v", i].wait()
    fetch["wq"].wait()
    fetch["wk"].wait()
    fetch["wv"].wait()

    scale = HEAD ** (-0.5)

    def qkv_step(i):
        cols = ds(i * 256, 256)
        xs = x_buf[...]
        q = ((dot_nn(xs, wq[:, cols]) + vecs[b_q, :, cols]) * scale).astype(BF16)
        q_t[cols, :] = q.T
        k = dot_nn(xs, wk[:, cols]).astype(BF16)
        k_n[:, cols] = k
        k_t[cols, :] = k.T
        v = (dot_nn(xs, wv[:, cols]) + vecs[b_v, :, cols]).astype(BF16)
        v_n[:, cols] = v
        v_t[cols, :] = v.T

    loop(width // 256, qkv_step)

    length = lengths[me]
    row = lax.broadcasted_iota(jnp.int32, (rows, LANES), 0)
    lane = lax.broadcasted_iota(jnp.int32, (rows, LANES), 1)
    key_bias = jnp.where((row >= length) & (lane == 0), NEG, 0.0).astype(BF16)

    def attn_step(p):
        lanes = ds(p * LANES, LANES)
        k_pair = k_n[:, lanes]
        v_pair = v_t[lanes, :]
        q_aug = jnp.concatenate([q_t[lanes, :], jnp.ones((LANES, rows), BF16)], 0)
        ones = jnp.ones((16, rows), BF16)
        half = lax.broadcasted_iota(jnp.int32, (rows, LANES), 1) < HEAD
        parts = []
        for j in range(2):
            k_one = jnp.where(half if j == 0 else ~half, k_pair, jnp.zeros_like(k_pair))
            scores = dot_nn(jnp.concatenate([k_one, key_bias], 1), q_aug)
            top = jnp.max(scores, 0, keepdims=True)
            e = jnp.exp(scores - top).astype(BF16)
            probs[2 * p + j] = e
            o = dot_nn(jnp.concatenate([v_pair[HEAD * j : HEAD * j + HEAD], ones], 0), e)
            inv = 1.0 / o[HEAD : HEAD + 1]
            recip[pl.ds(2 * p + j, 1), :] = inv
            parts.append(o[:HEAD] * inv)
        c = jnp.concatenate(parts, 0).astype(BF16)
        ctx_t[lanes, :] = c
        ctx_n[:, lanes] = c.T

    loop(HEADS // 2, attn_step)

    fetch["wo"].wait()

    def out_proj_step(i):
        part_rows = ds(i * 256, 256)
        ao = dot_nn(ctx_n[part_rows, :], wo[...]) + vecs[b_o]
        h = x_buf[part_rows, :].astype(F32) + ao
        center = h - jnp.mean(h, -1, keepdims=True)
        r = lax.rsqrt(jnp.mean(center * center, -1, keepdims=True) + EPSILON)
        xh = center * r
        xh1[part_rows, :] = xh
        rstd1[part_rows, :] = jnp.broadcast_to(r, (256, LANES))
        low[part_rows, :] = (xh * vecs[gain1] + vecs[shift1]).astype(BF16)

    loop(rows // 256, out_proj_step)

    fetch["we"].wait()
    fetch["be"].wait()

    def expand_step(i):
        cols = ds(i * 512, 512)
        f = dot_nn(low[...], we[:, cols]) + vec_expand[:, cols]
        phi = 0.5 * (1.0 + lax.erf(f * (0.5**0.5)))
        big_a[:, cols] = (f * phi).astype(BF16)
        dens = jnp.exp(f * f * -0.5) * (0.5 / jnp.pi) ** 0.5
        big_b[:, cols] = (phi + f * dens).astype(BF16)

    loop(ff // 512, expand_step)
    fetch["wc"].wait()

    def contract_step(i):
        cols = ds(i * 256, 256)
        n1 = xh1[:, cols] * vecs[gain1, :, cols] + vecs[shift1, :, cols]
        resid[:, cols] = n1 + dot_nn(big_a[...], wc[:, cols]) + vecs[b_c, :, cols]

    loop(width // 256, contract_step)

    fetch["cot"].wait()
    for copy in cot_copies:
        copy.wait()

    def norm2_step(i):
        part_rows = ds(i * 32, 32)
        h = resid[part_rows, :]
        center = h - jnp.mean(h, -1, keepdims=True)
        r = lax.rsqrt(jnp.mean(center * center, -1, keepdims=True) + EPSILON)
        xh = center * r
        ctx_n[part_rows, :] = (xh * vecs[gain2] + vecs[shift2]).astype(BF16)
        dy = cot_buf[part_rows, :].astype(F32)
        sums[s_ffn, :, :width] += fold8(dy)
        e = dy * vecs[gain2]
        d = r * (e - jnp.mean(e, -1, keepdims=True) - xh * jnp.mean(e * xh, -1, keepdims=True))
        resid[part_rows, :] = d
        d_low = d.astype(BF16)
        low[part_rows, :] = d_low
        sums[s_contract, :, :width] += fold8(d_low.astype(F32))

    loop(rows // 32, norm2_step)

    def rows_of(peer):
        return ctx_n.at[ds(peer * part, part)]

    out_copies = exchange(2, rows_of, out.at[me])
    for copy in out_copies:
        copy.start()
    fetch_start("out", rows_of(me), out.at[me])

    def contract_back_step(i):
        cols = ds(i * 512, 512)
        df = (dot_nt(low[...], wc[cols, :]) * big_b[:, cols].astype(F32)).astype(BF16)
        big_b[:, cols] = df
        sums[s_expand, :, cols] += fold8(df.astype(F32))

    loop(ff // 512, contract_back_step)

    def expand_back_step(i):
        cols = ds(i * 256, 256)
        resid[:, cols] += dot_nt(big_b[...], we[cols, :])

    loop(width // 256, expand_back_step)

    def norm1_step(i):
        part_rows = ds(i * 32, 32)
        dn = resid[part_rows, :]
        sums[s_attn, :, :width] += fold8(dn)
        e = dn * vecs[gain1]
        xh = xh1[part_rows, :]
        r = rstd1[part_rows, :1]
        d = r * (e - jnp.mean(e, -1, keepdims=True) - xh * jnp.mean(e * xh, -1, keepdims=True))
        resid[part_rows, :] = d
        d_low = d.astype(BF16)
        low[part_rows, :] = d_low
        sums[s_output, :, :width] += fold8(d_low.astype(F32))

    loop(rows // 32, norm1_step)

    def ctx_back_step(i):
        feats = ds(i * 256, 256)
        v_t[feats, :] = dot_nt(wo[feats, :], low[...]).astype(BF16)

    loop(width // 256, ctx_back_step)
    dq_n, dk_n, dv_n = (big_a.at[:, i * width : (i + 1) * width] for i in range(3))

    def attn_back_step(p):
        lanes = ds(p * LANES, LANES)
        v_pair, q_pair, k_pair = v_n[:, lanes], q_t[lanes, :], k_t[lanes, :]
        half = lax.broadcasted_iota(jnp.int32, (rows, LANES), 1) < HEAD
        dctx = v_t[lanes, :].astype(F32)
        ctx = ctx_t[lanes, :].astype(F32)
        scaled, inner = [], []
        for j in range(2):
            sub = slice(HEAD * j, HEAD * j + HEAD)
            d = dctx[sub] * recip[pl.ds(2 * p + j, 1), :]
            inner.append(jnp.sum(d * ctx[sub], 0, keepdims=True))
            scaled.append(d.astype(BF16))
        both = jnp.concatenate(scaled, 0)
        dqs, dks, dvs = [], [], []
        for j in range(2):
            sub = slice(HEAD * j, HEAD * j + HEAD)
            v_one = jnp.where(half if j == 0 else ~half, v_pair, jnp.zeros_like(v_pair))
            dprobs = dot_nn(v_one, both)
            e = probs[2 * p + j]
            dscores = (e.astype(F32) * (dprobs - inner[j])).astype(BF16)
            dvs.append(dot_nt(scaled[j], e))
            dqs.append(dot_nn(k_pair[sub], dscores) * scale)
            dks.append(dot_nt(q_pair[sub], dscores))
        dq_n[:, lanes] = jnp.concatenate(dqs, 0).astype(BF16).T
        dk_n[:, lanes] = jnp.concatenate(dks, 0).astype(BF16).T
        dv_n[:, lanes] = jnp.concatenate(dvs, 0).astype(BF16).T

    loop(HEADS // 2, attn_back_step)

    def bias_step(i):
        part_rows = ds(i * 64, 64)
        sums[s_query, :, :width] += fold8(dq_n[part_rows, :].astype(F32))
        sums[s_value, :, :width] += fold8(dv_n[part_rows, :].astype(F32))

    loop(rows // 64, bias_step)

    red[0] = jnp.zeros(red.shape[1:], F32)
    for i in range(6):
        red[0, i : i + 1, :] = jnp.sum(sums[i, :, :width], 0, keepdims=True)
    expand_rows = ff // width
    for i in range(expand_rows):
        red[0, 6 + i : 7 + i, :] = jnp.sum(
            sums[s_expand, :, i * width : (i + 1) * width], 0, keepdims=True
        )

    def send_partial(slot, src, where):
        return pltpu.make_async_remote_copy(
            src_ref=red.at[src],
            dst_ref=red_in.at[slot],
            send_sem=red_send.at[slot],
            recv_sem=red_recv.at[slot],
            device_id=where,
            device_id_type=MESH,
        )

    group_copies = [send_partial(j - 1, 0, {"seq": flip(me, j)}) for j in peers]
    for copy in group_copies:
        copy.start()

    def grad_step(peer):
        part_rows = ds(peer * part, part)
        g = (
            resid[part_rows, :]
            + dot_nt(dq_n[part_rows, :], wq[...])
            + dot_nt(dk_n[part_rows, :], wk[...])
            + dot_nt(dv_n[part_rows, :], wv[...])
        )
        x_buf[part_rows, :] = g.astype(BF16)

    grad_copies = exchange(3, lambda peer: x_buf.at[ds(peer * part, part)], grad_in.at[me])
    for j in reversed(peers):
        grad_step(flip(me, j))
        grad_copies[j - 1].start()
    grad_step(me)
    fetch_start("grad", x_buf.at[mine], grad_in.at[me])

    for copy in group_copies:
        copy.wait()
    total = jnp.zeros(red.shape[1:], F32)
    for member in range(group):
        piece = red[0]
        for j in peers:
            piece = jnp.where(flip(me, j) == member, red_in[j - 1], piece)
        total = total + piece
    red[1] = total
    for step, b in enumerate(dp_bits):
        copy = send_partial(len(peers) + step, 1 + step, {"dp": flip(dp, b)})
        copy.start()
        copy.wait()
        red[2 + step] = red[1 + step] + red_in[len(peers) + step]
    final = 1 + len(dp_bits)
    for i, ref in enumerate(
        (g_shift_ffn, g_bias_contract, g_shift_attn, g_bias_output, g_bias_query, g_bias_value)
    ):
        ref[...] = red[final, i : i + 1, :] * factor
    for i in range(expand_rows):
        g_bias_expand[:, i * width : (i + 1) * width] = red[final, 6 + i : 7 + i, :] * factor

    for copy in out_copies + grad_copies:
        copy.wait()
    fetch["out"].wait()
    fetch["grad"].wait()


def local(mesh, *args):
    hidden_in, lengths = args[:2]
    group, dp_size = mesh.shape["seq"], mesh.shape["dp"]
    seqs, part, width = hidden_in.shape
    ff = args[7].shape[1]
    rows = part * group
    assert seqs == group
    assert group & (group - 1) == 0 and dp_size & (dp_size - 1) == 0
    factor = (rows * seqs // group * dp_size * group) ** (-0.5)
    steps = dp_size.bit_length() - 1
    anywhere = pl.BlockSpec(memory_space=pl.ANY)
    in_specs = [anywhere] * len(args)
    in_specs[1] = pl.BlockSpec(memory_space=pltpu.SMEM)
    vmem = pl.BlockSpec(memory_space=pltpu.VMEM)
    operands = [a.reshape(1, -1) if a.ndim == 1 and i != 1 else a for i, a in enumerate(args)]
    row = jax.ShapeDtypeStruct((1, width), F32)
    outs = pl.pallas_call(
        functools.partial(kernel, group, dp_size, factor),
        out_shape=[jax.ShapeDtypeStruct(hidden_in.shape, BF16)] * 2
        + [row] * 4
        + [jax.ShapeDtypeStruct((1, ff), F32), row, row],
        in_specs=in_specs,
        out_specs=[anywhere] * 2 + [vmem] * 7,
        scratch_shapes=[
            pltpu.VMEM((width, width), BF16),
            pltpu.VMEM((width, width), BF16),
            pltpu.VMEM((width, width), BF16),
            pltpu.VMEM((width, width), BF16),
            pltpu.VMEM((width, ff), BF16),
            pltpu.VMEM((ff, width), BF16),
            pltpu.VMEM((8, 1, width), F32),
            pltpu.VMEM((1, ff), F32),
            pltpu.VMEM((rows, width), BF16),
            pltpu.VMEM((rows, width), BF16),
            pltpu.VMEM((width, rows), BF16),
            pltpu.VMEM((rows, width), BF16),
            pltpu.VMEM((width, rows), BF16),
            pltpu.VMEM((rows, width), BF16),
            pltpu.VMEM((width, rows), BF16),
            pltpu.VMEM((HEADS, rows, rows), BF16),
            pltpu.VMEM((HEADS, rows), F32),
            pltpu.VMEM((width, rows), BF16),
            pltpu.VMEM((rows, width), BF16),
            pltpu.VMEM((rows, width), F32),
            pltpu.VMEM((rows, LANES), F32),
            pltpu.VMEM((rows, width), BF16),
            pltpu.VMEM((rows, ff), BF16),
            pltpu.VMEM((rows, ff), BF16),
            pltpu.VMEM((rows, width), F32),
            pltpu.VMEM((7, 8, ff), F32),
            pltpu.VMEM((2 + steps, 16, width), F32),
            pltpu.VMEM((group - 1 + steps, 16, width), F32),
            pltpu.SemaphoreType.DMA((24,)),
            pltpu.SemaphoreType.DMA((4, group - 1)),
            pltpu.SemaphoreType.DMA((4, group - 1)),
            pltpu.SemaphoreType.DMA((group - 1 + steps,)),
            pltpu.SemaphoreType.DMA((group - 1 + steps,)),
        ],
        compiler_params=pltpu.CompilerParams(
            collective_id=0, has_side_effects=True, vmem_limit_bytes=67043328
        ),
        name="layer",
    )(*operands)
    return tuple(o.reshape(-1) if o.shape[0] == 1 else o for o in outs)


def solution(mesh):
    placed = (P("dp", "seq", None), P("dp")) + (P(),) * 15 + (P("dp", "seq", None),)
    return jax.shard_map(
        functools.partial(local, mesh),
        mesh=mesh,
        in_specs=placed,
        out_specs=(P("dp", "seq", None), P("dp", "seq", None), P(), P(), P(), P(), P(), P(), P()),
        check_vma=False,
    )
```

```python
import functools

import jax
import jax.numpy as jnp
from jax import lax
from jax.experimental import pallas as pl
from jax.experimental.pallas import tpu as pltpu
from jax.sharding import PartitionSpec as P

HEADS = 16
HEAD = 64
NEG = -1e30
EPSILON = 1e-12
LANES = 128
MESH = pl.DeviceIdType.MESH
F32 = jnp.float32
BF16 = jnp.bfloat16


def dot_nn(left, right):
    return jnp.dot(left, right, preferred_element_type=F32)


def dot_nt(left, right):
    return lax.dot_general(left, right, (((1,), (1,)), ((), ())), preferred_element_type=F32)


def flip(index, mask):
    bit = 1
    while bit <= mask:
        if mask & bit:
            index = index + bit - 2 * bit * ((index // bit) % 2)
        bit *= 2
    return index


def ds(start, size):
    return pl.ds(start if isinstance(start, int) else pl.multiple_of(start, size), size)


def fold8(value):
    rows, width = value.shape
    return jnp.sum(value.reshape(rows // 8, 8, width), 0)


def loop(count, body):
    def step(index, carry):
        body(index)
        return carry

    lax.fori_loop(0, count, step, 0)


def kernel(
    group,
    dp_size,
    factor,
    hidden_in,
    lengths,
    w_query,
    w_key,
    w_value,
    w_output,
    gain_attn,
    w_expand,
    w_contract,
    gain_ffn,
    bias_query,
    bias_value,
    bias_output,
    shift_attn,
    bias_expand,
    bias_contract,
    shift_ffn,
    cotangent,
    out,
    grad_in,
    small_out,
    wq,
    wk,
    wv,
    wo,
    we,
    wc,
    vecs,
    vec_expand,
    x_buf,
    cot_buf,
    q_t,
    k_n,
    k_t,
    v_n,
    v_t,
    probs,
    recip,
    ctx_t,
    ctx_n,
    xh1,
    rstd1,
    low,
    big_a,
    big_b,
    resid,
    s_a,
    s_b,
    top_a,
    top_b,
    ds_a,
    ds_b,
    key_bias,
    sums,
    red,
    red_in,
    local_sem,
    send_sem,
    recv_sem,
    red_send,
    red_recv,
):
    me = lax.axis_index("seq")
    dp = lax.axis_index("dp")
    part = hidden_in.shape[1]
    rows, width = x_buf.shape
    ff = we.shape[1]
    peers = list(range(1, group))
    members = [flip(me, j) for j in peers]
    core = me % 2
    by_core = [flip(me, 1)] + [
        flip(me, hi) - core + c for c in range(2) for hi in range(2, group, 2)
    ]
    dp_bits = [1 << b for b in range(dp_size.bit_length() - 1)]

    small = (
        bias_query,
        bias_value,
        bias_output,
        gain_attn,
        shift_attn,
        bias_contract,
        gain_ffn,
        shift_ffn,
    )
    b_q, b_v, b_o, gain1, shift1, b_c, gain2, shift2 = range(8)
    fetch = {}

    def fetch_start(name, src, dst):
        fetch[name] = pltpu.make_async_copy(src, dst, local_sem.at[len(fetch)])
        fetch[name].start()

    mine = ds(me * part, part)
    fetch_start("x", hidden_in.at[me], x_buf.at[mine])
    fetch_start("wq", w_query, wq)
    fetch_start("wk", w_key, wk)
    fetch_start("wv", w_value, wv)

    barrier = pltpu.get_barrier_semaphore()
    for j in peers:
        pl.semaphore_signal(barrier, inc=1, device_id={"seq": flip(me, j)}, device_id_type=MESH)
    for b in dp_bits:
        pl.semaphore_signal(barrier, inc=1, device_id={"dp": flip(dp, b)}, device_id_type=MESH)
    pl.semaphore_wait(barrier, len(peers) + len(dp_bits))

    def exchange(kind, src_of, dst):
        def send(peer):
            return pltpu.make_async_remote_copy(
                src_ref=src_of(peer),
                dst_ref=dst,
                send_sem=send_sem.at[kind, peer],
                recv_sem=recv_sem.at[kind, me],
                device_id={"seq": peer},
                device_id_type=MESH,
            )

        return send

    def block_of(buf):
        return lambda peer: buf.at[ds(peer * part, part)]

    def arrived(kind, dst_of, peer):
        pltpu.make_async_remote_copy(
            src_ref=dst_of(peer),
            dst_ref=dst_of(peer),
            send_sem=send_sem.at[kind, peer],
            recv_sem=recv_sem.at[kind, peer],
            device_id={"seq": peer},
            device_id_type=MESH,
        ).wait_recv()

    send_x = exchange(0, lambda peer: hidden_in.at[peer], x_buf.at[mine])
    for peer in by_core:
        send_x(peer).start()
    for i, vec in enumerate(small):
        fetch_start(("v", i), vec, vecs.at[i])
    fetch_start("be", bias_expand, vec_expand)
    fetch_start("wo", w_output, wo)
    fetch_start("we", w_expand, we)
    send_cot = exchange(1, lambda peer: cotangent.at[peer], cot_buf.at[mine])
    for peer in by_core:
        send_cot(peer).start()
    fetch_start("cot", cotangent.at[me], cot_buf.at[mine])
    fetch_start("wc", w_contract, wc)

    sums[...] = jnp.zeros_like(sums)
    s_ffn, s_contract, s_attn, s_output, s_query, s_value, s_expand = range(7)

    scale = HEAD ** (-0.5)
    pair = 2 * part

    def qkv(base):
        here = ds(base, pair)
        xs = x_buf[here, :]

        def step(i):
            cols = ds(i * 256, 256)
            q = ((dot_nn(xs, wq[:, cols]) + vecs[b_q, :, cols]) * scale).astype(BF16)
            q_t[cols, here] = q.T
            k = dot_nn(xs, wk[:, cols]).astype(BF16)
            k_n[here, cols] = k
            k_t[cols, here] = k.T
            v = (dot_nn(xs, wv[:, cols]) + vecs[b_v, :, cols]).astype(BF16)
            v_n[here, cols] = v
            v_t[cols, here] = v.T

        loop(width // 256, step)

    length = lengths[me]
    row = lax.broadcasted_iota(jnp.int32, (rows, LANES), 0)
    lane = lax.broadcasted_iota(jnp.int32, (rows, LANES), 1)
    for j in range(2):
        key_bias[j] = jnp.where((row >= length) & (lane == HEAD * (1 - j)), NEG, 0.0).astype(BF16)

    for i in range(len(small)):
        fetch["v", i].wait()
    fetch["x"].wait()
    fetch["wq"].wait()
    fetch["wk"].wait()
    fetch["wv"].wait()
    arrived(0, block_of(x_buf), flip(me, 1))
    qkv((me - core) * part)
    for hi in range(2, group, 2):
        for c in range(2):
            arrived(0, block_of(x_buf), flip(me, hi) - core + c)
        qkv((flip(me, hi) - core) * part)

    score_refs, top_refs = (s_a, s_b), (top_a, top_b)

    def score(p, j):
        lanes = ds(p * LANES, LANES)
        half = lax.broadcasted_iota(jnp.int32, (rows, LANES), 1) < HEAD
        k_one = jnp.where(half if j == 0 else ~half, k_n[:, lanes], key_bias[j])
        q_one = q_t[ds(p * LANES + HEAD * j, HEAD), :]
        pad = [jnp.ones((16, rows), BF16), jnp.zeros((HEAD - 16, rows), BF16)]
        q_one = jnp.concatenate([q_one] + pad if j == 0 else pad + [q_one], 0)
        for c in range(0, rows, 256):
            cols = slice(c, c + 256)
            block = dot_nn(k_one, q_one[:, cols])
            score_refs[j][:, cols] = block
            top_refs[j][:, cols] = jnp.max(block, 0, keepdims=True)

    def exponential(h, j):
        for c in range(0, rows, 256):
            cols = slice(c, c + 256)
            probs[h, :, cols] = jnp.exp(score_refs[j][:, cols] - top_refs[j][:, cols]).astype(BF16)

    def weigh(h):
        feats = ds(h * HEAD, HEAD)
        o = dot_nn(jnp.concatenate([v_t[feats, :], jnp.ones((16, rows), BF16)], 0), probs[h])
        inv = 1.0 / o[HEAD : HEAD + 1]
        recip[pl.ds(h, 1), :] = inv
        ctx_t[feats, :] = (o[:HEAD] * inv).astype(BF16)

    def turn(p):
        lanes = ds(p * LANES, LANES)
        ctx_n[:, lanes] = ctx_t[lanes, :].T

    score(0, 0)
    exponential(0, 0)
    score(0, 1)

    def attn_step(p):
        exponential(2 * p + 1, 1)
        score(p + 1, 0)
        weigh(2 * p)
        exponential(2 * p + 2, 0)
        score(p + 1, 1)
        weigh(2 * p + 1)
        turn(p)

    loop(HEADS // 2 - 1, attn_step)
    exponential(HEADS - 1, 1)
    weigh(HEADS - 2)
    weigh(HEADS - 1)
    turn(HEADS // 2 - 1)

    fetch["wo"].wait()

    def out_proj_step(i):
        part_rows = ds(i * 256, 256)
        ao = dot_nn(ctx_n[part_rows, :], wo[...]) + vecs[b_o]
        h = x_buf[part_rows, :].astype(F32) + ao
        center = h - jnp.mean(h, -1, keepdims=True)
        r = lax.rsqrt(jnp.mean(center * center, -1, keepdims=True) + EPSILON)
        xh = center * r
        xh1[part_rows, :] = xh
        rstd1[part_rows, :] = jnp.broadcast_to(r, (256, LANES))
        low[part_rows, :] = (xh * vecs[gain1] + vecs[shift1]).astype(BF16)

    loop(rows // 256, out_proj_step)

    fetch["we"].wait()
    fetch["be"].wait()

    def expand(i):
        cols = ds(i * 512, 512)
        s_a[...] = dot_nn(low[...], we[:, cols]) + vec_expand[:, cols]

    def gelu(i):
        cols = ds(i * 512, 512)
        f = s_a[...]
        phi = 0.5 * (1.0 + lax.erf(f * (0.5**0.5)))
        big_a[:, cols] = (f * phi).astype(BF16)
        dens = jnp.exp(f * f * -0.5) * (0.5 / jnp.pi) ** 0.5
        big_b[:, cols] = (phi + f * dens).astype(BF16)

    expand(0)

    def expand_step(i):
        gelu(i)
        expand(i + 1)

    loop(ff // 512 - 1, expand_step)
    gelu(ff // 512 - 1)
    fetch["wc"].wait()

    def contract_step(i):
        cols = ds(i * 256, 256)
        n1 = xh1[:, cols] * vecs[gain1, :, cols] + vecs[shift1, :, cols]
        resid[:, cols] = n1 + dot_nn(big_a[...], wc[:, cols]) + vecs[b_c, :, cols]

    loop(width // 256, contract_step)

    fetch["cot"].wait()
    for peer in members:
        arrived(1, block_of(cot_buf), peer)

    def norm2_step(i):
        part_rows = ds(i * 32, 32)
        h = resid[part_rows, :]
        center = h - jnp.mean(h, -1, keepdims=True)
        r = lax.rsqrt(jnp.mean(center * center, -1, keepdims=True) + EPSILON)
        xh = center * r
        ctx_n[part_rows, :] = (xh * vecs[gain2] + vecs[shift2]).astype(BF16)
        dy = cot_buf[part_rows, :].astype(F32)
        sums[s_ffn, :, :width] += fold8(dy)
        e = dy * vecs[gain2]
        d = r * (e - jnp.mean(e, -1, keepdims=True) - xh * jnp.mean(e * xh, -1, keepdims=True))
        resid[part_rows, :] = d
        d_low = d.astype(BF16)
        low[part_rows, :] = d_low
        sums[s_contract, :, :width] += fold8(d_low.astype(F32))

    loop(rows // 32, norm2_step)

    send_out = exchange(2, block_of(ctx_n), out.at[me])
    for peer in by_core:
        send_out(peer).start()
    fetch_start("out", block_of(ctx_n)(me), out.at[me])

    def contract_back_step(i):
        cols = ds(i * 512, 512)
        df = (dot_nt(low[...], wc[cols, :]) * big_b[:, cols].astype(F32)).astype(BF16)
        big_b[:, cols] = df
        sums[s_expand, :, cols] += fold8(df.astype(F32))

    loop(ff // 512, contract_back_step)

    def expand_back_step(i):
        cols = ds(i * 256, 256)
        resid[:, cols] += dot_nt(big_b[...], we[cols, :])

    loop(width // 256, expand_back_step)

    def norm1_step(i):
        part_rows = ds(i * 32, 32)
        dn = resid[part_rows, :]
        sums[s_attn, :, :width] += fold8(dn)
        e = dn * vecs[gain1]
        xh = xh1[part_rows, :]
        r = rstd1[part_rows, :1]
        d = r * (e - jnp.mean(e, -1, keepdims=True) - xh * jnp.mean(e * xh, -1, keepdims=True))
        resid[part_rows, :] = d
        d_low = d.astype(BF16)
        low[part_rows, :] = d_low
        sums[s_output, :, :width] += fold8(d_low.astype(F32))

    loop(rows // 32, norm1_step)

    expand_rows = ff // width
    early = [s_ffn, s_contract, s_attn, s_output]

    def send_partial(kind, slot, src, where):
        return pltpu.make_async_remote_copy(
            src_ref=red.at[kind, src],
            dst_ref=red_in.at[kind, slot],
            send_sem=red_send.at[kind, slot],
            recv_sem=red_recv.at[kind, slot],
            device_id=where,
            device_id_type=MESH,
        )

    group_copies = {}

    def reduce_start(kind):
        group_copies[kind] = [
            send_partial(kind, j - 1, 0, {"seq": flip(me, j)}) for j in peers
        ]
        for copy in group_copies[kind]:
            copy.start()

    def halving_copy(kind, step):
        return send_partial(kind, len(peers) + step, 1 + step, {"dp": flip(dp, dp_bits[step])})

    def reduce_group(kind):
        for copy in group_copies[kind]:
            copy.wait()
        total = jnp.zeros(red.shape[2:], F32)
        for member in range(group):
            piece = red[kind, 0]
            for j in peers:
                piece = jnp.where(flip(me, j) == member, red_in[kind, j - 1], piece)
            total = total + piece
        red[kind, 1] = total
        if dp_bits:
            halving_copy(kind, 0).start()

    def reduce_halving(kind, step):
        halving_copy(kind, step).wait()
        red[kind, 2 + step] = red[kind, 1 + step] + red_in[kind, len(peers) + step]
        if step + 1 < len(dp_bits):
            halving_copy(kind, step + 1).start()

    red[0, 0] = jnp.zeros(red.shape[2:], F32)
    red[1, 0] = jnp.zeros(red.shape[2:], F32)
    for i, which in enumerate(early):
        red[0, 0, i : i + 1, :] = jnp.sum(sums[which, :, :width], 0, keepdims=True)
    for i in range(expand_rows):
        red[0, 0, 4 + i : 5 + i, :] = jnp.sum(
            sums[s_expand, :, i * width : (i + 1) * width], 0, keepdims=True
        )
    reduce_start(0)

    def ctx_back_step(i):
        feats = ds(i * 256, 256)
        v_t[feats, :] = dot_nt(wo[feats, :], low[...]).astype(BF16)

    loop(width // 256, ctx_back_step)
    reduce_group(0)
    dq_n, dk_n, dv_n = (big_a.at[:, i * width : (i + 1) * width] for i in range(3))
    dscore_refs = (ds_a, ds_b)

    def dscore(p, j):
        lanes = ds(p * LANES, LANES)
        feats = ds(p * LANES + HEAD * j, HEAD)
        d = v_t[feats, :].astype(F32) * recip[pl.ds(2 * p + j, 1), :]
        inner = jnp.sum(d * ctx_t[feats, :].astype(F32), 0, keepdims=True)
        d_low = d.astype(BF16)
        zeros = jnp.zeros((HEAD, rows), BF16)
        padded = jnp.concatenate([d_low, zeros] if j == 0 else [zeros, d_low], 0)
        dprobs = dot_nn(v_n[:, lanes], padded)
        dscore_refs[j][...] = (probs[2 * p + j].astype(F32) * (dprobs - inner)).astype(BF16)
        return padded

    def attn_back_step(p):
        lanes = ds(p * LANES, LANES)
        padded = [dscore(p, j) for j in range(2)]
        dv = dot_nn(probs[2 * p], padded[0].T) + dot_nn(probs[2 * p + 1], padded[1].T)
        dv_n[:, lanes] = dv.astype(BF16)
        dqs, dks = [], []
        for j in range(2):
            feats = ds(p * LANES + HEAD * j, HEAD)
            dqs.append((dot_nn(k_t[feats, :], dscore_refs[j][...]) * scale).astype(BF16))
            dks.append(dot_nt(q_t[feats, :], dscore_refs[j][...]).astype(BF16))
        dq_n[:, lanes] = jnp.concatenate(dqs, 0).T
        dk_n[:, lanes] = jnp.concatenate(dks, 0).T

    cuts = len(dp_bits) + 1
    marks = [HEADS // 2 * i // cuts for i in range(cuts + 1)]
    for cut in range(cuts):
        lax.fori_loop(marks[cut], marks[cut + 1], lambda p, c: (attn_back_step(p), c)[1], 0)
        if cut < len(dp_bits):
            reduce_halving(0, cut)

    def bias_step(i):
        part_rows = ds(i * 64, 64)
        sums[s_query, :, :width] += fold8(dq_n[part_rows, :].astype(F32))
        sums[s_value, :, :width] += fold8(dv_n[part_rows, :].astype(F32))

    loop(rows // 64, bias_step)
    for i, which in enumerate((s_query, s_value)):
        red[1, 0, i : i + 1, :] = jnp.sum(sums[which, :, :width], 0, keepdims=True)
    reduce_start(1)

    def grad_step(peer):
        part_rows = ds(peer * part, part)
        g = (
            resid[part_rows, :]
            + dot_nt(dq_n[part_rows, :], wq[...])
            + dot_nt(dk_n[part_rows, :], wk[...])
            + dot_nt(dv_n[part_rows, :], wv[...])
        )
        x_buf[part_rows, :] = g.astype(BF16)

    send_grad = exchange(3, block_of(x_buf), grad_in.at[me])
    far = [flip(me, j) for j in range(2, group)]
    for peer in far + [flip(me, 1)]:
        grad_step(peer)
        send_grad(peer).start()
    grad_step(me)
    fetch_start("grad", x_buf.at[mine], grad_in.at[me])

    reduce_group(1)
    for step in range(len(dp_bits)):
        reduce_halving(1, step)
    final = 1 + len(dp_bits)
    small_out[0] = red[0, final] * factor
    small_out[1] = red[1, final] * factor

    for kind, dst in ((2, out), (3, grad_in)):
        for peer in members:
            arrived(kind, lambda member: dst.at[member], peer)
    for send in (send_x, send_cot, send_out, send_grad):
        for peer in members:
            send(peer).wait_send()
    fetch["out"].wait()
    fetch["grad"].wait()


def finish(
    early_out,
    early_grad,
    early_small,
    out,
    grad_in,
    g_bias_query,
    g_bias_value,
    g_bias_output,
    g_shift_attn,
    g_bias_expand,
    g_bias_contract,
    g_shift_ffn,
    held,
    sem_in,
    sem_out,
):
    pairs = [
        (src.at[i], dst.at[i], n * early_out.shape[0] + i)
        for n, (src, dst) in enumerate(((early_out, out), (early_grad, grad_in)))
        for i in range(early_out.shape[0])
    ]
    takes = [pltpu.make_async_copy(src, held.at[n], sem_in.at[n]) for src, _, n in pairs]
    puts = [pltpu.make_async_copy(held.at[n], dst, sem_out.at[n]) for _, dst, n in pairs]
    for take in takes:
        take.start()
    width = early_small.shape[-1]
    for i, ref in enumerate((g_shift_ffn, g_bias_contract, g_shift_attn, g_bias_output)):
        ref[...] = early_small[0, i : i + 1, :]
    for i in range(g_bias_expand.shape[1] // width):
        g_bias_expand[:, i * width : (i + 1) * width] = early_small[0, 4 + i : 5 + i, :]
    for i, ref in enumerate((g_bias_query, g_bias_value)):
        ref[...] = early_small[1, i : i + 1, :]
    for take, put in zip(takes, puts):
        take.wait()
        put.start()
    for put in puts:
        put.wait()


def local(mesh, *args):
    hidden_in, lengths = args[:2]
    group, dp_size = mesh.shape["seq"], mesh.shape["dp"]
    seqs, part, width = hidden_in.shape
    ff = args[7].shape[1]
    rows = part * group
    assert seqs == group
    assert group & (group - 1) == 0 and dp_size & (dp_size - 1) == 0
    factor = (rows * seqs // group * dp_size * group) ** (-0.5)
    steps = dp_size.bit_length() - 1
    anywhere = pl.BlockSpec(memory_space=pl.ANY)
    in_specs = [anywhere] * len(args)
    in_specs[1] = pl.BlockSpec(memory_space=pltpu.SMEM)
    vmem = pl.BlockSpec(memory_space=pltpu.VMEM)
    operands = [a.reshape(1, -1) if a.ndim == 1 and i != 1 else a for i, a in enumerate(args)]
    row = jax.ShapeDtypeStruct((1, width), F32)
    outs = pl.pallas_call(
        functools.partial(kernel, group, dp_size, factor),
        out_shape=[jax.ShapeDtypeStruct(hidden_in.shape, BF16)] * 2
        + [jax.ShapeDtypeStruct((2, 8, width), F32)],
        in_specs=in_specs,
        out_specs=[anywhere] * 2 + [vmem],
        scratch_shapes=[
            pltpu.VMEM((width, width), BF16),
            pltpu.VMEM((width, width), BF16),
            pltpu.VMEM((width, width), BF16),
            pltpu.VMEM((width, width), BF16),
            pltpu.VMEM((width, ff), BF16),
            pltpu.VMEM((ff, width), BF16),
            pltpu.VMEM((8, 1, width), F32),
            pltpu.VMEM((1, ff), F32),
            pltpu.VMEM((rows, width), BF16),
            pltpu.VMEM((rows, width), BF16),
            pltpu.VMEM((width, rows), BF16),
            pltpu.VMEM((rows, width), BF16),
            pltpu.VMEM((width, rows), BF16),
            pltpu.VMEM((rows, width), BF16),
            pltpu.VMEM((width, rows), BF16),
            pltpu.VMEM((HEADS, rows, rows), BF16),
            pltpu.VMEM((HEADS, rows), F32),
            pltpu.VMEM((width, rows), BF16),
            pltpu.VMEM((rows, width), BF16),
            pltpu.VMEM((rows, width), F32),
            pltpu.VMEM((rows, LANES), F32),
            pltpu.VMEM((rows, width), BF16),
            pltpu.VMEM((rows, ff), BF16),
            pltpu.VMEM((rows, ff), BF16),
            pltpu.VMEM((rows, width), F32),
            pltpu.VMEM((rows, rows), F32),
            pltpu.VMEM((rows, rows), F32),
            pltpu.VMEM((1, rows), F32),
            pltpu.VMEM((1, rows), F32),
            pltpu.VMEM((rows, rows), BF16),
            pltpu.VMEM((rows, rows), BF16),
            pltpu.VMEM((2, rows, LANES), BF16),
            pltpu.VMEM((7, 8, ff), F32),
            pltpu.VMEM((2, 2 + steps, 8, width), F32),
            pltpu.VMEM((2, group - 1 + steps, 8, width), F32),
            pltpu.SemaphoreType.DMA((24,)),
            pltpu.SemaphoreType.DMA((4, group)),
            pltpu.SemaphoreType.DMA((4, group)),
            pltpu.SemaphoreType.DMA((2, group - 1 + steps)),
            pltpu.SemaphoreType.DMA((2, group - 1 + steps)),
        ],
        compiler_params=pltpu.CompilerParams(
            collective_id=0, has_side_effects=True, vmem_limit_bytes=67043328
        ),
        name="layer",
    )(*operands)
    blocks = 2 * seqs
    outs = pl.pallas_call(
        finish,
        out_shape=[jax.ShapeDtypeStruct(hidden_in.shape, BF16)] * 2
        + [row] * 4
        + [jax.ShapeDtypeStruct((1, ff), F32), row, row],
        in_specs=[anywhere, anywhere, vmem],
        out_specs=[anywhere] * 2 + [vmem] * 7,
        scratch_shapes=[
            pltpu.VMEM((blocks, part, width), BF16),
            pltpu.SemaphoreType.DMA((blocks,)),
            pltpu.SemaphoreType.DMA((blocks,)),
        ],
        name="finish",
    )(*outs)
    return tuple(o.reshape(-1) if o.shape[0] == 1 else o for o in outs)


def solution(mesh):
    placed = (P("dp", "seq", None), P("dp")) + (P(),) * 15 + (P("dp", "seq", None),)
    return jax.shard_map(
        functools.partial(local, mesh),
        mesh=mesh,
        in_specs=placed,
        out_specs=(P("dp", "seq", None), P("dp", "seq", None), P(), P(), P(), P(), P(), P(), P()),
        check_vma=False,
    )
```

```python
import functools

import jax
import jax.numpy as jnp
from jax import lax
from jax.experimental import pallas as pl
from jax.experimental.pallas import tpu as pltpu
from jax.sharding import PartitionSpec as P

HEADS = 16
HEAD = 64
NEG = -1e30
EPSILON = 1e-12
LANES = 128
MESH = pl.DeviceIdType.MESH
F32 = jnp.float32
BF16 = jnp.bfloat16


def dot_nn(left, right):
    return jnp.dot(left, right, preferred_element_type=F32)


def dot_nt(left, right):
    return lax.dot_general(left, right, (((1,), (1,)), ((), ())), preferred_element_type=F32)


def flip(index, mask):
    bit = 1
    while bit <= mask:
        if mask & bit:
            index = index + bit - 2 * bit * ((index // bit) % 2)
        bit *= 2
    return index


def ds(start, size):
    return pl.ds(start if isinstance(start, int) else pl.multiple_of(start, size), size)


def dp_rounds(size):
    rounds, low = [], 1
    while low < size:
        high = min(low * 8, size)
        rounds.append([m * low for m in range(1, high // low)])
        low = high
    return rounds


def fold8(value):
    rows, width = value.shape
    return jnp.sum(value.reshape(rows // 8, 8, width), 0)


def loop(count, body):
    def step(index, carry):
        body(index)
        return carry

    lax.fori_loop(0, count, step, 0)


def kernel(
    group,
    dp_size,
    factor,
    hidden_in,
    lengths,
    w_query,
    w_key,
    w_value,
    w_output,
    gain_attn,
    w_expand,
    w_contract,
    gain_ffn,
    bias_query,
    bias_value,
    bias_output,
    shift_attn,
    bias_expand,
    bias_contract,
    shift_ffn,
    cotangent,
    out,
    grad_in,
    small_out,
    late_out,
    wq,
    wk,
    wv,
    wo,
    we,
    wc,
    vecs,
    vec_expand,
    x_buf,
    cot_buf,
    q_t,
    k_n,
    k_t,
    v_n,
    v_t,
    probs,
    recip,
    ctx_t,
    ctx_n,
    xh1,
    rstd1,
    low,
    big_a,
    big_b,
    resid,
    s_a,
    s_b,
    top_a,
    top_b,
    ds_a,
    ds_b,
    key_bias,
    sums,
    red,
    red_in,
    red_late,
    red_late_in,
    local_sem,
    send_sem,
    recv_sem,
    red_send,
    red_recv,
):
    me = lax.axis_index("seq")
    dp = lax.axis_index("dp")
    part = hidden_in.shape[1]
    rows, width = x_buf.shape
    ff = we.shape[1]
    peers = list(range(1, group))
    members = [flip(me, j) for j in peers]
    core = me % 2
    by_core = [flip(me, 1)] + [
        flip(me, hi) - core + c for c in range(2) for hi in range(2, group, 2)
    ]
    rounds = dp_rounds(dp_size)
    dp_masks = [m for masks in rounds for m in masks]

    small = (
        bias_query,
        bias_value,
        bias_output,
        gain_attn,
        shift_attn,
        bias_contract,
        gain_ffn,
        shift_ffn,
    )
    b_q, b_v, b_o, gain1, shift1, b_c, gain2, shift2 = range(8)
    fetch = {}

    def fetch_start(name, src, dst):
        fetch[name] = pltpu.make_async_copy(src, dst, local_sem.at[len(fetch)])
        fetch[name].start()

    mine = ds(me * part, part)
    fetch_start("x", hidden_in.at[me], x_buf.at[mine])
    fetch_start("wq", w_query, wq)
    fetch_start("wk", w_key, wk)
    fetch_start("wv", w_value, wv)

    barrier = pltpu.get_barrier_semaphore()
    for j in peers:
        pl.semaphore_signal(barrier, inc=1, device_id={"seq": flip(me, j)}, device_id_type=MESH)
    for m in dp_masks:
        pl.semaphore_signal(barrier, inc=1, device_id={"dp": flip(dp, m)}, device_id_type=MESH)
    pl.semaphore_wait(barrier, len(peers) + len(dp_masks))

    def exchange(kind, src_of, dst):
        def send(peer):
            return pltpu.make_async_remote_copy(
                src_ref=src_of(peer),
                dst_ref=dst,
                send_sem=send_sem.at[kind, peer],
                recv_sem=recv_sem.at[kind, me],
                device_id={"seq": peer},
                device_id_type=MESH,
            )

        return send

    def block_of(buf):
        return lambda peer: buf.at[ds(peer * part, part)]

    def arrived(kind, dst_of, peer):
        pltpu.make_async_remote_copy(
            src_ref=dst_of(peer),
            dst_ref=dst_of(peer),
            send_sem=send_sem.at[kind, peer],
            recv_sem=recv_sem.at[kind, peer],
            device_id={"seq": peer},
            device_id_type=MESH,
        ).wait_recv()

    send_x = exchange(0, lambda peer: hidden_in.at[peer], x_buf.at[mine])
    for peer in by_core:
        send_x(peer).start()
    for i, vec in enumerate(small):
        fetch_start(("v", i), vec, vecs.at[i])
    fetch_start("be", bias_expand, vec_expand)
    fetch_start("wo", w_output, wo)
    fetch_start("we", w_expand, we)
    send_cot = exchange(1, lambda peer: cotangent.at[peer], cot_buf.at[mine])
    for peer in by_core:
        send_cot(peer).start()
    fetch_start("cot", cotangent.at[me], cot_buf.at[mine])
    fetch_start("wc", w_contract, wc)

    sums[...] = jnp.zeros_like(sums)
    s_ffn, s_contract, s_attn, s_output, s_query, s_value, s_expand = range(7)

    scale = HEAD ** (-0.5)
    pair = 2 * part

    def qkv(base):
        here = ds(base, pair)
        xs = x_buf[here, :]

        def step(i):
            cols = ds(i * 256, 256)
            q = ((dot_nn(xs, wq[:, cols]) + vecs[b_q, :, cols]) * scale).astype(BF16)
            q_t[cols, here] = q.T
            k = dot_nn(xs, wk[:, cols]).astype(BF16)
            k_n[here, cols] = k
            k_t[cols, here] = k.T
            v = (dot_nn(xs, wv[:, cols]) + vecs[b_v, :, cols]).astype(BF16)
            v_n[here, cols] = v
            v_t[cols, here] = v.T

        loop(width // 256, step)

    length = lengths[me]
    row = lax.broadcasted_iota(jnp.int32, (rows, LANES), 0)
    lane = lax.broadcasted_iota(jnp.int32, (rows, LANES), 1)
    for j in range(2):
        key_bias[j] = jnp.where((row >= length) & (lane == HEAD * (1 - j)), NEG, 0.0).astype(BF16)

    for i in range(len(small)):
        fetch["v", i].wait()
    fetch["x"].wait()
    fetch["wq"].wait()
    fetch["wk"].wait()
    fetch["wv"].wait()
    arrived(0, block_of(x_buf), flip(me, 1))
    qkv((me - core) * part)
    for hi in range(2, group, 2):
        for c in range(2):
            arrived(0, block_of(x_buf), flip(me, hi) - core + c)
        qkv((flip(me, hi) - core) * part)

    score_refs, top_refs = (s_a, s_b), (top_a, top_b)

    def score(p, j):
        lanes = ds(p * LANES, LANES)
        half = lax.broadcasted_iota(jnp.int32, (rows, LANES), 1) < HEAD
        k_one = jnp.where(half if j == 0 else ~half, k_n[:, lanes], key_bias[j])
        q_one = q_t[ds(p * LANES + HEAD * j, HEAD), :]
        pad = [jnp.ones((16, rows), BF16), jnp.zeros((HEAD - 16, rows), BF16)]
        q_one = jnp.concatenate([q_one] + pad if j == 0 else pad + [q_one], 0)
        for c in range(0, rows, 256):
            cols = slice(c, c + 256)
            block = dot_nn(k_one, q_one[:, cols])
            score_refs[j][:, cols] = block
            top_refs[j][:, cols] = jnp.max(block, 0, keepdims=True)

    def exponential(h, j):
        for c in range(0, rows, 256):
            cols = slice(c, c + 256)
            probs[h, :, cols] = jnp.exp(score_refs[j][:, cols] - top_refs[j][:, cols]).astype(BF16)

    def weigh(h):
        feats = ds(h * HEAD, HEAD)
        o = dot_nn(jnp.concatenate([v_t[feats, :], jnp.ones((16, rows), BF16)], 0), probs[h])
        inv = 1.0 / o[HEAD : HEAD + 1]
        recip[pl.ds(h, 1), :] = inv
        ctx_t[feats, :] = (o[:HEAD] * inv).astype(BF16)

    def turn(p):
        lanes = ds(p * LANES, LANES)
        ctx_n[:, lanes] = ctx_t[lanes, :].T

    score(0, 0)
    exponential(0, 0)
    score(0, 1)

    def attn_step(p):
        exponential(2 * p + 1, 1)
        score(p + 1, 0)
        weigh(2 * p)
        exponential(2 * p + 2, 0)
        score(p + 1, 1)
        weigh(2 * p + 1)
        turn(p)

    loop(HEADS // 2 - 1, attn_step)
    exponential(HEADS - 1, 1)
    weigh(HEADS - 2)
    weigh(HEADS - 1)
    turn(HEADS // 2 - 1)

    fetch["wo"].wait()

    def out_proj_step(i):
        part_rows = ds(i * 256, 256)
        ao = dot_nn(ctx_n[part_rows, :], wo[...]) + vecs[b_o]
        h = x_buf[part_rows, :].astype(F32) + ao
        center = h - jnp.mean(h, -1, keepdims=True)
        r = lax.rsqrt(jnp.mean(center * center, -1, keepdims=True) + EPSILON)
        xh = center * r
        xh1[part_rows, :] = xh
        rstd1[part_rows, :] = jnp.broadcast_to(r, (256, LANES))
        low[part_rows, :] = (xh * vecs[gain1] + vecs[shift1]).astype(BF16)

    loop(rows // 256, out_proj_step)

    fetch["we"].wait()
    fetch["be"].wait()

    def expand(i):
        cols = ds(i * 512, 512)
        s_a[...] = dot_nn(low[...], we[:, cols]) + vec_expand[:, cols]

    def gelu(i):
        cols = ds(i * 512, 512)
        f = s_a[...]
        phi = 0.5 * (1.0 + lax.erf(f * (0.5**0.5)))
        big_a[:, cols] = (f * phi).astype(BF16)
        dens = jnp.exp(f * f * -0.5) * (0.5 / jnp.pi) ** 0.5
        big_b[:, cols] = (phi + f * dens).astype(BF16)

    expand(0)

    def expand_step(i):
        gelu(i)
        expand(i + 1)

    loop(ff // 512 - 1, expand_step)
    gelu(ff // 512 - 1)
    fetch["wc"].wait()

    def contract_step(i):
        cols = ds(i * 256, 256)
        n1 = xh1[:, cols] * vecs[gain1, :, cols] + vecs[shift1, :, cols]
        resid[:, cols] = n1 + dot_nn(big_a[...], wc[:, cols]) + vecs[b_c, :, cols]

    loop(width // 256, contract_step)

    fetch["cot"].wait()
    for peer in members:
        arrived(1, block_of(cot_buf), peer)

    def norm2_step(i):
        part_rows = ds(i * 32, 32)
        h = resid[part_rows, :]
        center = h - jnp.mean(h, -1, keepdims=True)
        r = lax.rsqrt(jnp.mean(center * center, -1, keepdims=True) + EPSILON)
        xh = center * r
        ctx_n[part_rows, :] = (xh * vecs[gain2] + vecs[shift2]).astype(BF16)
        dy = cot_buf[part_rows, :].astype(F32)
        sums[s_ffn, :, :width] += fold8(dy)
        e = dy * vecs[gain2]
        d = r * (e - jnp.mean(e, -1, keepdims=True) - xh * jnp.mean(e * xh, -1, keepdims=True))
        resid[part_rows, :] = d
        d_low = d.astype(BF16)
        low[part_rows, :] = d_low
        sums[s_contract, :, :width] += fold8(d_low.astype(F32))

    loop(rows // 32, norm2_step)

    send_out = exchange(2, block_of(ctx_n), out.at[me])
    for peer in by_core:
        send_out(peer).start()
    fetch_start("out", block_of(ctx_n)(me), out.at[me])

    def contract_back_step(i):
        cols = ds(i * 512, 512)
        df = (dot_nt(low[...], wc[cols, :]) * big_b[:, cols].astype(F32)).astype(BF16)
        big_b[:, cols] = df
        sums[s_expand, :, cols] += fold8(df.astype(F32))

    loop(ff // 512, contract_back_step)

    def expand_back_step(i):
        cols = ds(i * 256, 256)
        resid[:, cols] += dot_nt(big_b[...], we[cols, :])

    loop(width // 256, expand_back_step)

    def norm1_step(i):
        part_rows = ds(i * 32, 32)
        dn = resid[part_rows, :]
        sums[s_attn, :, :width] += fold8(dn)
        e = dn * vecs[gain1]
        xh = xh1[part_rows, :]
        r = rstd1[part_rows, :1]
        d = r * (e - jnp.mean(e, -1, keepdims=True) - xh * jnp.mean(e * xh, -1, keepdims=True))
        resid[part_rows, :] = d
        d_low = d.astype(BF16)
        low[part_rows, :] = d_low
        sums[s_output, :, :width] += fold8(d_low.astype(F32))

    loop(rows // 32, norm1_step)

    expand_rows = ff // width
    early = [s_ffn, s_contract, s_attn, s_output]

    partials, received = (red, red_late), (red_in, red_late_in)

    def send_partial(kind, slot, src, where):
        return pltpu.make_async_remote_copy(
            src_ref=partials[kind].at[src],
            dst_ref=received[kind].at[slot],
            send_sem=red_send.at[kind, slot],
            recv_sem=red_recv.at[kind, slot],
            device_id=where,
            device_id_type=MESH,
        )

    def round_copies(kind, which):
        if which == 0:
            return [send_partial(kind, j - 1, 0, {"seq": flip(me, j)}) for j in peers]
        first = len(peers) + sum(len(masks) for masks in rounds[: which - 1])
        return [
            send_partial(kind, first + i, which, {"dp": flip(dp, m)})
            for i, m in enumerate(rounds[which - 1])
        ]

    def reduce_start(kind, which=0):
        for copy in round_copies(kind, which):
            copy.start()

    def reduce_end(kind, which):
        for copy in round_copies(kind, which):
            copy.wait()
        first = len(peers) + sum(len(masks) for masks in rounds[: which - 1]) if which else 0
        count = len(peers) if which == 0 else len(rounds[which - 1])
        parts = [partials[kind][which]] + [received[kind][first + i] for i in range(count)]
        while len(parts) > 1:
            parts = [parts[i] + parts[i + 1] for i in range(0, len(parts), 2)]
        partials[kind][which + 1] = parts[0]
        if which < len(rounds):
            reduce_start(kind, which + 1)

    for i, which in enumerate(early):
        red[0, i : i + 1, :] = jnp.sum(sums[which, :, :width], 0, keepdims=True)
    for i in range(expand_rows):
        red[0, 4 + i : 5 + i, :] = jnp.sum(
            sums[s_expand, :, i * width : (i + 1) * width], 0, keepdims=True
        )
    reduce_start(0)

    def ctx_back_step(i):
        feats = ds(i * 256, 256)
        v_t[feats, :] = dot_nt(wo[feats, :], low[...]).astype(BF16)

    loop(width // 256, ctx_back_step)
    dq_n, dk_n, dv_n = (big_a.at[:, i * width : (i + 1) * width] for i in range(3))
    dscore_refs = (ds_a, ds_b)

    def dscore(p, j):
        lanes = ds(p * LANES, LANES)
        feats = ds(p * LANES + HEAD * j, HEAD)
        d = v_t[feats, :].astype(F32) * recip[pl.ds(2 * p + j, 1), :]
        inner = jnp.sum(d * ctx_t[feats, :].astype(F32), 0, keepdims=True)
        d_low = d.astype(BF16)
        zeros = jnp.zeros((HEAD, rows), BF16)
        padded = jnp.concatenate([d_low, zeros] if j == 0 else [zeros, d_low], 0)
        dprobs = dot_nn(v_n[:, lanes], padded)
        dscore_refs[j][...] = (probs[2 * p + j].astype(F32) * (dprobs - inner)).astype(BF16)
        return padded

    def attn_back_step(p):
        lanes = ds(p * LANES, LANES)
        padded = [dscore(p, j) for j in range(2)]
        dv = dot_nn(probs[2 * p], padded[0].T) + dot_nn(probs[2 * p + 1], padded[1].T)
        dqs, dks = [], []
        for j in range(2):
            feats = ds(p * LANES + HEAD * j, HEAD)
            dqs.append((dot_nn(k_t[feats, :], dscore_refs[j][...]) * scale).astype(BF16))
            dks.append(dot_nt(q_t[feats, :], dscore_refs[j][...]).astype(BF16))
        dq_low, dv_low = jnp.concatenate(dqs, 0).T, dv.astype(BF16)
        dq_n[:, lanes] = dq_low
        dk_n[:, lanes] = jnp.concatenate(dks, 0).T
        dv_n[:, lanes] = dv_low
        sums[s_query, :, lanes] = fold8(dq_low.astype(F32))
        sums[s_value, :, lanes] = fold8(dv_low.astype(F32))

    pairs, late = HEADS // 2, HEADS // 2 - 2
    loop(late, attn_back_step)
    reduce_end(0, 0)
    loop(pairs - late, lambda i: attn_back_step(late + i))
    quarter = width // 4
    for i, which in enumerate((s_query, s_value)):
        for j in range(4):
            red_late[0, 4 * i + j : 4 * i + j + 1, :] = jnp.sum(
                sums[which, :, j * quarter : (j + 1) * quarter], 0, keepdims=True
            )
    reduce_start(1)

    def grad_step(peer):
        part_rows = ds(peer * part, part)
        g = (
            resid[part_rows, :]
            + dot_nt(dq_n[part_rows, :], wq[...])
            + dot_nt(dk_n[part_rows, :], wk[...])
            + dot_nt(dv_n[part_rows, :], wv[...])
        )
        x_buf[part_rows, :] = g.astype(BF16)

    send_grad = exchange(3, block_of(x_buf), grad_in.at[me])
    order = [flip(me, j) for j in range(2, group)] + [flip(me, 1)]
    for i, peer in enumerate(order):
        grad_step(peer)
        send_grad(peer).start()
        if i == 1:
            reduce_end(1, 0)
    grad_step(me)
    fetch_start("grad", x_buf.at[mine], grad_in.at[me])

    for which in range(1, len(rounds) + 1):
        for kind in range(2):
            reduce_end(kind, which)
    final = 1 + len(rounds)
    small_out[...] = red[final] * factor
    late_out[...] = red_late[final] * factor

    for kind, dst in ((2, out), (3, grad_in)):
        for peer in members:
            arrived(kind, lambda member: dst.at[member], peer)
    for send in (send_x, send_cot, send_out, send_grad):
        for peer in members:
            send(peer).wait_send()
    fetch["out"].wait()
    fetch["grad"].wait()


def finish(
    early_out,
    early_grad,
    early_small,
    late_small,
    out,
    grad_in,
    g_bias_query,
    g_bias_value,
    g_bias_output,
    g_shift_attn,
    g_bias_expand,
    g_bias_contract,
    g_shift_ffn,
    held,
    sem_in,
    sem_out,
):
    pairs = [
        (src.at[i], dst.at[i], n * early_out.shape[0] + i)
        for n, (src, dst) in enumerate(((early_out, out), (early_grad, grad_in)))
        for i in range(early_out.shape[0])
    ]
    takes = [pltpu.make_async_copy(src, held.at[n], sem_in.at[n]) for src, _, n in pairs]
    puts = [pltpu.make_async_copy(held.at[n], dst, sem_out.at[n]) for _, dst, n in pairs]
    for take in takes:
        take.start()
    width = early_small.shape[-1]
    for i, ref in enumerate((g_shift_ffn, g_bias_contract, g_shift_attn, g_bias_output)):
        ref[...] = early_small[i : i + 1, :]
    for i in range(g_bias_expand.shape[1] // width):
        g_bias_expand[:, i * width : (i + 1) * width] = early_small[4 + i : 5 + i, :]
    for i, ref in enumerate((g_bias_query, g_bias_value)):
        for j in range(4):
            ref[:, j * width // 4 : (j + 1) * width // 4] = late_small[4 * i + j : 4 * i + j + 1, :]
    for take, put in zip(takes, puts):
        take.wait()
        put.start()
    for put in puts:
        put.wait()


def local(mesh, *args):
    hidden_in, lengths = args[:2]
    group, dp_size = mesh.shape["seq"], mesh.shape["dp"]
    seqs, part, width = hidden_in.shape
    ff = args[7].shape[1]
    rows = part * group
    assert seqs == group
    assert group & (group - 1) == 0 and dp_size & (dp_size - 1) == 0
    factor = (rows * seqs // group * dp_size * group) ** (-0.5)
    rounds = dp_rounds(dp_size)
    slots = group - 1 + sum(len(masks) for masks in rounds)
    anywhere = pl.BlockSpec(memory_space=pl.ANY)
    in_specs = [anywhere] * len(args)
    in_specs[1] = pl.BlockSpec(memory_space=pltpu.SMEM)
    vmem = pl.BlockSpec(memory_space=pltpu.VMEM)
    operands = [a.reshape(1, -1) if a.ndim == 1 and i != 1 else a for i, a in enumerate(args)]
    row = jax.ShapeDtypeStruct((1, width), F32)
    outs = pl.pallas_call(
        functools.partial(kernel, group, dp_size, factor),
        out_shape=[jax.ShapeDtypeStruct(hidden_in.shape, BF16)] * 2
        + [jax.ShapeDtypeStruct((8, width), F32), jax.ShapeDtypeStruct((8, width // 4), F32)],
        in_specs=in_specs,
        out_specs=[anywhere] * 2 + [vmem] * 2,
        scratch_shapes=[
            pltpu.VMEM((width, width), BF16),
            pltpu.VMEM((width, width), BF16),
            pltpu.VMEM((width, width), BF16),
            pltpu.VMEM((width, width), BF16),
            pltpu.VMEM((width, ff), BF16),
            pltpu.VMEM((ff, width), BF16),
            pltpu.VMEM((8, 1, width), F32),
            pltpu.VMEM((1, ff), F32),
            pltpu.VMEM((rows, width), BF16),
            pltpu.VMEM((rows, width), BF16),
            pltpu.VMEM((width, rows), BF16),
            pltpu.VMEM((rows, width), BF16),
            pltpu.VMEM((width, rows), BF16),
            pltpu.VMEM((rows, width), BF16),
            pltpu.VMEM((width, rows), BF16),
            pltpu.VMEM((HEADS, rows, rows), BF16),
            pltpu.VMEM((HEADS, rows), F32),
            pltpu.VMEM((width, rows), BF16),
            pltpu.VMEM((rows, width), BF16),
            pltpu.VMEM((rows, width), F32),
            pltpu.VMEM((rows, LANES), F32),
            pltpu.VMEM((rows, width), BF16),
            pltpu.VMEM((rows, ff), BF16),
            pltpu.VMEM((rows, ff), BF16),
            pltpu.VMEM((rows, width), F32),
            pltpu.VMEM((rows, rows), F32),
            pltpu.VMEM((rows, rows), F32),
            pltpu.VMEM((1, rows), F32),
            pltpu.VMEM((1, rows), F32),
            pltpu.VMEM((rows, rows), BF16),
            pltpu.VMEM((rows, rows), BF16),
            pltpu.VMEM((2, rows, LANES), BF16),
            pltpu.VMEM((7, 8, ff), F32),
            pltpu.VMEM((2 + len(rounds), 8, width), F32),
            pltpu.VMEM((slots, 8, width), F32),
            pltpu.VMEM((2 + len(rounds), 8, width // 4), F32),
            pltpu.VMEM((slots, 8, width // 4), F32),
            pltpu.SemaphoreType.DMA((24,)),
            pltpu.SemaphoreType.DMA((4, group)),
            pltpu.SemaphoreType.DMA((4, group)),
            pltpu.SemaphoreType.DMA((2, slots)),
            pltpu.SemaphoreType.DMA((2, slots)),
        ],
        compiler_params=pltpu.CompilerParams(
            collective_id=0, has_side_effects=True, vmem_limit_bytes=67043328
        ),
        name="layer",
    )(*operands)
    blocks = 2 * seqs
    outs = pl.pallas_call(
        finish,
        out_shape=[jax.ShapeDtypeStruct(hidden_in.shape, BF16)] * 2
        + [row] * 4
        + [jax.ShapeDtypeStruct((1, ff), F32), row, row],
        in_specs=[anywhere, anywhere, vmem, vmem],
        out_specs=[anywhere] * 2 + [vmem] * 7,
        scratch_shapes=[
            pltpu.VMEM((blocks, part, width), BF16),
            pltpu.SemaphoreType.DMA((blocks,)),
            pltpu.SemaphoreType.DMA((blocks,)),
        ],
        name="finish",
    )(*outs)
    return tuple(o.reshape(-1) if o.shape[0] == 1 else o for o in outs)


def solution(mesh):
    placed = (P("dp", "seq", None), P("dp")) + (P(),) * 15 + (P("dp", "seq", None),)
    return jax.shard_map(
        functools.partial(local, mesh),
        mesh=mesh,
        in_specs=placed,
        out_specs=(P("dp", "seq", None), P("dp", "seq", None), P(), P(), P(), P(), P(), P(), P()),
        check_vma=False,
    )
```

```python
import functools

import jax
import jax.numpy as jnp
from jax import lax
from jax.experimental import pallas as pl
from jax.experimental.pallas import tpu as pltpu
from jax.sharding import PartitionSpec as P

HEADS = 16
HEAD = 64
NEG = -1e30
EPSILON = 1e-12
LANES = 128
MESH = pl.DeviceIdType.MESH
F32 = jnp.float32
BF16 = jnp.bfloat16


def dot_nn(left, right):
    return jnp.dot(left, right, preferred_element_type=F32)


def dot_nt(left, right):
    return lax.dot_general(left, right, (((1,), (1,)), ((), ())), preferred_element_type=F32)


def flip(index, mask):
    bit = 1
    while bit <= mask:
        if mask & bit:
            index = index + bit - 2 * bit * ((index // bit) % 2)
        bit *= 2
    return index


def ds(start, size):
    return pl.ds(start if isinstance(start, int) else pl.multiple_of(start, size), size)


def dp_rounds(size):
    rounds, low = [], 1
    while low < size:
        high = min(low * 8, size)
        rounds.append([m * low for m in range(1, high // low)])
        low = high
    return rounds


def fold8(value):
    rows, width = value.shape
    return jnp.sum(value.reshape(rows // 8, 8, width), 0)


def loop(count, body):
    def step(index, carry):
        body(index)
        return carry

    lax.fori_loop(0, count, step, 0)


def kernel(
    group,
    dp_size,
    factor,
    hidden_in,
    lengths,
    w_query,
    w_key,
    w_value,
    w_output,
    gain_attn,
    w_expand,
    w_contract,
    gain_ffn,
    bias_query,
    bias_value,
    bias_output,
    shift_attn,
    bias_expand,
    bias_contract,
    shift_ffn,
    cotangent,
    out,
    grad_in,
    small_out,
    late_out,
    wq,
    wk,
    wv,
    wo,
    we,
    wc,
    vecs,
    vec_expand,
    x_buf,
    cot_buf,
    q_t,
    k_n,
    k_t,
    v_n,
    v_t,
    probs,
    recip,
    ctx_t,
    ctx_n,
    xh1,
    rstd1,
    low,
    big_a,
    big_b,
    resid,
    s_a,
    s_b,
    top_a,
    top_b,
    ds_a,
    ds_b,
    key_bias,
    sums,
    sum_expand,
    red,
    red_in,
    red_late,
    red_late_in,
    local_sem,
    send_sem,
    recv_sem,
    red_send,
    red_recv,
):
    me = lax.axis_index("seq")
    dp = lax.axis_index("dp")
    part = hidden_in.shape[1]
    rows, width = x_buf.shape
    ff = we.shape[1]
    peers = list(range(1, group))
    members = [flip(me, j) for j in peers]
    core = me % 2
    by_core = [flip(me, 1)] + [
        flip(me, hi) - core + c for c in range(2) for hi in range(2, group, 2)
    ]
    rounds = dp_rounds(dp_size)
    dp_masks = [m for masks in rounds for m in masks]

    small = (
        bias_query,
        bias_value,
        bias_output,
        gain_attn,
        shift_attn,
        bias_contract,
        gain_ffn,
        shift_ffn,
    )
    b_q, b_v, b_o, gain1, shift1, b_c, gain2, shift2 = range(8)
    fetch = {}

    def fetch_start(name, src, dst):
        fetch[name] = pltpu.make_async_copy(src, dst, local_sem.at[len(fetch)])
        fetch[name].start()

    mine = ds(me * part, part)
    fetch_start("x", hidden_in.at[me], x_buf.at[mine])
    fetch_start("wq", w_query, wq)
    fetch_start("wk", w_key, wk)
    fetch_start("wv", w_value, wv)

    barrier = pltpu.get_barrier_semaphore()
    for j in peers:
        pl.semaphore_signal(barrier, inc=1, device_id={"seq": flip(me, j)}, device_id_type=MESH)
    for m in dp_masks:
        pl.semaphore_signal(barrier, inc=1, device_id={"dp": flip(dp, m)}, device_id_type=MESH)
    pl.semaphore_wait(barrier, len(peers) + len(dp_masks))

    def exchange(kind, src_of, dst):
        def send(peer):
            return pltpu.make_async_remote_copy(
                src_ref=src_of(peer),
                dst_ref=dst,
                send_sem=send_sem.at[kind, peer],
                recv_sem=recv_sem.at[kind, me],
                device_id={"seq": peer},
                device_id_type=MESH,
            )

        return send

    def block_of(buf):
        return lambda peer: buf.at[ds(peer * part, part)]

    def arrived(kind, dst_of, peer):
        pltpu.make_async_remote_copy(
            src_ref=dst_of(peer),
            dst_ref=dst_of(peer),
            send_sem=send_sem.at[kind, peer],
            recv_sem=recv_sem.at[kind, peer],
            device_id={"seq": peer},
            device_id_type=MESH,
        ).wait_recv()

    send_x = exchange(0, lambda peer: hidden_in.at[peer], x_buf.at[mine])
    for peer in by_core:
        send_x(peer).start()
    for i, vec in enumerate(small):
        fetch_start(("v", i), vec, vecs.at[i])
    fetch_start("be", bias_expand, vec_expand)
    fetch_start("wo", w_output, wo)
    fetch_start("we", w_expand, we)
    send_cot = exchange(1, lambda peer: cotangent.at[peer], cot_buf.at[mine])
    for peer in by_core:
        send_cot(peer).start()
    fetch_start("cot", cotangent.at[me], cot_buf.at[mine])
    fetch_start("wc", w_contract, wc)

    sums[...] = jnp.zeros_like(sums)
    sum_expand[...] = jnp.zeros_like(sum_expand)
    s_ffn, s_contract, s_attn, s_output, s_query, s_value = range(6)

    scale = HEAD ** (-0.5)
    pair = 2 * part

    def qkv(base):
        here = ds(base, pair)
        xs = x_buf[here, :]

        def step(i):
            cols = ds(i * 256, 256)
            q = ((dot_nn(xs, wq[:, cols]) + vecs[b_q, :, cols]) * scale).astype(BF16)
            q_t[cols, here] = q.T
            k = dot_nn(xs, wk[:, cols]).astype(BF16)
            k_n[here, cols] = k
            k_t[cols, here] = k.T
            v = (dot_nn(xs, wv[:, cols]) + vecs[b_v, :, cols]).astype(BF16)
            v_n[here, cols] = v
            v_t[cols, here] = v.T

        loop(width // 256, step)

    length = lengths[me]
    row = lax.broadcasted_iota(jnp.int32, (rows, LANES), 0)
    lane = lax.broadcasted_iota(jnp.int32, (rows, LANES), 1)
    for j in range(2):
        key_bias[j] = jnp.where((row >= length) & (lane == HEAD * (1 - j)), NEG, 0.0).astype(BF16)

    for i in range(len(small)):
        fetch["v", i].wait()
    fetch["x"].wait()
    fetch["wq"].wait()
    fetch["wk"].wait()
    fetch["wv"].wait()
    arrived(0, block_of(x_buf), flip(me, 1))
    qkv((me - core) * part)
    for hi in range(2, group, 2):
        for c in range(2):
            arrived(0, block_of(x_buf), flip(me, hi) - core + c)
        qkv((flip(me, hi) - core) * part)

    score_refs, top_refs = (s_a, s_b), (top_a, top_b)

    def score(p, j):
        lanes = ds(p * LANES, LANES)
        half = lax.broadcasted_iota(jnp.int32, (rows, LANES), 1) < HEAD
        k_one = jnp.where(half if j == 0 else ~half, k_n[:, lanes], key_bias[j])
        q_one = q_t[ds(p * LANES + HEAD * j, HEAD), :]
        pad = [jnp.ones((16, rows), BF16), jnp.zeros((HEAD - 16, rows), BF16)]
        q_one = jnp.concatenate([q_one] + pad if j == 0 else pad + [q_one], 0)
        for c in range(0, rows, 256):
            cols = slice(c, c + 256)
            block = dot_nn(k_one, q_one[:, cols])
            score_refs[j][:, cols] = block
            top_refs[j][:, cols] = jnp.max(block, 0, keepdims=True)

    def exponential(h, j):
        for c in range(0, rows, 256):
            cols = slice(c, c + 256)
            probs[h, :, cols] = jnp.exp(score_refs[j][:, cols] - top_refs[j][:, cols]).astype(BF16)

    def weigh(h):
        feats = ds(h * HEAD, HEAD)
        o = dot_nn(jnp.concatenate([v_t[feats, :], jnp.ones((16, rows), BF16)], 0), probs[h])
        inv = 1.0 / o[HEAD : HEAD + 1]
        recip[pl.ds(h, 1), :] = inv
        ctx_t[feats, :] = (o[:HEAD] * inv).astype(BF16)

    def turn(p):
        lanes = ds(p * LANES, LANES)
        ctx_n[:, lanes] = ctx_t[lanes, :].T

    score(0, 0)
    exponential(0, 0)
    score(0, 1)

    def attn_step(p):
        exponential(2 * p + 1, 1)
        score(p + 1, 0)
        weigh(2 * p)
        exponential(2 * p + 2, 0)
        score(p + 1, 1)
        weigh(2 * p + 1)
        turn(p)

    loop(HEADS // 2 - 1, attn_step)
    exponential(HEADS - 1, 1)
    weigh(HEADS - 2)
    weigh(HEADS - 1)
    turn(HEADS // 2 - 1)

    fetch["wo"].wait()

    def out_proj_step(i):
        part_rows = ds(i * 256, 256)
        ao = dot_nn(ctx_n[part_rows, :], wo[...]) + vecs[b_o]
        h = x_buf[part_rows, :].astype(F32) + ao
        center = h - jnp.mean(h, -1, keepdims=True)
        r = lax.rsqrt(jnp.mean(center * center, -1, keepdims=True) + EPSILON)
        xh = center * r
        xh1[part_rows, :] = xh
        rstd1[part_rows, :] = jnp.broadcast_to(r, (256, LANES))
        low[part_rows, :] = (xh * vecs[gain1] + vecs[shift1]).astype(BF16)

    loop(rows // 256, out_proj_step)

    fetch["we"].wait()
    fetch["be"].wait()

    def expand(i):
        cols = ds(i * 512, 512)
        s_a[...] = dot_nn(low[...], we[:, cols]) + vec_expand[:, cols]

    def gelu(i):
        cols = ds(i * 512, 512)
        f = s_a[...]
        phi = 0.5 * (1.0 + lax.erf(f * (0.5**0.5)))
        big_a[:, cols] = (f * phi).astype(BF16)
        dens = jnp.exp(f * f * -0.5) * (0.5 / jnp.pi) ** 0.5
        big_b[:, cols] = (phi + f * dens).astype(BF16)

    expand(0)

    def expand_step(i):
        gelu(i)
        expand(i + 1)

    loop(ff // 512 - 1, expand_step)
    gelu(ff // 512 - 1)
    fetch["wc"].wait()

    def contract_step(i):
        cols = ds(i * 256, 256)
        n1 = xh1[:, cols] * vecs[gain1, :, cols] + vecs[shift1, :, cols]
        resid[:, cols] = n1 + dot_nn(big_a[...], wc[:, cols]) + vecs[b_c, :, cols]

    loop(width // 256, contract_step)

    fetch["cot"].wait()
    for peer in members:
        arrived(1, block_of(cot_buf), peer)

    def norm2_step(i):
        part_rows = ds(i * 128, 128)
        h = resid[part_rows, :]
        center = h - jnp.mean(h, -1, keepdims=True)
        r = lax.rsqrt(jnp.mean(center * center, -1, keepdims=True) + EPSILON)
        xh = center * r
        ctx_n[part_rows, :] = (xh * vecs[gain2] + vecs[shift2]).astype(BF16)
        dy = cot_buf[part_rows, :].astype(F32)
        sums[s_ffn] += fold8(dy)
        e = dy * vecs[gain2]
        d = r * (e - jnp.mean(e, -1, keepdims=True) - xh * jnp.mean(e * xh, -1, keepdims=True))
        resid[part_rows, :] = d
        d_low = d.astype(BF16)
        low[part_rows, :] = d_low
        sums[s_contract] += fold8(d_low.astype(F32))

    loop(rows // 128, norm2_step)

    send_out = exchange(2, block_of(ctx_n), out.at[me])
    for peer in by_core:
        send_out(peer).start()
    fetch_start("out", block_of(ctx_n)(me), out.at[me])

    def contract_back_step(i):
        cols = ds(i * 512, 512)
        df = (dot_nt(low[...], wc[cols, :]) * big_b[:, cols].astype(F32)).astype(BF16)
        big_b[:, cols] = df
        sum_expand[:, cols] += fold8(df.astype(F32))

    loop(ff // 512, contract_back_step)

    def expand_back_step(i):
        cols = ds(i * 256, 256)
        resid[:, cols] += dot_nt(big_b[...], we[cols, :])

    loop(width // 256, expand_back_step)

    def norm1_step(i):
        part_rows = ds(i * 128, 128)
        dn = resid[part_rows, :]
        sums[s_attn] += fold8(dn)
        e = dn * vecs[gain1]
        xh = xh1[part_rows, :]
        r = rstd1[part_rows, :1]
        d = r * (e - jnp.mean(e, -1, keepdims=True) - xh * jnp.mean(e * xh, -1, keepdims=True))
        resid[part_rows, :] = d
        d_low = d.astype(BF16)
        low[part_rows, :] = d_low
        sums[s_output] += fold8(d_low.astype(F32))

    loop(rows // 128, norm1_step)

    expand_rows = ff // width
    early = [s_ffn, s_contract, s_attn, s_output]

    partials, received = (red, red_late), (red_in, red_late_in)

    def send_partial(kind, slot, src, where):
        return pltpu.make_async_remote_copy(
            src_ref=partials[kind].at[src],
            dst_ref=received[kind].at[slot],
            send_sem=red_send.at[kind, slot],
            recv_sem=red_recv.at[kind, slot],
            device_id=where,
            device_id_type=MESH,
        )

    def round_copies(kind, which):
        if which == 0:
            return [send_partial(kind, j - 1, 0, {"seq": flip(me, j)}) for j in peers]
        first = len(peers) + sum(len(masks) for masks in rounds[: which - 1])
        return [
            send_partial(kind, first + i, which, {"dp": flip(dp, m)})
            for i, m in enumerate(rounds[which - 1])
        ]

    def reduce_start(kind, which=0):
        for copy in round_copies(kind, which):
            copy.start()

    def reduce_end(kind, which):
        for copy in round_copies(kind, which):
            copy.wait()
        first = len(peers) + sum(len(masks) for masks in rounds[: which - 1]) if which else 0
        count = len(peers) if which == 0 else len(rounds[which - 1])
        parts = [partials[kind][which]] + [received[kind][first + i] for i in range(count)]
        while len(parts) > 1:
            parts = [parts[i] + parts[i + 1] for i in range(0, len(parts), 2)]
        partials[kind][which + 1] = parts[0]
        if which < len(rounds):
            reduce_start(kind, which + 1)

    for i, which in enumerate(early):
        red[0, i : i + 1, :] = jnp.sum(sums[which], 0, keepdims=True)
    for i in range(expand_rows):
        red[0, 4 + i : 5 + i, :] = jnp.sum(
            sum_expand[:, i * width : (i + 1) * width], 0, keepdims=True
        )
    reduce_start(0)

    def ctx_back_step(i):
        feats = ds(i * 256, 256)
        v_t[feats, :] = dot_nt(wo[feats, :], low[...]).astype(BF16)

    loop(width // 256, ctx_back_step)
    dq_n, dk_n, dv_n = (big_a.at[:, i * width : (i + 1) * width] for i in range(3))
    dscore_refs = (ds_a, ds_b)

    def dscore(p, j):
        lanes = ds(p * LANES, LANES)
        feats = ds(p * LANES + HEAD * j, HEAD)
        d = v_t[feats, :].astype(F32) * recip[pl.ds(2 * p + j, 1), :]
        inner = jnp.sum(d * ctx_t[feats, :].astype(F32), 0, keepdims=True)
        d_low = d.astype(BF16)
        zeros = jnp.zeros((HEAD, rows), BF16)
        padded = jnp.concatenate([d_low, zeros] if j == 0 else [zeros, d_low], 0)
        dprobs = dot_nn(v_n[:, lanes], padded)
        dscore_refs[j][...] = (probs[2 * p + j].astype(F32) * (dprobs - inner)).astype(BF16)
        return padded

    def attn_back_step(p):
        lanes = ds(p * LANES, LANES)
        padded = [dscore(p, j) for j in range(2)]
        dv = dot_nn(probs[2 * p], padded[0].T) + dot_nn(probs[2 * p + 1], padded[1].T)
        dqs, dks = [], []
        for j in range(2):
            feats = ds(p * LANES + HEAD * j, HEAD)
            dqs.append((dot_nn(k_t[feats, :], dscore_refs[j][...]) * scale).astype(BF16))
            dks.append(dot_nt(q_t[feats, :], dscore_refs[j][...]).astype(BF16))
        dq_low, dv_low = jnp.concatenate(dqs, 0).T, dv.astype(BF16)
        dq_n[:, lanes] = dq_low
        dk_n[:, lanes] = jnp.concatenate(dks, 0).T
        dv_n[:, lanes] = dv_low
        sums[s_query, :, lanes] = fold8(dq_low.astype(F32))
        sums[s_value, :, lanes] = fold8(dv_low.astype(F32))

    pairs, late = HEADS // 2, HEADS // 2 - 2
    loop(late, attn_back_step)
    reduce_end(0, 0)
    loop(pairs - late, lambda i: attn_back_step(late + i))
    quarter = width // 4
    for i, which in enumerate((s_query, s_value)):
        for j in range(4):
            red_late[0, 4 * i + j : 4 * i + j + 1, :] = jnp.sum(
                sums[which, :, j * quarter : (j + 1) * quarter], 0, keepdims=True
            )
    reduce_start(1)

    chunk = 256

    def grad_step(base, i):
        here, cols = ds(base, pair), slice(i * chunk, (i + 1) * chunk)
        g = (
            resid[here, cols]
            + dot_nt(dq_n[here, :], wq[cols, :])
            + dot_nt(dk_n[here, :], wk[cols, :])
            + dot_nt(dv_n[here, :], wv[cols, :])
        )
        x_buf[here, cols] = g.astype(BF16)

    def grad_cols(buf, i):
        return lambda peer: buf.at[ds(peer * part, part), i * chunk : (i + 1) * chunk]

    def grad_home(i):
        return lambda member: grad_in.at[member, :, i * chunk : (i + 1) * chunk]

    chunks = width // chunk
    send_grad = [
        exchange(3 + i, grad_cols(x_buf, i), grad_home(i)(me)) for i in range(chunks)
    ]
    for hi in range(2, group, 2):
        base = flip(me, hi) - core
        for i in range(chunks):
            grad_step(base * part, i)
            for c in range(2):
                send_grad[i](base + c).start()
    reduce_end(1, 0)
    for i in range(chunks):
        grad_step((me - core) * part, i)
        send_grad[i](flip(me, 1)).start()
    fetch_start("grad", x_buf.at[mine], grad_in.at[me])

    for which in range(1, len(rounds) + 1):
        for kind in range(2):
            reduce_end(kind, which)
    final = 1 + len(rounds)
    small_out[...] = red[final] * factor
    late_out[...] = red_late[final] * factor

    for peer in members:
        arrived(2, lambda member: out.at[member], peer)
        for i in range(chunks):
            arrived(3 + i, grad_home(i), peer)
    for send in [send_x, send_cot, send_out] + send_grad:
        for peer in members:
            send(peer).wait_send()
    fetch["out"].wait()
    fetch["grad"].wait()


def finish(
    early_out,
    early_grad,
    early_small,
    late_small,
    out,
    grad_in,
    g_bias_query,
    g_bias_value,
    g_bias_output,
    g_shift_attn,
    g_bias_expand,
    g_bias_contract,
    g_shift_ffn,
    sem_out,
):
    pairs = [
        (src.at[i], dst.at[i], n * early_out.shape[0] + i)
        for n, (src, dst) in enumerate(((early_out, out), (early_grad, grad_in)))
        for i in range(early_out.shape[0])
    ]
    puts = [pltpu.make_async_copy(src, dst, sem_out.at[n]) for src, dst, n in pairs]
    for put in puts:
        put.start()
    width = early_small.shape[-1]
    for i, ref in enumerate((g_shift_ffn, g_bias_contract, g_shift_attn, g_bias_output)):
        ref[...] = early_small[i : i + 1, :]
    for i in range(g_bias_expand.shape[1] // width):
        g_bias_expand[:, i * width : (i + 1) * width] = early_small[4 + i : 5 + i, :]
    for i, ref in enumerate((g_bias_query, g_bias_value)):
        for j in range(4):
            ref[:, j * width // 4 : (j + 1) * width // 4] = late_small[4 * i + j : 4 * i + j + 1, :]
    for put in puts:
        put.wait()


def local(mesh, *args):
    hidden_in, lengths = args[:2]
    group, dp_size = mesh.shape["seq"], mesh.shape["dp"]
    seqs, part, width = hidden_in.shape
    ff = args[7].shape[1]
    rows = part * group
    assert seqs == group
    assert group & (group - 1) == 0 and dp_size & (dp_size - 1) == 0
    factor = (rows * seqs // group * dp_size * group) ** (-0.5)
    rounds = dp_rounds(dp_size)
    slots = group - 1 + sum(len(masks) for masks in rounds)
    anywhere = pl.BlockSpec(memory_space=pl.ANY)
    in_specs = [anywhere] * len(args)
    in_specs[1] = pl.BlockSpec(memory_space=pltpu.SMEM)
    vmem = pl.BlockSpec(memory_space=pltpu.VMEM)
    operands = [a.reshape(1, -1) if a.ndim == 1 and i != 1 else a for i, a in enumerate(args)]
    row = jax.ShapeDtypeStruct((1, width), F32)
    outs = pl.pallas_call(
        functools.partial(kernel, group, dp_size, factor),
        out_shape=[pltpu.VMEM(hidden_in.shape, BF16)] * 2
        + [pltpu.VMEM((8, width), F32), pltpu.VMEM((8, width // 4), F32)],
        in_specs=in_specs,
        out_specs=[vmem] * 4,
        scratch_shapes=[
            pltpu.VMEM((width, width), BF16),
            pltpu.VMEM((width, width), BF16),
            pltpu.VMEM((width, width), BF16),
            pltpu.VMEM((width, width), BF16),
            pltpu.VMEM((width, ff), BF16),
            pltpu.VMEM((ff, width), BF16),
            pltpu.VMEM((8, 1, width), F32),
            pltpu.VMEM((1, ff), F32),
            pltpu.VMEM((rows, width), BF16),
            pltpu.VMEM((rows, width), BF16),
            pltpu.VMEM((width, rows), BF16),
            pltpu.VMEM((rows, width), BF16),
            pltpu.VMEM((width, rows), BF16),
            pltpu.VMEM((rows, width), BF16),
            pltpu.VMEM((width, rows), BF16),
            pltpu.VMEM((HEADS, rows, rows), BF16),
            pltpu.VMEM((HEADS, rows), F32),
            pltpu.VMEM((width, rows), BF16),
            pltpu.VMEM((rows, width), BF16),
            pltpu.VMEM((rows, width), F32),
            pltpu.VMEM((rows, LANES), F32),
            pltpu.VMEM((rows, width), BF16),
            pltpu.VMEM((rows, ff), BF16),
            pltpu.VMEM((rows, ff), BF16),
            pltpu.VMEM((rows, width), F32),
            pltpu.VMEM((rows, rows), F32),
            pltpu.VMEM((rows, rows), F32),
            pltpu.VMEM((1, rows), F32),
            pltpu.VMEM((1, rows), F32),
            pltpu.VMEM((rows, rows), BF16),
            pltpu.VMEM((rows, rows), BF16),
            pltpu.VMEM((2, rows, LANES), BF16),
            pltpu.VMEM((6, 8, width), F32),
            pltpu.VMEM((8, ff), F32),
            pltpu.VMEM((2 + len(rounds), 8, width), F32),
            pltpu.VMEM((slots, 8, width), F32),
            pltpu.VMEM((2 + len(rounds), 8, width // 4), F32),
            pltpu.VMEM((slots, 8, width // 4), F32),
            pltpu.SemaphoreType.DMA((24,)),
            pltpu.SemaphoreType.DMA((3 + width // 256, group)),
            pltpu.SemaphoreType.DMA((3 + width // 256, group)),
            pltpu.SemaphoreType.DMA((2, slots)),
            pltpu.SemaphoreType.DMA((2, slots)),
        ],
        compiler_params=pltpu.CompilerParams(
            collective_id=0, has_side_effects=True, vmem_limit_bytes=64700000
        ),
        name="layer",
    )(*operands)
    blocks = 2 * seqs
    outs = pl.pallas_call(
        finish,
        out_shape=[jax.ShapeDtypeStruct(hidden_in.shape, BF16)] * 2
        + [row] * 4
        + [jax.ShapeDtypeStruct((1, ff), F32), row, row],
        in_specs=[vmem] * 4,
        out_specs=[anywhere] * 2 + [vmem] * 7,
        scratch_shapes=[pltpu.SemaphoreType.DMA((blocks,))],
        name="finish",
    )(*outs)
    return tuple(o.reshape(-1) if o.shape[0] == 1 else o for o in outs)


def solution(mesh):
    placed = (P("dp", "seq", None), P("dp")) + (P(),) * 15 + (P("dp", "seq", None),)
    return jax.shard_map(
        functools.partial(local, mesh),
        mesh=mesh,
        in_specs=placed,
        out_specs=(P("dp", "seq", None), P("dp", "seq", None), P(), P(), P(), P(), P(), P(), P()),
        check_vma=False,
    )
```

```python
import functools

import jax
import jax.numpy as jnp
from jax import lax
from jax.experimental import pallas as pl
from jax.experimental.pallas import tpu as pltpu
from jax.sharding import PartitionSpec as P

HEADS = 16
HEAD = 64
NEG = -1e30
EPSILON = 1e-12
LANES = 128
MESH = pl.DeviceIdType.MESH
F32 = jnp.float32
BF16 = jnp.bfloat16


def dot_nn(left, right):
    return jnp.dot(left, right, preferred_element_type=F32)


def dot_nt(left, right):
    return lax.dot_general(left, right, (((1,), (1,)), ((), ())), preferred_element_type=F32)


def flip(index, mask):
    bit = 1
    while bit <= mask:
        if mask & bit:
            index = index + bit - 2 * bit * ((index // bit) % 2)
        bit *= 2
    return index


def ds(start, size):
    return pl.ds(start if isinstance(start, int) else pl.multiple_of(start, size), size)


def dp_rounds(size):
    rounds, low = [], 1
    while low < size:
        high = min(low * 8, size)
        rounds.append([m * low for m in range(1, high // low)])
        low = high
    return rounds


def fold8(value):
    rows, width = value.shape
    return jnp.sum(value.reshape(rows // 8, 8, width), 0)


def loop(count, body):
    def step(index, carry):
        body(index)
        return carry

    lax.fori_loop(0, count, step, 0)


def kernel(
    group,
    dp_size,
    factor,
    hidden_in,
    lengths,
    w_query,
    w_key,
    w_value,
    w_output,
    gain_attn,
    w_expand,
    w_contract,
    gain_ffn,
    bias_query,
    bias_value,
    bias_output,
    shift_attn,
    bias_expand,
    bias_contract,
    shift_ffn,
    cotangent,
    out,
    grad_in,
    small_out,
    late_out,
    wq,
    wk,
    wv,
    wo,
    we,
    wc,
    vecs,
    vec_expand,
    x_buf,
    cot_buf,
    q_t,
    k_n,
    k_t,
    v_n,
    v_t,
    probs,
    recip,
    ctx_t,
    ctx_n,
    xh1,
    rstd1,
    low,
    big_a,
    big_b,
    resid,
    s_a,
    s_b,
    top_a,
    top_b,
    ds_a,
    ds_b,
    key_bias,
    sums,
    sum_expand,
    red,
    red_in,
    red_late,
    red_late_in,
    local_sem,
    send_sem,
    recv_sem,
    red_send,
    red_recv,
):
    me = lax.axis_index("seq")
    dp = lax.axis_index("dp")
    part = hidden_in.shape[1]
    rows, width = x_buf.shape
    ff = we.shape[1]
    peers = list(range(1, group))
    members = [flip(me, j) for j in peers]
    core = me % 2
    by_core = [flip(me, 1)] + [
        flip(me, hi) - core + c for c in range(2) for hi in range(2, group, 2)
    ]
    rounds = dp_rounds(dp_size)
    dp_masks = [m for masks in rounds for m in masks]

    small = (
        bias_query,
        bias_value,
        bias_output,
        gain_attn,
        shift_attn,
        bias_contract,
        gain_ffn,
        shift_ffn,
    )
    b_q, b_v, b_o, gain1, shift1, b_c, gain2, shift2 = range(8)
    fetch = {}

    def fetch_start(name, src, dst):
        fetch[name] = pltpu.make_async_copy(src, dst, local_sem.at[len(fetch)])
        fetch[name].start()

    mine = ds(me * part, part)
    fetch_start("x", hidden_in.at[me], x_buf.at[mine])
    fetch_start("wq", w_query, wq)
    fetch_start("wk", w_key, wk)
    fetch_start("wv", w_value, wv)

    barrier = pltpu.get_barrier_semaphore()
    for j in peers:
        pl.semaphore_signal(barrier, inc=1, device_id={"seq": flip(me, j)}, device_id_type=MESH)
    for m in dp_masks:
        pl.semaphore_signal(barrier, inc=1, device_id={"dp": flip(dp, m)}, device_id_type=MESH)
    pl.semaphore_wait(barrier, len(peers) + len(dp_masks))

    def exchange(kind, src_of, dst):
        def send(peer):
            return pltpu.make_async_remote_copy(
                src_ref=src_of(peer),
                dst_ref=dst,
                send_sem=send_sem.at[kind, peer],
                recv_sem=recv_sem.at[kind, me],
                device_id={"seq": peer},
                device_id_type=MESH,
            )

        return send

    def block_of(buf):
        return lambda peer: buf.at[ds(peer * part, part)]

    def arrived(kind, dst_of, peer):
        pltpu.make_async_remote_copy(
            src_ref=dst_of(peer),
            dst_ref=dst_of(peer),
            send_sem=send_sem.at[kind, peer],
            recv_sem=recv_sem.at[kind, peer],
            device_id={"seq": peer},
            device_id_type=MESH,
        ).wait_recv()

    send_x = exchange(0, lambda peer: hidden_in.at[peer], x_buf.at[mine])
    for peer in by_core:
        send_x(peer).start()
    for i, vec in enumerate(small):
        fetch_start(("v", i), vec, vecs.at[i])
    fetch_start("be", bias_expand, vec_expand)
    fetch_start("wo", w_output, wo)
    fetch_start("we", w_expand, we)
    send_cot = exchange(1, lambda peer: cotangent.at[peer], cot_buf.at[mine])
    for peer in by_core:
        send_cot(peer).start()
    fetch_start("cot", cotangent.at[me], cot_buf.at[mine])
    fetch_start("wc", w_contract, wc)

    sums[...] = jnp.zeros_like(sums)
    sum_expand[...] = jnp.zeros_like(sum_expand)
    s_ffn, s_contract, s_attn, s_output, s_query, s_value = range(6)

    scale = HEAD ** (-0.5)
    pair = 2 * part

    def qkv(base):
        here = ds(base, pair)
        xs = x_buf[here, :]

        def step(i):
            cols = ds(i * 256, 256)
            q = ((dot_nn(xs, wq[:, cols]) + vecs[b_q, :, cols]) * scale).astype(BF16)
            q_t[cols, here] = q.T
            k = dot_nn(xs, wk[:, cols]).astype(BF16)
            k_n[here, cols] = k
            k_t[cols, here] = k.T
            v = (dot_nn(xs, wv[:, cols]) + vecs[b_v, :, cols]).astype(BF16)
            v_n[here, cols] = v
            v_t[cols, here] = v.T

        loop(width // 256, step)

    length = lengths[me]
    row = lax.broadcasted_iota(jnp.int32, (rows, LANES), 0)
    lane = lax.broadcasted_iota(jnp.int32, (rows, LANES), 1)
    for j in range(2):
        key_bias[j] = jnp.where((row >= length) & (lane == HEAD * (1 - j)), NEG, 0.0).astype(BF16)

    for i in range(len(small)):
        fetch["v", i].wait()
    fetch["x"].wait()
    fetch["wq"].wait()
    fetch["wk"].wait()
    fetch["wv"].wait()
    arrived(0, block_of(x_buf), flip(me, 1))
    qkv((me - core) * part)
    for hi in range(2, group, 2):
        for c in range(2):
            arrived(0, block_of(x_buf), flip(me, hi) - core + c)
        qkv((flip(me, hi) - core) * part)

    score_refs, top_refs = (s_a, s_b), (top_a, top_b)

    def score(p, j):
        lanes = ds(p * LANES, LANES)
        half = lax.broadcasted_iota(jnp.int32, (rows, LANES), 1) < HEAD
        k_one = jnp.where(half if j == 0 else ~half, k_n[:, lanes], key_bias[j])
        q_one = q_t[ds(p * LANES + HEAD * j, HEAD), :]
        pad = [jnp.ones((16, rows), BF16), jnp.zeros((HEAD - 16, rows), BF16)]
        q_one = jnp.concatenate([q_one] + pad if j == 0 else pad + [q_one], 0)
        for c in range(0, rows, 256):
            cols = slice(c, c + 256)
            block = dot_nn(k_one, q_one[:, cols])
            score_refs[j][:, cols] = block
            top_refs[j][:, cols] = jnp.max(block, 0, keepdims=True)

    def exponential(h, j):
        for c in range(0, rows, 256):
            cols = slice(c, c + 256)
            probs[h, :, cols] = jnp.exp(score_refs[j][:, cols] - top_refs[j][:, cols]).astype(BF16)

    def weigh(h):
        feats = ds(h * HEAD, HEAD)
        o = dot_nn(jnp.concatenate([v_t[feats, :], jnp.ones((16, rows), BF16)], 0), probs[h])
        inv = 1.0 / o[HEAD : HEAD + 1]
        recip[pl.ds(h, 1), :] = inv
        ctx_t[feats, :] = (o[:HEAD] * inv).astype(BF16)

    def turn(p):
        lanes = ds(p * LANES, LANES)
        ctx_n[:, lanes] = ctx_t[lanes, :].T

    score(0, 0)
    exponential(0, 0)
    score(0, 1)

    def attn_step(p):
        exponential(2 * p + 1, 1)
        score(p + 1, 0)
        weigh(2 * p)
        exponential(2 * p + 2, 0)
        score(p + 1, 1)
        weigh(2 * p + 1)
        turn(p)

    loop(HEADS // 2 - 1, attn_step)
    exponential(HEADS - 1, 1)
    weigh(HEADS - 2)
    weigh(HEADS - 1)
    turn(HEADS // 2 - 1)

    fetch["wo"].wait()

    def out_proj_step(i):
        part_rows = ds(i * 256, 256)
        ao = dot_nn(ctx_n[part_rows, :], wo[...]) + vecs[b_o]
        h = x_buf[part_rows, :].astype(F32) + ao
        center = h - jnp.mean(h, -1, keepdims=True)
        r = lax.rsqrt(jnp.mean(center * center, -1, keepdims=True) + EPSILON)
        xh = center * r
        xh1[part_rows, :] = xh
        rstd1[part_rows, :] = jnp.broadcast_to(r, (256, LANES))
        low[part_rows, :] = (xh * vecs[gain1] + vecs[shift1]).astype(BF16)

    loop(rows // 256, out_proj_step)

    fetch["we"].wait()
    fetch["be"].wait()

    def expand(i):
        cols = ds(i * 512, 512)
        s_a[...] = dot_nn(low[...], we[:, cols]) + vec_expand[:, cols]

    def gelu(i):
        cols = ds(i * 512, 512)
        f = s_a[...]
        phi = 0.5 * (1.0 + lax.erf(f * (0.5**0.5)))
        big_a[:, cols] = (f * phi).astype(BF16)
        dens = jnp.exp(f * f * -0.5) * (0.5 / jnp.pi) ** 0.5
        big_b[:, cols] = (phi + f * dens).astype(BF16)

    expand(0)

    def expand_step(i):
        gelu(i)
        expand(i + 1)

    loop(ff // 512 - 1, expand_step)
    gelu(ff // 512 - 1)
    fetch["wc"].wait()

    def contract_step(i):
        cols = ds(i * 256, 256)
        n1 = xh1[:, cols] * vecs[gain1, :, cols] + vecs[shift1, :, cols]
        resid[:, cols] = n1 + dot_nn(big_a[...], wc[:, cols]) + vecs[b_c, :, cols]

    loop(width // 256, contract_step)

    fetch["cot"].wait()
    for peer in members:
        arrived(1, block_of(cot_buf), peer)

    def norm2_step(i):
        part_rows = ds(i * 128, 128)
        h = resid[part_rows, :]
        center = h - jnp.mean(h, -1, keepdims=True)
        r = lax.rsqrt(jnp.mean(center * center, -1, keepdims=True) + EPSILON)
        xh = center * r
        ctx_n[part_rows, :] = (xh * vecs[gain2] + vecs[shift2]).astype(BF16)
        dy = cot_buf[part_rows, :].astype(F32)
        sums[s_ffn] += fold8(dy)
        e = dy * vecs[gain2]
        d = r * (e - jnp.mean(e, -1, keepdims=True) - xh * jnp.mean(e * xh, -1, keepdims=True))
        resid[part_rows, :] = d
        d_low = d.astype(BF16)
        low[part_rows, :] = d_low
        sums[s_contract] += fold8(d_low.astype(F32))

    loop(rows // 128, norm2_step)

    send_out = exchange(2, block_of(ctx_n), out.at[me])
    for peer in by_core:
        send_out(peer).start()
    fetch_start("out", block_of(ctx_n)(me), out.at[me])

    def contract_back_step(i):
        cols = ds(i * 512, 512)
        df = (dot_nt(low[...], wc[cols, :]) * big_b[:, cols].astype(F32)).astype(BF16)
        big_b[:, cols] = df
        sum_expand[:, cols] += fold8(df.astype(F32))

    loop(ff // 512, contract_back_step)

    def expand_back_step(i):
        cols = ds(i * 256, 256)
        resid[:, cols] += dot_nt(big_b[...], we[cols, :])

    loop(width // 256, expand_back_step)

    def norm1_step(i):
        part_rows = ds(i * 128, 128)
        dn = resid[part_rows, :]
        sums[s_attn] += fold8(dn)
        e = dn * vecs[gain1]
        xh = xh1[part_rows, :]
        r = rstd1[part_rows, :1]
        d = r * (e - jnp.mean(e, -1, keepdims=True) - xh * jnp.mean(e * xh, -1, keepdims=True))
        resid[part_rows, :] = d
        d_low = d.astype(BF16)
        low[part_rows, :] = d_low
        sums[s_output] += fold8(d_low.astype(F32))

    loop(rows // 128, norm1_step)

    expand_rows = ff // width
    early = [s_ffn, s_contract, s_attn, s_output]

    partials, received = (red, red_late), (red_in, red_late_in)

    def send_partial(kind, slot, src, where):
        return pltpu.make_async_remote_copy(
            src_ref=partials[kind].at[src],
            dst_ref=received[kind].at[slot],
            send_sem=red_send.at[kind, slot],
            recv_sem=red_recv.at[kind, slot],
            device_id=where,
            device_id_type=MESH,
        )

    def round_copies(kind, which):
        if which == 0:
            return [send_partial(kind, j - 1, 0, {"seq": flip(me, j)}) for j in peers]
        first = len(peers) + sum(len(masks) for masks in rounds[: which - 1])
        return [
            send_partial(kind, first + i, which, {"dp": flip(dp, m)})
            for i, m in enumerate(rounds[which - 1])
        ]

    def reduce_start(kind, which=0):
        for copy in round_copies(kind, which):
            copy.start()

    def reduce_end(kind, which):
        for copy in round_copies(kind, which):
            copy.wait()
        first = len(peers) + sum(len(masks) for masks in rounds[: which - 1]) if which else 0
        count = len(peers) if which == 0 else len(rounds[which - 1])
        parts = [partials[kind][which]] + [received[kind][first + i] for i in range(count)]
        while len(parts) > 1:
            parts = [parts[i] + parts[i + 1] for i in range(0, len(parts), 2)]
        partials[kind][which + 1] = parts[0]
        if which < len(rounds):
            reduce_start(kind, which + 1)

    for i, which in enumerate(early):
        red[0, i : i + 1, :] = jnp.sum(sums[which], 0, keepdims=True)
    for i in range(expand_rows):
        red[0, 4 + i : 5 + i, :] = jnp.sum(
            sum_expand[:, i * width : (i + 1) * width], 0, keepdims=True
        )
    reduce_start(0)

    def ctx_back_step(i):
        feats = ds(i * 256, 256)
        v_t[feats, :] = dot_nt(wo[feats, :], low[...]).astype(BF16)

    loop(width // 256, ctx_back_step)
    dq_n, dk_n, dv_n = (big_a.at[:, i * width : (i + 1) * width] for i in range(3))
    dscore_refs = (ds_a, ds_b)

    def dscore(p, j):
        lanes = ds(p * LANES, LANES)
        feats = ds(p * LANES + HEAD * j, HEAD)
        d = v_t[feats, :].astype(F32) * recip[pl.ds(2 * p + j, 1), :]
        inner = jnp.sum(d * ctx_t[feats, :].astype(F32), 0, keepdims=True)
        d_low = d.astype(BF16)
        zeros = jnp.zeros((HEAD, rows), BF16)
        padded = jnp.concatenate([d_low, zeros] if j == 0 else [zeros, d_low], 0)
        dprobs = dot_nn(v_n[:, lanes], padded)
        dscore_refs[j][...] = (probs[2 * p + j].astype(F32) * (dprobs - inner)).astype(BF16)
        return padded

    def attn_back_step(p):
        lanes = ds(p * LANES, LANES)
        padded = [dscore(p, j) for j in range(2)]
        dv = dot_nn(probs[2 * p], padded[0].T) + dot_nn(probs[2 * p + 1], padded[1].T)
        dqs, dks = [], []
        for j in range(2):
            feats = ds(p * LANES + HEAD * j, HEAD)
            dqs.append((dot_nn(k_t[feats, :], dscore_refs[j][...]) * scale).astype(BF16))
            dks.append(dot_nt(q_t[feats, :], dscore_refs[j][...]).astype(BF16))
        dq_low, dv_low = jnp.concatenate(dqs, 0).T, dv.astype(BF16)
        dq_n[:, lanes] = dq_low
        dk_n[:, lanes] = jnp.concatenate(dks, 0).T
        dv_n[:, lanes] = dv_low
        sums[s_query, :, lanes] = fold8(dq_low.astype(F32))
        sums[s_value, :, lanes] = fold8(dv_low.astype(F32))

    pairs, late = HEADS // 2, HEADS // 2 - 2
    loop(late, attn_back_step)
    reduce_end(0, 0)
    loop(pairs - late, lambda i: attn_back_step(late + i))
    quarter = width // 4
    for i, which in enumerate((s_query, s_value)):
        for j in range(4):
            red_late[0, 4 * i + j : 4 * i + j + 1, :] = jnp.sum(
                sums[which, :, j * quarter : (j + 1) * quarter], 0, keepdims=True
            )
    reduce_start(1)

    chunk = 256

    def grad_step(base, i):
        here, cols = ds(base, pair), slice(i * chunk, (i + 1) * chunk)
        g = (
            resid[here, cols]
            + dot_nt(dq_n[here, :], wq[cols, :])
            + dot_nt(dk_n[here, :], wk[cols, :])
            + dot_nt(dv_n[here, :], wv[cols, :])
        )
        x_buf[here, cols] = g.astype(BF16)

    def grad_cols(buf, i):
        return lambda peer: buf.at[ds(peer * part, part), i * chunk : (i + 1) * chunk]

    def grad_home(i):
        return lambda member: grad_in.at[member, :, i * chunk : (i + 1) * chunk]

    chunks = width // chunk
    send_grad = [
        exchange(3 + i, grad_cols(x_buf, i), grad_home(i)(me)) for i in range(chunks)
    ]
    for hi in range(2, group, 2):
        base = flip(me, hi) - core
        for i in range(chunks):
            grad_step(base * part, i)
            for c in range(2):
                send_grad[i](base + c).start()
    reduce_end(1, 0)
    for i in range(chunks):
        grad_step((me - core) * part, i)
        send_grad[i](flip(me, 1)).start()
    fetch_start("grad", x_buf.at[mine], grad_in.at[me])

    for which in range(1, len(rounds) + 1):
        for kind in range(2):
            reduce_end(kind, which)
    final = 1 + len(rounds)
    small_out[...] = red[final] * factor
    late_out[...] = red_late[final] * factor

    for peer in members:
        arrived(2, lambda member: out.at[member], peer)
        for i in range(chunks):
            arrived(3 + i, grad_home(i), peer)
    for send in [send_x, send_cot, send_out] + send_grad:
        for peer in members:
            send(peer).wait_send()
    fetch["out"].wait()
    fetch["grad"].wait()


def finish(
    early_out,
    early_grad,
    early_small,
    late_small,
    out,
    grad_in,
    g_bias_query,
    g_bias_value,
    g_bias_output,
    g_shift_attn,
    g_bias_expand,
    g_bias_contract,
    g_shift_ffn,
    sem_out,
):
    pairs = [
        (src.at[i], dst.at[i], n * early_out.shape[0] + i)
        for n, (src, dst) in enumerate(((early_out, out), (early_grad, grad_in)))
        for i in range(early_out.shape[0])
    ]
    puts = [pltpu.make_async_copy(src, dst, sem_out.at[n]) for src, dst, n in pairs]
    for put in puts:
        put.start()
    width = early_small.shape[-1]
    for i, ref in enumerate((g_shift_ffn, g_bias_contract, g_shift_attn, g_bias_output)):
        ref[...] = early_small[i : i + 1, :]
    for i in range(g_bias_expand.shape[1] // width):
        g_bias_expand[:, i * width : (i + 1) * width] = early_small[4 + i : 5 + i, :]
    for i, ref in enumerate((g_bias_query, g_bias_value)):
        for j in range(4):
            ref[:, j * width // 4 : (j + 1) * width // 4] = late_small[4 * i + j : 4 * i + j + 1, :]
    for put in puts:
        put.wait()


def local(mesh, *args):
    hidden_in, lengths = args[:2]
    group, dp_size = mesh.shape["seq"], mesh.shape["dp"]
    seqs, part, width = hidden_in.shape
    ff = args[7].shape[1]
    rows = part * group
    assert seqs == group
    assert group & (group - 1) == 0 and dp_size & (dp_size - 1) == 0
    factor = (rows * seqs // group * dp_size * group) ** (-0.5)
    rounds = dp_rounds(dp_size)
    slots = group - 1 + sum(len(masks) for masks in rounds)
    anywhere = pl.BlockSpec(memory_space=pl.ANY)
    in_specs = [anywhere] * len(args)
    in_specs[1] = pl.BlockSpec(memory_space=pltpu.SMEM)
    vmem = pl.BlockSpec(memory_space=pltpu.VMEM)
    operands = [a.reshape(1, -1) if a.ndim == 1 and i != 1 else a for i, a in enumerate(args)]
    row = jax.ShapeDtypeStruct((1, width), F32)
    outs = pl.pallas_call(
        functools.partial(kernel, group, dp_size, factor),
        out_shape=[pltpu.VMEM(hidden_in.shape, BF16)] * 2
        + [pltpu.VMEM((8, width), F32), pltpu.VMEM((8, width // 4), F32)],
        in_specs=in_specs,
        out_specs=[vmem] * 4,
        scratch_shapes=[
            pltpu.VMEM((width, width), BF16),
            pltpu.VMEM((width, width), BF16),
            pltpu.VMEM((width, width), BF16),
            pltpu.VMEM((width, width), BF16),
            pltpu.VMEM((width, ff), BF16),
            pltpu.VMEM((ff, width), BF16),
            pltpu.VMEM((8, 1, width), F32),
            pltpu.VMEM((1, ff), F32),
            pltpu.VMEM((rows, width), BF16),
            pltpu.VMEM((rows, width), BF16),
            pltpu.VMEM((width, rows), BF16),
            pltpu.VMEM((rows, width), BF16),
            pltpu.VMEM((width, rows), BF16),
            pltpu.VMEM((rows, width), BF16),
            pltpu.VMEM((width, rows), BF16),
            pltpu.VMEM((HEADS, rows, rows), BF16),
            pltpu.VMEM((HEADS, rows), F32),
            pltpu.VMEM((width, rows), BF16),
            pltpu.VMEM((rows, width), BF16),
            pltpu.VMEM((rows, width), F32),
            pltpu.VMEM((rows, LANES), F32),
            pltpu.VMEM((rows, width), BF16),
            pltpu.VMEM((rows, ff), BF16),
            pltpu.VMEM((rows, ff), BF16),
            pltpu.VMEM((rows, width), F32),
            pltpu.VMEM((rows, rows), F32),
            pltpu.VMEM((rows, rows), F32),
            pltpu.VMEM((1, rows), F32),
            pltpu.VMEM((1, rows), F32),
            pltpu.VMEM((rows, rows), BF16),
            pltpu.VMEM((rows, rows), BF16),
            pltpu.VMEM((2, rows, LANES), BF16),
            pltpu.VMEM((6, 8, width), F32),
            pltpu.VMEM((8, ff), F32),
            pltpu.VMEM((2 + len(rounds), 8, width), F32),
            pltpu.VMEM((slots, 8, width), F32),
            pltpu.VMEM((2 + len(rounds), 8, width // 4), F32),
            pltpu.VMEM((slots, 8, width // 4), F32),
            pltpu.SemaphoreType.DMA((24,)),
            pltpu.SemaphoreType.DMA((3 + width // 256, group)),
            pltpu.SemaphoreType.DMA((3 + width // 256, group)),
            pltpu.SemaphoreType.DMA((2, slots)),
            pltpu.SemaphoreType.DMA((2, slots)),
        ],
        compiler_params=pltpu.CompilerParams(
            collective_id=0, has_side_effects=True, vmem_limit_bytes=64700000
        ),
        name="layer",
    )(*operands)
    outs = [pltpu.with_memory_space_constraint(o, pltpu.VMEM) for o in outs]
    blocks = 2 * seqs
    outs = pl.pallas_call(
        finish,
        out_shape=[jax.ShapeDtypeStruct(hidden_in.shape, BF16)] * 2
        + [row] * 4
        + [jax.ShapeDtypeStruct((1, ff), F32), row, row],
        in_specs=[vmem] * 4,
        out_specs=[anywhere] * 2 + [vmem] * 7,
        scratch_shapes=[pltpu.SemaphoreType.DMA((blocks,))],
        compiler_params=pltpu.CompilerParams(vmem_limit_bytes=4 * 2**20),
        name="finish",
    )(*outs)
    return tuple(o.reshape(-1) if o.shape[0] == 1 else o for o in outs)


def solution(mesh):
    placed = (P("dp", "seq", None), P("dp")) + (P(),) * 15 + (P("dp", "seq", None),)
    return jax.shard_map(
        functools.partial(local, mesh),
        mesh=mesh,
        in_specs=placed,
        out_specs=(P("dp", "seq", None), P("dp", "seq", None), P(), P(), P(), P(), P(), P(), P()),
        check_vma=False,
    )
```

```python
import functools

import jax
import jax.numpy as jnp
from jax import lax
from jax.experimental import pallas as pl
from jax.experimental.pallas import tpu as pltpu
from jax.sharding import PartitionSpec as P

HEADS = 16
HEAD = 64
NEG = -1e30
EPSILON = 1e-12
LANES = 128
MESH = pl.DeviceIdType.MESH
F32 = jnp.float32
BF16 = jnp.bfloat16


def dot_nn(left, right):
    return jnp.dot(left, right, preferred_element_type=F32)


def dot_nt(left, right):
    return lax.dot_general(left, right, (((1,), (1,)), ((), ())), preferred_element_type=F32)


def flip(index, mask):
    bit = 1
    while bit <= mask:
        if mask & bit:
            index = index + bit - 2 * bit * ((index // bit) % 2)
        bit *= 2
    return index


def ds(start, size):
    return pl.ds(start if isinstance(start, int) else pl.multiple_of(start, size), size)


def dp_rounds(size):
    rounds, low = [], 1
    while low < size:
        high = min(low * 8, size)
        rounds.append([m * low for m in range(1, high // low)])
        low = high
    return rounds


def fold8(value):
    rows, width = value.shape
    return jnp.sum(value.reshape(rows // 8, 8, width), 0)


def loop(count, body, unroll=1):
    def step(index, carry):
        body(index)
        return carry

    lax.fori_loop(0, count, step, 0, unroll=unroll)


def kernel(
    group,
    dp_size,
    factor,
    hidden_in,
    lengths,
    w_query,
    w_key,
    w_value,
    w_output,
    gain_attn,
    w_expand,
    w_contract,
    gain_ffn,
    bias_query,
    bias_value,
    bias_output,
    shift_attn,
    bias_expand,
    bias_contract,
    shift_ffn,
    cotangent,
    out,
    grad_in,
    small_out,
    late_out,
    wq,
    wk,
    wv,
    wo,
    we,
    wc,
    vecs,
    vec_expand,
    x_buf,
    cot_buf,
    q_t,
    k_n,
    k_t,
    v_n,
    v_t,
    probs,
    recip,
    ctx_t,
    ctx_n,
    xh1,
    rstd1,
    low,
    big_a,
    big_b,
    resid,
    s_a,
    s_b,
    top_a,
    top_b,
    key_bias,
    sums,
    sum_expand,
    red,
    red_in,
    red_late,
    red_late_in,
    local_sem,
    send_sem,
    recv_sem,
    red_send,
    red_recv,
):
    me = lax.axis_index("seq")
    dp = lax.axis_index("dp")
    part = hidden_in.shape[1]
    rows, width = x_buf.shape
    ff = we.shape[1]
    peers = list(range(1, group))
    members = [flip(me, j) for j in peers]
    core = me % 2
    by_core = [flip(me, 1)] + [
        flip(me, hi) - core + c for c in range(2) for hi in range(2, group, 2)
    ]
    rounds = dp_rounds(dp_size)
    dp_masks = [m for masks in rounds for m in masks]

    small = (
        bias_query,
        bias_value,
        bias_output,
        gain_attn,
        shift_attn,
        bias_contract,
        gain_ffn,
        shift_ffn,
    )
    b_q, b_v, b_o, gain1, shift1, b_c, gain2, shift2 = range(8)
    fetch = {}

    def fetch_start(name, src, dst):
        fetch[name] = pltpu.make_async_copy(src, dst, local_sem.at[len(fetch)])
        fetch[name].start()

    mine = ds(me * part, part)
    fetch_start("x", hidden_in.at[me], x_buf.at[mine])
    fetch_start("wq", w_query, wq)
    fetch_start("wk", w_key, wk)
    fetch_start("wv", w_value, wv)

    barrier = pltpu.get_barrier_semaphore()
    for j in peers:
        pl.semaphore_signal(barrier, inc=1, device_id={"seq": flip(me, j)}, device_id_type=MESH)
    for m in dp_masks:
        pl.semaphore_signal(barrier, inc=1, device_id={"dp": flip(dp, m)}, device_id_type=MESH)
    pl.semaphore_wait(barrier, len(peers) + len(dp_masks))

    def exchange(kind, src_of, dst):
        def send(peer):
            return pltpu.make_async_remote_copy(
                src_ref=src_of(peer),
                dst_ref=dst,
                send_sem=send_sem.at[kind, peer],
                recv_sem=recv_sem.at[kind, me],
                device_id={"seq": peer},
                device_id_type=MESH,
            )

        return send

    def block_of(buf):
        return lambda peer: buf.at[ds(peer * part, part)]

    def arrived(kind, dst_of, peer):
        pltpu.make_async_remote_copy(
            src_ref=dst_of(peer),
            dst_ref=dst_of(peer),
            send_sem=send_sem.at[kind, peer],
            recv_sem=recv_sem.at[kind, peer],
            device_id={"seq": peer},
            device_id_type=MESH,
        ).wait_recv()

    send_x = exchange(0, lambda peer: hidden_in.at[peer], x_buf.at[mine])
    for peer in by_core:
        send_x(peer).start()
    for i, vec in enumerate(small):
        fetch_start(("v", i), vec, vecs.at[i])
    fetch_start("be", bias_expand, vec_expand)
    fetch_start("wo", w_output, wo)
    fetch_start("we", w_expand, we)
    send_cot = exchange(1, lambda peer: cotangent.at[peer], cot_buf.at[mine])
    for peer in by_core:
        send_cot(peer).start()
    fetch_start("cot", cotangent.at[me], cot_buf.at[mine])
    fetch_start("wc", w_contract, wc)

    sums[...] = jnp.zeros_like(sums)
    sum_expand[...] = jnp.zeros_like(sum_expand)
    s_ffn, s_contract, s_attn, s_output, s_query, s_value = range(6)

    scale = HEAD ** (-0.5)
    pair = 2 * part

    def qkv(base):
        here = ds(base, pair)
        xs = x_buf[here, :]

        def step(i):
            cols = ds(i * 256, 256)
            q = ((dot_nn(xs, wq[:, cols]) + vecs[b_q, :, cols]) * scale).astype(BF16)
            q_t[cols, here] = q.T
            k = dot_nn(xs, wk[:, cols]).astype(BF16)
            k_n[here, cols] = k
            k_t[cols, here] = k.T
            v = (dot_nn(xs, wv[:, cols]) + vecs[b_v, :, cols]).astype(BF16)
            v_n[here, cols] = v
            v_t[cols, here] = v.T

        loop(width // 256, step, width // 256)

    length = lengths[me]
    row = lax.broadcasted_iota(jnp.int32, (rows, LANES), 0)
    lane = lax.broadcasted_iota(jnp.int32, (rows, LANES), 1)
    for j in range(2):
        key_bias[j] = jnp.where((row >= length) & (lane == HEAD * (1 - j)), NEG, 0.0).astype(BF16)

    for i in range(len(small)):
        fetch["v", i].wait()
    fetch["x"].wait()
    fetch["wq"].wait()
    fetch["wk"].wait()
    fetch["wv"].wait()
    arrived(0, block_of(x_buf), flip(me, 1))
    qkv((me - core) * part)
    for hi in range(2, group, 2):
        for c in range(2):
            arrived(0, block_of(x_buf), flip(me, hi) - core + c)
        qkv((flip(me, hi) - core) * part)

    score_refs, top_refs = (s_a, s_b), (top_a, top_b)

    def score(p, j):
        lanes = ds(p * LANES, LANES)
        half = lax.broadcasted_iota(jnp.int32, (rows, LANES), 1) < HEAD
        k_one = jnp.where(half if j == 0 else ~half, k_n[:, lanes], key_bias[j])
        q_one = q_t[ds(p * LANES + HEAD * j, HEAD), :]
        pad = [jnp.ones((16, rows), BF16), jnp.zeros((HEAD - 16, rows), BF16)]
        q_one = jnp.concatenate([q_one] + pad if j == 0 else pad + [q_one], 0)
        for c in range(0, rows, 256):
            cols = slice(c, c + 256)
            block = dot_nn(k_one, q_one[:, cols])
            score_refs[j][:, cols] = block
            top_refs[j][:, cols] = jnp.max(block, 0, keepdims=True)

    def exponential(h, j):
        for c in range(0, rows, 256):
            cols = slice(c, c + 256)
            probs[h, :, cols] = jnp.exp(score_refs[j][:, cols] - top_refs[j][:, cols]).astype(BF16)

    def weigh(h):
        feats = ds(h * HEAD, HEAD)
        o = dot_nn(jnp.concatenate([v_t[feats, :], jnp.ones((16, rows), BF16)], 0), probs[h])
        inv = 1.0 / o[HEAD : HEAD + 1]
        recip[pl.ds(h, 1), :] = inv
        ctx_t[feats, :] = (o[:HEAD] * inv).astype(BF16)

    def turn(p):
        lanes = ds(p * LANES, LANES)
        ctx_n[:, lanes] = ctx_t[lanes, :].T

    score(0, 0)
    exponential(0, 0)
    score(0, 1)

    def attn_step(p):
        exponential(2 * p + 1, 1)
        score(p + 1, 0)
        weigh(2 * p)
        exponential(2 * p + 2, 0)
        score(p + 1, 1)
        weigh(2 * p + 1)
        turn(p)

    loop(HEADS // 2 - 1, attn_step, 7)
    exponential(HEADS - 1, 1)
    weigh(HEADS - 2)
    weigh(HEADS - 1)
    turn(HEADS // 2 - 1)

    fetch["wo"].wait()

    def out_proj_step(i):
        part_rows = ds(i * 256, 256)
        ao = dot_nn(ctx_n[part_rows, :], wo[...]) + vecs[b_o]
        h = x_buf[part_rows, :].astype(F32) + ao
        center = h - jnp.mean(h, -1, keepdims=True)
        r = lax.rsqrt(jnp.mean(center * center, -1, keepdims=True) + EPSILON)
        xh = center * r
        xh1[part_rows, :] = xh
        rstd1[part_rows, :] = jnp.broadcast_to(r, (256, LANES))
        low[part_rows, :] = (xh * vecs[gain1] + vecs[shift1]).astype(BF16)

    loop(rows // 256, out_proj_step, rows // 256)

    fetch["we"].wait()
    fetch["be"].wait()

    def expand(i):
        cols = ds(i * 512, 512)
        s_a[...] = dot_nn(low[...], we[:, cols]) + vec_expand[:, cols]

    def gelu(i):
        cols = ds(i * 512, 512)
        f = s_a[...]
        phi = 0.5 * (1.0 + lax.erf(f * (0.5**0.5)))
        big_a[:, cols] = (f * phi).astype(BF16)
        dens = jnp.exp(f * f * -0.5) * (0.5 / jnp.pi) ** 0.5
        big_b[:, cols] = (phi + f * dens).astype(BF16)

    expand(0)

    def expand_step(i):
        gelu(i)
        expand(i + 1)

    loop(ff // 512 - 1, expand_step, ff // 512 - 1)
    gelu(ff // 512 - 1)
    fetch["wc"].wait()

    def contract_step(i):
        cols = ds(i * 256, 256)
        n1 = xh1[:, cols] * vecs[gain1, :, cols] + vecs[shift1, :, cols]
        resid[:, cols] = n1 + dot_nn(big_a[...], wc[:, cols]) + vecs[b_c, :, cols]

    loop(width // 256, contract_step, width // 256)

    fetch["cot"].wait()
    for peer in members:
        arrived(1, block_of(cot_buf), peer)

    def norm2_step(i):
        part_rows = ds(i * 128, 128)
        h = resid[part_rows, :]
        center = h - jnp.mean(h, -1, keepdims=True)
        r = lax.rsqrt(jnp.mean(center * center, -1, keepdims=True) + EPSILON)
        xh = center * r
        ctx_n[part_rows, :] = (xh * vecs[gain2] + vecs[shift2]).astype(BF16)
        dy = cot_buf[part_rows, :].astype(F32)
        sums[s_ffn] += fold8(dy)
        e = dy * vecs[gain2]
        d = r * (e - jnp.mean(e, -1, keepdims=True) - xh * jnp.mean(e * xh, -1, keepdims=True))
        resid[part_rows, :] = d
        d_low = d.astype(BF16)
        low[part_rows, :] = d_low
        sums[s_contract] += fold8(d_low.astype(F32))

    loop(rows // 128, norm2_step)

    send_out = exchange(2, block_of(ctx_n), out.at[me])
    for peer in by_core:
        send_out(peer).start()
    fetch_start("out", block_of(ctx_n)(me), out.at[me])

    def contract_back_step(i):
        cols = ds(i * 1024, 1024)
        df = (dot_nt(low[...], wc[cols, :]) * big_b[:, cols].astype(F32)).astype(BF16)
        big_b[:, cols] = df
        sum_expand[:, cols] += fold8(df.astype(F32))

    loop(ff // 1024, contract_back_step, ff // 1024)

    def expand_back_step(i):
        cols = ds(i * 256, 256)
        resid[:, cols] += dot_nt(big_b[...], we[cols, :])

    loop(width // 256, expand_back_step, width // 256)

    def norm1_step(i):
        part_rows = ds(i * 128, 128)
        dn = resid[part_rows, :]
        sums[s_attn] += fold8(dn)
        e = dn * vecs[gain1]
        xh = xh1[part_rows, :]
        r = rstd1[part_rows, :1]
        d = r * (e - jnp.mean(e, -1, keepdims=True) - xh * jnp.mean(e * xh, -1, keepdims=True))
        resid[part_rows, :] = d
        d_low = d.astype(BF16)
        low[part_rows, :] = d_low
        sums[s_output] += fold8(d_low.astype(F32))

    loop(rows // 128, norm1_step)

    expand_rows = ff // width
    early = [s_ffn, s_contract, s_attn, s_output]

    partials, received = (red, red_late), (red_in, red_late_in)

    def send_partial(kind, slot, src, where):
        return pltpu.make_async_remote_copy(
            src_ref=partials[kind].at[src],
            dst_ref=received[kind].at[slot],
            send_sem=red_send.at[kind, slot],
            recv_sem=red_recv.at[kind, slot],
            device_id=where,
            device_id_type=MESH,
        )

    def round_copies(kind, which):
        if which == 0:
            return [send_partial(kind, j - 1, 0, {"seq": flip(me, j)}) for j in peers]
        first = len(peers) + sum(len(masks) for masks in rounds[: which - 1])
        return [
            send_partial(kind, first + i, which, {"dp": flip(dp, m)})
            for i, m in enumerate(rounds[which - 1])
        ]

    def reduce_start(kind, which=0):
        for copy in round_copies(kind, which):
            copy.start()

    def reduce_end(kind, which):
        for copy in round_copies(kind, which):
            copy.wait()
        first = len(peers) + sum(len(masks) for masks in rounds[: which - 1]) if which else 0
        count = len(peers) if which == 0 else len(rounds[which - 1])
        parts = [partials[kind][which]] + [received[kind][first + i] for i in range(count)]
        while len(parts) > 1:
            parts = [parts[i] + parts[i + 1] for i in range(0, len(parts), 2)]
        partials[kind][which + 1] = parts[0]
        if which < len(rounds):
            reduce_start(kind, which + 1)

    for i, which in enumerate(early):
        red[0, i : i + 1, :] = jnp.sum(sums[which], 0, keepdims=True)
    for i in range(expand_rows):
        red[0, 4 + i : 5 + i, :] = jnp.sum(
            sum_expand[:, i * width : (i + 1) * width], 0, keepdims=True
        )
    reduce_start(0)

    def ctx_back_step(i):
        feats = ds(i * 256, 256)
        v_t[feats, :] = dot_nt(wo[feats, :], low[...]).astype(BF16)

    loop(width // 256, ctx_back_step, width // 256)
    dq_n, dk_n, dv_n = (big_a.at[:, i * width : (i + 1) * width] for i in range(3))
    dscore_refs = tuple(cot_buf.at[:, i * rows : (i + 1) * rows] for i in range(2))
    turned_q, turned_k = (k_n.at[:LANES, i * rows : (i + 1) * rows] for i in range(2))

    def dscore(p, j):
        lanes = ds(p * LANES, LANES)
        feats = ds(p * LANES + HEAD * j, HEAD)
        d = v_t[feats, :].astype(F32) * recip[pl.ds(2 * p + j, 1), :]
        inner = jnp.sum(d * ctx_t[feats, :].astype(F32), 0, keepdims=True)
        d_low = d.astype(BF16)
        zeros = jnp.zeros((HEAD, rows), BF16)
        padded = jnp.concatenate([d_low, zeros] if j == 0 else [zeros, d_low], 0)
        dprobs = dot_nn(v_n[:, lanes], padded)
        dscore_refs[j][...] = (probs[2 * p + j].astype(F32) * (dprobs - inner)).astype(BF16)
        return padded

    def turn_back(p):
        lanes = ds(p * LANES, LANES)
        dq_low = turned_q[...].T
        dq_n[:, lanes] = dq_low
        dk_n[:, lanes] = turned_k[...].T
        sums[s_query, :, lanes] = fold8(dq_low.astype(F32))

    def attn_back_step(p):
        turn_back(lax.rem(p + pairs - 1, pairs))
        lanes = ds(p * LANES, LANES)
        dv = None
        for j in range(2):
            padded = dscore(p, j)
            term = dot_nn(probs[2 * p + j], padded.T)
            dv = term if dv is None else dv + term
        dv_low = dv.astype(BF16)
        dv_n[:, lanes] = dv_low
        sums[s_value, :, lanes] = fold8(dv_low.astype(F32))
        for j in range(2):
            feats, half = ds(p * LANES + HEAD * j, HEAD), slice(HEAD * j, HEAD * j + HEAD)
            dq = dot_nn(k_t[feats, :], dscore_refs[j][...]) * scale
            turned_q[half, :] = dq.astype(BF16)
            turned_k[half, :] = dot_nt(q_t[feats, :], dscore_refs[j][...]).astype(BF16)

    pairs = HEADS // 2
    late = pairs - 2
    turned_q[...] = jnp.zeros_like(turned_q)
    turned_k[...] = jnp.zeros_like(turned_k)
    loop(late, attn_back_step, 2)
    reduce_end(0, 0)
    loop(2, lambda i: attn_back_step(late + i), 2)
    turn_back(pairs - 1)
    quarter = width // 4
    for i, which in enumerate((s_query, s_value)):
        for j in range(4):
            red_late[0, 4 * i + j : 4 * i + j + 1, :] = jnp.sum(
                sums[which, :, j * quarter : (j + 1) * quarter], 0, keepdims=True
            )
    reduce_start(1)

    chunk = 256

    def grad_step(base, i):
        here, cols = ds(base, pair), slice(i * chunk, (i + 1) * chunk)
        g = (
            resid[here, cols]
            + dot_nt(dq_n[here, :], wq[cols, :])
            + dot_nt(dk_n[here, :], wk[cols, :])
            + dot_nt(dv_n[here, :], wv[cols, :])
        )
        x_buf[here, cols] = g.astype(BF16)

    def grad_cols(buf, i):
        return lambda peer: buf.at[ds(peer * part, part), i * chunk : (i + 1) * chunk]

    def grad_home(i):
        return lambda member: grad_in.at[member, :, i * chunk : (i + 1) * chunk]

    chunks = width // chunk
    send_grad = [
        exchange(3 + i, grad_cols(x_buf, i), grad_home(i)(me)) for i in range(chunks)
    ]
    for hi in range(2, group, 2):
        base = flip(me, hi) - core
        for i in range(chunks):
            grad_step(base * part, i)
            for c in range(2):
                send_grad[i](base + c).start()
    reduce_end(1, 0)
    for i in range(chunks):
        grad_step((me - core) * part, i)
        send_grad[i](flip(me, 1)).start()
    fetch_start("grad", x_buf.at[mine], grad_in.at[me])

    for which in range(1, len(rounds) + 1):
        for kind in range(2):
            reduce_end(kind, which)
    final = 1 + len(rounds)
    small_out[...] = red[final] * factor
    late_out[...] = red_late[final] * factor

    for peer in members:
        arrived(2, lambda member: out.at[member], peer)
        for i in range(chunks):
            arrived(3 + i, grad_home(i), peer)
    for send in [send_x, send_cot, send_out] + send_grad:
        for peer in members:
            send(peer).wait_send()
    fetch["out"].wait()
    fetch["grad"].wait()


def finish(
    early_out,
    early_grad,
    early_small,
    late_small,
    out,
    grad_in,
    g_bias_query,
    g_bias_value,
    g_bias_output,
    g_shift_attn,
    g_bias_expand,
    g_bias_contract,
    g_shift_ffn,
    sem_out,
):
    pairs = [
        (src.at[i], dst.at[i], n * early_out.shape[0] + i)
        for n, (src, dst) in enumerate(((early_out, out), (early_grad, grad_in)))
        for i in range(early_out.shape[0])
    ]
    puts = [pltpu.make_async_copy(src, dst, sem_out.at[n]) for src, dst, n in pairs]
    for put in puts:
        put.start()
    width = early_small.shape[-1]
    for i, ref in enumerate((g_shift_ffn, g_bias_contract, g_shift_attn, g_bias_output)):
        ref[...] = early_small[i : i + 1, :]
    for i in range(g_bias_expand.shape[1] // width):
        g_bias_expand[:, i * width : (i + 1) * width] = early_small[4 + i : 5 + i, :]
    for i, ref in enumerate((g_bias_query, g_bias_value)):
        for j in range(4):
            ref[:, j * width // 4 : (j + 1) * width // 4] = late_small[4 * i + j : 4 * i + j + 1, :]
    for put in puts:
        put.wait()


def local(mesh, *args):
    hidden_in, lengths = args[:2]
    group, dp_size = mesh.shape["seq"], mesh.shape["dp"]
    seqs, part, width = hidden_in.shape
    ff = args[7].shape[1]
    rows = part * group
    assert seqs == group
    assert group & (group - 1) == 0 and dp_size & (dp_size - 1) == 0
    factor = (rows * seqs // group * dp_size * group) ** (-0.5)
    rounds = dp_rounds(dp_size)
    slots = group - 1 + sum(len(masks) for masks in rounds)
    anywhere = pl.BlockSpec(memory_space=pl.ANY)
    in_specs = [anywhere] * len(args)
    in_specs[1] = pl.BlockSpec(memory_space=pltpu.SMEM)
    vmem = pl.BlockSpec(memory_space=pltpu.VMEM)
    operands = [a.reshape(1, -1) if a.ndim == 1 and i != 1 else a for i, a in enumerate(args)]
    row = jax.ShapeDtypeStruct((1, width), F32)
    outs = pl.pallas_call(
        functools.partial(kernel, group, dp_size, factor),
        out_shape=[pltpu.VMEM(hidden_in.shape, BF16)] * 2
        + [pltpu.VMEM((8, width), F32), pltpu.VMEM((8, width // 4), F32)],
        in_specs=in_specs,
        out_specs=[vmem] * 4,
        scratch_shapes=[
            pltpu.VMEM((width, width), BF16),
            pltpu.VMEM((width, width), BF16),
            pltpu.VMEM((width, width), BF16),
            pltpu.VMEM((width, width), BF16),
            pltpu.VMEM((width, ff), BF16),
            pltpu.VMEM((ff, width), BF16),
            pltpu.VMEM((8, 1, width), F32),
            pltpu.VMEM((1, ff), F32),
            pltpu.VMEM((rows, width), BF16),
            pltpu.VMEM((rows, width), BF16),
            pltpu.VMEM((width, rows), BF16),
            pltpu.VMEM((rows, width), BF16),
            pltpu.VMEM((width, rows), BF16),
            pltpu.VMEM((rows, width), BF16),
            pltpu.VMEM((width, rows), BF16),
            pltpu.VMEM((HEADS, rows, rows), BF16),
            pltpu.VMEM((HEADS, rows), F32),
            pltpu.VMEM((width, rows), BF16),
            pltpu.VMEM((rows, width), BF16),
            pltpu.VMEM((rows, width), F32),
            pltpu.VMEM((rows, LANES), F32),
            pltpu.VMEM((rows, width), BF16),
            pltpu.VMEM((rows, ff), BF16),
            pltpu.VMEM((rows, ff), BF16),
            pltpu.VMEM((rows, width), F32),
            pltpu.VMEM((rows, rows), F32),
            pltpu.VMEM((rows, rows), F32),
            pltpu.VMEM((1, rows), F32),
            pltpu.VMEM((1, rows), F32),
            pltpu.VMEM((2, rows, LANES), BF16),
            pltpu.VMEM((6, 8, width), F32),
            pltpu.VMEM((8, ff), F32),
            pltpu.VMEM((2 + len(rounds), 8, width), F32),
            pltpu.VMEM((slots, 8, width), F32),
            pltpu.VMEM((2 + len(rounds), 8, width // 4), F32),
            pltpu.VMEM((slots, 8, width // 4), F32),
            pltpu.SemaphoreType.DMA((24,)),
            pltpu.SemaphoreType.DMA((3 + width // 256, group)),
            pltpu.SemaphoreType.DMA((3 + width // 256, group)),
            pltpu.SemaphoreType.DMA((2, slots)),
            pltpu.SemaphoreType.DMA((2, slots)),
        ],
        compiler_params=pltpu.CompilerParams(
            collective_id=0, has_side_effects=True, vmem_limit_bytes=64700000
        ),
        name="layer",
    )(*operands)
    outs = [pltpu.with_memory_space_constraint(o, pltpu.VMEM) for o in outs]
    blocks = 2 * seqs
    outs = pl.pallas_call(
        finish,
        out_shape=[jax.ShapeDtypeStruct(hidden_in.shape, BF16)] * 2
        + [row] * 4
        + [jax.ShapeDtypeStruct((1, ff), F32), row, row],
        in_specs=[vmem] * 4,
        out_specs=[anywhere] * 2 + [vmem] * 7,
        scratch_shapes=[pltpu.SemaphoreType.DMA((blocks,))],
        compiler_params=pltpu.CompilerParams(vmem_limit_bytes=4 * 2**20),
        name="finish",
    )(*outs)
    return tuple(o.reshape(-1) if o.shape[0] == 1 else o for o in outs)


def solution(mesh):
    placed = (P("dp", "seq", None), P("dp")) + (P(),) * 15 + (P("dp", "seq", None),)
    return jax.shard_map(
        functools.partial(local, mesh),
        mesh=mesh,
        in_specs=placed,
        out_specs=(P("dp", "seq", None), P("dp", "seq", None), P(), P(), P(), P(), P(), P(), P()),
        check_vma=False,
    )
```

```python
import functools
import math

import jax
import jax.numpy as jnp
from jax import lax
from jax.experimental import pallas as pl
from jax.experimental.pallas import tpu as pltpu
from jax.sharding import PartitionSpec as P

HEADS = 16
HEAD = 64
NEG = -1e30
EPSILON = 1e-12
LANES = 128
MESH = pl.DeviceIdType.MESH
F32 = jnp.float32
BF16 = jnp.bfloat16


def dot_nn(left, right):
    return jnp.dot(left, right, preferred_element_type=F32)


def dot_nt(left, right):
    return lax.dot_general(left, right, (((1,), (1,)), ((), ())), preferred_element_type=F32)


def flip(index, mask):
    bit = 1
    while bit <= mask:
        if mask & bit:
            index = index + bit - 2 * bit * ((index // bit) % 2)
        bit *= 2
    return index


def ds(start, size):
    return pl.ds(start if isinstance(start, int) else pl.multiple_of(start, size), size)


def dp_rounds(size):
    rounds, low = [], 1
    while low < size:
        high = min(low * 8, size)
        rounds.append([m * low for m in range(1, high // low)])
        low = high
    return rounds


def fold8(value):
    rows, width = value.shape
    return jnp.sum(value.reshape(rows // 8, 8, width), 0)


def loop(count, body, unroll=1):
    def step(index, carry):
        body(index)
        return carry

    lax.fori_loop(0, count, step, 0, unroll=unroll)


def kernel(
    group,
    dp_size,
    factor,
    hidden_in,
    lengths,
    w_query,
    w_key,
    w_value,
    w_output,
    gain_attn,
    w_expand,
    w_contract,
    gain_ffn,
    bias_query,
    bias_value,
    bias_output,
    shift_attn,
    bias_expand,
    bias_contract,
    shift_ffn,
    cotangent,
    out,
    grad_in,
    small_out,
    late_out,
    wq,
    wk,
    wv,
    wo,
    we,
    wc,
    vecs,
    vec_expand,
    x_buf,
    cot_buf,
    q_t,
    k_n,
    k_t,
    v_n,
    v_t,
    probs,
    recip,
    ctx_t,
    ctx_n,
    xh1,
    rstd1,
    low,
    big_a,
    big_b,
    resid,
    s_a,
    s_b,
    top_a,
    top_b,
    key_bias,
    sums,
    sum_expand,
    red,
    red_in,
    red_late,
    red_late_in,
    local_sem,
    send_sem,
    recv_sem,
    red_send,
    red_recv,
):
    me = lax.axis_index("seq")
    dp = lax.axis_index("dp")
    part = hidden_in.shape[1]
    rows, width = x_buf.shape
    ff = we.shape[1]
    peers = list(range(1, group))
    members = [flip(me, j) for j in peers]
    core = me % 2
    by_core = [flip(me, 1)] + [
        flip(me, hi) - core + c for c in range(2) for hi in range(2, group, 2)
    ]
    rounds = dp_rounds(dp_size)
    dp_masks = [m for masks in rounds for m in masks]

    small = (
        bias_query,
        bias_value,
        bias_output,
        gain_attn,
        shift_attn,
        bias_contract,
        gain_ffn,
        shift_ffn,
    )
    b_q, b_v, b_o, gain1, shift1, b_c, gain2, shift2 = range(8)
    fetch = {}

    def fetch_start(name, src, dst):
        fetch[name] = pltpu.make_async_copy(src, dst, local_sem.at[len(fetch)])
        fetch[name].start()

    mine = ds(me * part, part)
    fetch_start("x", hidden_in.at[me], x_buf.at[mine])
    fetch_start("wq", w_query, wq)
    fetch_start("wk", w_key, wk)
    fetch_start("wv", w_value, wv)

    barrier = pltpu.get_barrier_semaphore()
    for j in peers:
        pl.semaphore_signal(barrier, inc=1, device_id={"seq": flip(me, j)}, device_id_type=MESH)
    for m in dp_masks:
        pl.semaphore_signal(barrier, inc=1, device_id={"dp": flip(dp, m)}, device_id_type=MESH)
    pl.semaphore_wait(barrier, len(peers) + len(dp_masks))

    def exchange(kind, src_of, dst):
        def send(peer):
            return pltpu.make_async_remote_copy(
                src_ref=src_of(peer),
                dst_ref=dst,
                send_sem=send_sem.at[kind, peer],
                recv_sem=recv_sem.at[kind, me],
                device_id={"seq": peer},
                device_id_type=MESH,
            )

        return send

    def block_of(buf):
        return lambda peer: buf.at[ds(peer * part, part)]

    def arrived(kind, dst_of, peer):
        pltpu.make_async_remote_copy(
            src_ref=dst_of(peer),
            dst_ref=dst_of(peer),
            send_sem=send_sem.at[kind, peer],
            recv_sem=recv_sem.at[kind, peer],
            device_id={"seq": peer},
            device_id_type=MESH,
        ).wait_recv()

    send_x = exchange(0, lambda peer: hidden_in.at[peer], x_buf.at[mine])
    for peer in by_core:
        send_x(peer).start()
    for i, vec in enumerate(small):
        fetch_start(("v", i), vec, vecs.at[i])
    fetch_start("be", bias_expand, vec_expand)
    fetch_start("wo", w_output, wo)
    fetch_start("we", w_expand, we)
    send_cot = exchange(1, lambda peer: cotangent.at[peer], cot_buf.at[mine])

    def cot_start(which):
        @pl.when(core == which)
        def _():
            for peer in by_core:
                send_cot(peer).start()

    fetch_start("cot", cotangent.at[me], cot_buf.at[mine])
    fetch_start("wc", w_contract, wc)

    sums[...] = jnp.zeros_like(sums)
    sum_expand[...] = jnp.zeros_like(sum_expand)
    s_ffn, s_contract, s_attn, s_output, s_query, s_value = range(6)

    scale = HEAD ** (-0.5)
    pair = 2 * part

    def qkv(base, unroll):
        here = ds(base, pair)
        xs = x_buf[here, :]

        def step(i):
            cols = ds(i * 256, 256)
            q = ((dot_nn(xs, wq[:, cols]) + vecs[b_q, :, cols]) * scale).astype(BF16)
            q_t[cols, here] = q.T
            k = dot_nn(xs, wk[:, cols]).astype(BF16)
            k_n[here, cols] = k
            k_t[cols, here] = k.T
            v = (dot_nn(xs, wv[:, cols]) + vecs[b_v, :, cols]).astype(BF16)
            v_n[here, cols] = v
            v_t[cols, here] = v.T

        loop(width // 256, step, unroll)

    length = lengths[me]
    row = lax.broadcasted_iota(jnp.int32, (rows, LANES), 0)
    lane = lax.broadcasted_iota(jnp.int32, (rows, LANES), 1)
    for j in range(2):
        key_bias[j] = jnp.where((row >= length) & (lane == HEAD * (1 - j)), NEG, 0.0).astype(BF16)

    for i in range(len(small)):
        fetch["v", i].wait()
    fetch["x"].wait()
    fetch["wq"].wait()
    fetch["wk"].wait()
    fetch["wv"].wait()
    arrived(0, block_of(x_buf), flip(me, 1))
    qkv((me - core) * part, 1)
    for hi in range(2, group, 2):
        for c in range(2):
            arrived(0, block_of(x_buf), flip(me, hi) - core + c)
        if hi == group - 2:
            cot_start(1)
        qkv((flip(me, hi) - core) * part, width // 256)

    score_refs, top_refs = (s_a, s_b), (top_a, top_b)

    def score(p, j):
        lanes = ds(p * LANES, LANES)
        half = lax.broadcasted_iota(jnp.int32, (rows, LANES), 1) < HEAD
        k_one = jnp.where(half if j == 0 else ~half, k_n[:, lanes], key_bias[j])
        q_one = q_t[ds(p * LANES + HEAD * j, HEAD), :]
        pad = [jnp.ones((16, rows), BF16), jnp.zeros((HEAD - 16, rows), BF16)]
        q_one = jnp.concatenate([q_one] + pad if j == 0 else pad + [q_one], 0)
        for c in range(0, rows, 256):
            cols = slice(c, c + 256)
            block = dot_nn(k_one, q_one[:, cols])
            score_refs[j][:, cols] = block
            top_refs[j][:, cols] = jnp.max(block, 0, keepdims=True)

    def exponential(h, j):
        for c in range(0, rows, 256):
            cols = slice(c, c + 256)
            probs[h, :, cols] = jnp.exp(score_refs[j][:, cols] - top_refs[j][:, cols]).astype(BF16)

    def weigh(h):
        feats = ds(h * HEAD, HEAD)
        o = dot_nn(jnp.concatenate([v_t[feats, :], jnp.ones((16, rows), BF16)], 0), probs[h])
        inv = 1.0 / o[HEAD : HEAD + 1]
        recip[pl.ds(h, 1), :] = inv
        ctx_t[feats, :] = (o[:HEAD] * inv).astype(BF16)

    def turn(p):
        lanes = ds(p * LANES, LANES)
        ctx_n[:, lanes] = ctx_t[lanes, :].T

    pairs = HEADS // 2
    for j in range(2):
        score(0, j)

    def attn_step(p, last=False):
        for j in range(2):
            exponential(2 * p + j, j)
        if not last:
            for j in range(2):
                score(p + 1, j)
        for j in range(2):
            weigh(2 * p + j)
        turn(p)

    loop(pairs - 1, attn_step, pairs - 1)
    attn_step(pairs - 1, last=True)

    cot_start(0)

    fetch["wo"].wait()

    def out_proj_step(i):
        part_rows = ds(i * 256, 256)
        ao = dot_nn(ctx_n[part_rows, :], wo[...]) + vecs[b_o]
        h = x_buf[part_rows, :].astype(F32) + ao
        center = h - jnp.mean(h, -1, keepdims=True)
        r = lax.rsqrt(jnp.mean(center * center, -1, keepdims=True) + EPSILON)
        xh = center * r
        xh1[part_rows, :] = xh
        rstd1[part_rows, :] = jnp.broadcast_to(r, (256, LANES))
        low[part_rows, :] = (xh * vecs[gain1] + vecs[shift1]).astype(BF16)

    loop(rows // 256, out_proj_step, rows // 256)

    fetch["we"].wait()
    fetch["be"].wait()

    def expand(i):
        cols = ds(i * 512, 512)
        s_a[...] = dot_nn(low[...], we[:, cols]) + vec_expand[:, cols]

    def gelu(i):
        cols = ds(i * 512, 512)
        f = s_a[...]
        t = f * (0.5**0.5)
        phi = 0.5 * lax.erf(t) + 0.5
        big_a[:, cols] = (f * phi).astype(BF16)
        bell = jnp.exp2(t * t * (-1.0 / math.log(2.0)))
        big_b[:, cols] = (phi + t * (1.0 / math.pi) ** 0.5 * bell).astype(BF16)

    expand(0)

    def expand_step(i):
        gelu(i)
        expand(i + 1)

    loop(ff // 512 - 1, expand_step, ff // 512 - 1)
    gelu(ff // 512 - 1)
    fetch["wc"].wait()

    def contract_step(i):
        cols = ds(i * 256, 256)
        n1 = xh1[:, cols] * vecs[gain1, :, cols] + vecs[shift1, :, cols]
        resid[:, cols] = n1 + dot_nn(big_a[...], wc[:, cols]) + vecs[b_c, :, cols]

    loop(width // 256, contract_step, width // 256)

    fetch["cot"].wait()
    for peer in members:
        arrived(1, block_of(cot_buf), peer)

    def norm2_step(i):
        part_rows = ds(i * 128, 128)
        h = resid[part_rows, :]
        center = h - jnp.mean(h, -1, keepdims=True)
        r = lax.rsqrt(jnp.mean(center * center, -1, keepdims=True) + EPSILON)
        xh = center * r
        ctx_n[part_rows, :] = (xh * vecs[gain2] + vecs[shift2]).astype(BF16)
        dy = cot_buf[part_rows, :].astype(F32)
        sums[s_ffn] += fold8(dy)
        e = dy * vecs[gain2]
        d = r * (e - jnp.mean(e, -1, keepdims=True) - xh * jnp.mean(e * xh, -1, keepdims=True))
        resid[part_rows, :] = d
        d_low = d.astype(BF16)
        low[part_rows, :] = d_low
        sums[s_contract] += fold8(d_low.astype(F32))

    loop(rows // 128, norm2_step, 2)

    send_out = exchange(2, block_of(ctx_n), out.at[me])
    for peer in by_core:
        send_out(peer).start()
    fetch_start("out", block_of(ctx_n)(me), out.at[me])

    def contract_back_step(i):
        cols = ds(i * 1024, 1024)
        df = (dot_nt(low[...], wc[cols, :]) * big_b[:, cols].astype(F32)).astype(BF16)
        big_b[:, cols] = df
        sum_expand[:, cols] += fold8(df.astype(F32))

    loop(ff // 1024, contract_back_step, ff // 1024)

    def expand_back_step(i):
        cols = ds(i * 256, 256)
        resid[:, cols] += dot_nt(big_b[...], we[cols, :])

    loop(width // 256, expand_back_step, width // 256)

    def norm1_step(i):
        part_rows = ds(i * 128, 128)
        dn = resid[part_rows, :]
        sums[s_attn] += fold8(dn)
        e = dn * vecs[gain1]
        xh = xh1[part_rows, :]
        r = rstd1[part_rows, :1]
        d = r * (e - jnp.mean(e, -1, keepdims=True) - xh * jnp.mean(e * xh, -1, keepdims=True))
        resid[part_rows, :] = d
        d_low = d.astype(BF16)
        low[part_rows, :] = d_low
        sums[s_output] += fold8(d_low.astype(F32))

    loop(rows // 128, norm1_step, 2)

    expand_rows = ff // width
    early = [s_ffn, s_contract, s_attn, s_output]

    partials, received = (red, red_late), (red_in, red_late_in)

    def send_partial(kind, slot, src, where):
        return pltpu.make_async_remote_copy(
            src_ref=partials[kind].at[src],
            dst_ref=received[kind].at[slot],
            send_sem=red_send.at[kind, slot],
            recv_sem=red_recv.at[kind, slot],
            device_id=where,
            device_id_type=MESH,
        )

    def round_copies(kind, which):
        if which == 0:
            return [send_partial(kind, j - 1, 0, {"seq": flip(me, j)}) for j in peers]
        first = len(peers) + sum(len(masks) for masks in rounds[: which - 1])
        return [
            send_partial(kind, first + i, which, {"dp": flip(dp, m)})
            for i, m in enumerate(rounds[which - 1])
        ]

    def reduce_start(kind, which=0):
        for copy in round_copies(kind, which):
            copy.start()

    def reduce_end(kind, which):
        for copy in round_copies(kind, which):
            copy.wait()
        first = len(peers) + sum(len(masks) for masks in rounds[: which - 1]) if which else 0
        count = len(peers) if which == 0 else len(rounds[which - 1])
        parts = [partials[kind][which]] + [received[kind][first + i] for i in range(count)]
        while len(parts) > 1:
            parts = [parts[i] + parts[i + 1] for i in range(0, len(parts), 2)]
        partials[kind][which + 1] = parts[0]
        if which < len(rounds):
            reduce_start(kind, which + 1)

    for i, which in enumerate(early):
        red[0, i : i + 1, :] = jnp.sum(sums[which], 0, keepdims=True)
    for i in range(expand_rows):
        red[0, 4 + i : 5 + i, :] = jnp.sum(
            sum_expand[:, i * width : (i + 1) * width], 0, keepdims=True
        )
    reduce_start(0)

    def ctx_back_step(i):
        feats = ds(i * 256, 256)
        v_t[feats, :] = dot_nt(wo[feats, :], low[...]).astype(BF16)

    loop(width // 256, ctx_back_step, width // 256)
    dq_n, dk_n, dv_n = (big_a.at[:, i * width : (i + 1) * width] for i in range(3))
    dscore_refs = tuple(cot_buf.at[:, i * rows : (i + 1) * rows] for i in range(2))
    turned_q, turned_k = (k_n.at[:LANES, i * rows : (i + 1) * rows] for i in range(2))

    def dscore(p, j):
        lanes = ds(p * LANES, LANES)
        feats = ds(p * LANES + HEAD * j, HEAD)
        d = v_t[feats, :].astype(F32) * recip[pl.ds(2 * p + j, 1), :]
        inner = jnp.sum(d * ctx_t[feats, :].astype(F32), 0, keepdims=True)
        d_low = d.astype(BF16)
        zeros = jnp.zeros((HEAD, rows), BF16)
        padded = jnp.concatenate([d_low, zeros] if j == 0 else [zeros, d_low], 0)
        dprobs = dot_nn(v_n[:, lanes], padded)
        dscore_refs[j][...] = (probs[2 * p + j].astype(F32) * (dprobs - inner)).astype(BF16)
        return padded

    def turn_back(p):
        lanes = ds(p * LANES, LANES)
        dq_low = turned_q[...].T
        dq_n[:, lanes] = dq_low
        dk_n[:, lanes] = turned_k[...].T
        sums[s_query, :, lanes] = fold8(dq_low.astype(F32))

    def attn_back_step(p):
        turn_back(lax.rem(p + pairs - 1, pairs))
        lanes = ds(p * LANES, LANES)
        dv = None
        for j in range(2):
            padded = dscore(p, j)
            term = dot_nn(probs[2 * p + j], padded.T)
            dv = term if dv is None else dv + term
        dv_low = dv.astype(BF16)
        dv_n[:, lanes] = dv_low
        sums[s_value, :, lanes] = fold8(dv_low.astype(F32))
        for j in range(2):
            feats, half = ds(p * LANES + HEAD * j, HEAD), slice(HEAD * j, HEAD * j + HEAD)
            dq = dot_nn(k_t[feats, :], dscore_refs[j][...]) * scale
            turned_q[half, :] = dq.astype(BF16)
            turned_k[half, :] = dot_nt(q_t[feats, :], dscore_refs[j][...]).astype(BF16)

    late = pairs - 2
    turned_q[...] = jnp.zeros_like(turned_q)
    turned_k[...] = jnp.zeros_like(turned_k)
    loop(late, attn_back_step, 2)
    reduce_end(0, 0)
    loop(2, lambda i: attn_back_step(late + i), 2)
    turn_back(pairs - 1)
    quarter = width // 4
    for i, which in enumerate((s_query, s_value)):
        for j in range(4):
            red_late[0, 4 * i + j : 4 * i + j + 1, :] = jnp.sum(
                sums[which, :, j * quarter : (j + 1) * quarter], 0, keepdims=True
            )
    reduce_start(1)

    chunk = 256

    def grad_step(base, i):
        here, cols = ds(base, pair), ds(i * chunk, chunk)
        g = (
            resid[here, cols]
            + dot_nt(dq_n[here, :], wq[cols, :])
            + dot_nt(dk_n[here, :], wk[cols, :])
            + dot_nt(dv_n[here, :], wv[cols, :])
        )
        x_buf[here, cols] = g.astype(BF16)

    def grad_cols(buf, i):
        return lambda peer: buf.at[ds(peer * part, part), i * chunk : (i + 1) * chunk]

    def grad_home(i):
        return lambda member: grad_in.at[member, :, i * chunk : (i + 1) * chunk]

    chunks = width // chunk
    send_grad = [
        exchange(3 + i, grad_cols(x_buf, i), grad_home(i)(me)) for i in range(chunks)
    ]
    for hi in range(2, group, 2):
        base = flip(me, hi) - core
        for i in range(chunks):
            grad_step(base * part, i)
            for c in range(2):
                send_grad[i](base + c).start()
    reduce_end(1, 0)
    loop(chunks, lambda i: grad_step((me - core) * part, i))
    for i in range(chunks):
        send_grad[i](flip(me, 1)).start()
    fetch_start("grad", x_buf.at[mine], grad_in.at[me])

    for which in range(1, len(rounds) + 1):
        for kind in range(2):
            reduce_end(kind, which)
    final = 1 + len(rounds)
    small_out[...] = red[final] * factor
    late_out[...] = red_late[final] * factor

    for peer in members:
        arrived(2, lambda member: out.at[member], peer)
        for i in range(chunks):
            arrived(3 + i, grad_home(i), peer)
    for send in [send_x, send_cot, send_out] + send_grad:
        for peer in members:
            send(peer).wait_send()
    fetch["out"].wait()
    fetch["grad"].wait()


def finish(
    early_out,
    early_grad,
    early_small,
    late_small,
    out,
    grad_in,
    g_bias_query,
    g_bias_value,
    g_bias_output,
    g_shift_attn,
    g_bias_expand,
    g_bias_contract,
    g_shift_ffn,
    sem_out,
):
    pairs = [
        (src.at[i], dst.at[i], n * early_out.shape[0] + i)
        for n, (src, dst) in enumerate(((early_out, out), (early_grad, grad_in)))
        for i in range(early_out.shape[0])
    ]
    puts = [pltpu.make_async_copy(src, dst, sem_out.at[n]) for src, dst, n in pairs]
    for put in puts:
        put.start()
    width = early_small.shape[-1]
    for i, ref in enumerate((g_shift_ffn, g_bias_contract, g_shift_attn, g_bias_output)):
        ref[...] = early_small[i : i + 1, :]
    for i in range(g_bias_expand.shape[1] // width):
        g_bias_expand[:, i * width : (i + 1) * width] = early_small[4 + i : 5 + i, :]
    for i, ref in enumerate((g_bias_query, g_bias_value)):
        for j in range(4):
            ref[:, j * width // 4 : (j + 1) * width // 4] = late_small[4 * i + j : 4 * i + j + 1, :]
    for put in puts:
        put.wait()


def local(mesh, *args):
    hidden_in, lengths = args[:2]
    group, dp_size = mesh.shape["seq"], mesh.shape["dp"]
    seqs, part, width = hidden_in.shape
    ff = args[7].shape[1]
    rows = part * group
    assert seqs == group
    assert group & (group - 1) == 0 and dp_size & (dp_size - 1) == 0
    factor = (rows * seqs // group * dp_size * group) ** (-0.5)
    rounds = dp_rounds(dp_size)
    slots = group - 1 + sum(len(masks) for masks in rounds)
    anywhere = pl.BlockSpec(memory_space=pl.ANY)
    in_specs = [anywhere] * len(args)
    in_specs[1] = pl.BlockSpec(memory_space=pltpu.SMEM)
    vmem = pl.BlockSpec(memory_space=pltpu.VMEM)
    operands = [a.reshape(1, -1) if a.ndim == 1 and i != 1 else a for i, a in enumerate(args)]
    row = jax.ShapeDtypeStruct((1, width), F32)
    outs = pl.pallas_call(
        functools.partial(kernel, group, dp_size, factor),
        out_shape=[pltpu.VMEM(hidden_in.shape, BF16)] * 2
        + [pltpu.VMEM((8, width), F32), pltpu.VMEM((8, width // 4), F32)],
        in_specs=in_specs,
        out_specs=[vmem] * 4,
        scratch_shapes=[
            pltpu.VMEM((width, width), BF16),
            pltpu.VMEM((width, width), BF16),
            pltpu.VMEM((width, width), BF16),
            pltpu.VMEM((width, width), BF16),
            pltpu.VMEM((width, ff), BF16),
            pltpu.VMEM((ff, width), BF16),
            pltpu.VMEM((8, 1, width), F32),
            pltpu.VMEM((1, ff), F32),
            pltpu.VMEM((rows, width), BF16),
            pltpu.VMEM((rows, width), BF16),
            pltpu.VMEM((width, rows), BF16),
            pltpu.VMEM((rows, width), BF16),
            pltpu.VMEM((width, rows), BF16),
            pltpu.VMEM((rows, width), BF16),
            pltpu.VMEM((width, rows), BF16),
            pltpu.VMEM((HEADS, rows, rows), BF16),
            pltpu.VMEM((HEADS, rows), F32),
            pltpu.VMEM((width, rows), BF16),
            pltpu.VMEM((rows, width), BF16),
            pltpu.VMEM((rows, width), F32),
            pltpu.VMEM((rows, LANES), F32),
            pltpu.VMEM((rows, width), BF16),
            pltpu.VMEM((rows, ff), BF16),
            pltpu.VMEM((rows, ff), BF16),
            pltpu.VMEM((rows, width), F32),
            pltpu.VMEM((rows, rows), F32),
            pltpu.VMEM((rows, rows), F32),
            pltpu.VMEM((1, rows), F32),
            pltpu.VMEM((1, rows), F32),
            pltpu.VMEM((2, rows, LANES), BF16),
            pltpu.VMEM((6, 8, width), F32),
            pltpu.VMEM((8, ff), F32),
            pltpu.VMEM((2 + len(rounds), 8, width), F32),
            pltpu.VMEM((slots, 8, width), F32),
            pltpu.VMEM((2 + len(rounds), 8, width // 4), F32),
            pltpu.VMEM((slots, 8, width // 4), F32),
            pltpu.SemaphoreType.DMA((24,)),
            pltpu.SemaphoreType.DMA((3 + width // 256, group)),
            pltpu.SemaphoreType.DMA((3 + width // 256, group)),
            pltpu.SemaphoreType.DMA((2, slots)),
            pltpu.SemaphoreType.DMA((2, slots)),
        ],
        compiler_params=pltpu.CompilerParams(
            collective_id=0, has_side_effects=True, vmem_limit_bytes=64700000
        ),
        name="layer",
    )(*operands)
    outs = [pltpu.with_memory_space_constraint(o, pltpu.VMEM) for o in outs]
    blocks = 2 * seqs
    outs = pl.pallas_call(
        finish,
        out_shape=[jax.ShapeDtypeStruct(hidden_in.shape, BF16)] * 2
        + [row] * 4
        + [jax.ShapeDtypeStruct((1, ff), F32), row, row],
        in_specs=[vmem] * 4,
        out_specs=[anywhere] * 2 + [vmem] * 7,
        scratch_shapes=[pltpu.SemaphoreType.DMA((blocks,))],
        compiler_params=pltpu.CompilerParams(vmem_limit_bytes=4 * 2**20),
        name="finish",
    )(*outs)
    return tuple(o.reshape(-1) if o.shape[0] == 1 else o for o in outs)


def solution(mesh):
    placed = (P("dp", "seq", None), P("dp")) + (P(),) * 15 + (P("dp", "seq", None),)
    return jax.shard_map(
        functools.partial(local, mesh),
        mesh=mesh,
        in_specs=placed,
        out_specs=(P("dp", "seq", None), P("dp", "seq", None), P(), P(), P(), P(), P(), P(), P()),
        check_vma=False,
    )
```

```python
import functools
import math

import jax
import jax.numpy as jnp
from jax import lax
from jax.experimental import pallas as pl
from jax.experimental.pallas import tpu as pltpu
from jax.sharding import PartitionSpec as P

HEADS = 16
HEAD = 64
NEG = -1e30
EPSILON = 1e-12
LANES = 128
MESH = pl.DeviceIdType.MESH
F32 = jnp.float32
BF16 = jnp.bfloat16


def dot_nn(left, right):
    return jnp.dot(left, right, preferred_element_type=F32)


def dot_nt(left, right):
    return lax.dot_general(left, right, (((1,), (1,)), ((), ())), preferred_element_type=F32)


def flip(index, mask):
    bit = 1
    while bit <= mask:
        if mask & bit:
            index = index + bit - 2 * bit * ((index // bit) % 2)
        bit *= 2
    return index


def ds(start, size):
    return pl.ds(start if isinstance(start, int) else pl.multiple_of(start, size), size)


def dp_rounds(size):
    rounds, low = [], 1
    while low < size:
        high = min(low * 8, size)
        rounds.append([m * low for m in range(1, high // low)])
        low = high
    return rounds


def column_chunks(width):
    edges = [0, width // 2, width]
    return [slice(a, b) for a, b in zip(edges, edges[1:])]


def fold8(value):
    rows, width = value.shape
    return jnp.sum(value.reshape(rows // 8, 8, width), 0)


def loop(count, body, unroll=1):
    def step(index, carry):
        body(index)
        return carry

    lax.fori_loop(0, count, step, 0, unroll=unroll)


def kernel(
    group,
    dp_size,
    factor,
    hidden_in,
    lengths,
    w_query,
    w_key,
    w_value,
    w_output,
    gain_attn,
    w_expand,
    w_contract,
    gain_ffn,
    bias_query,
    bias_value,
    bias_output,
    shift_attn,
    bias_expand,
    bias_contract,
    shift_ffn,
    cotangent,
    out,
    grad_in,
    small_out,
    late_out,
    wq,
    wk,
    wv,
    wo,
    we,
    wc,
    vecs,
    vec_expand,
    x_buf,
    cot_buf,
    q_t,
    k_n,
    k_t,
    v_n,
    v_t,
    probs,
    recip,
    ctx_t,
    ctx_n,
    xh1,
    rstd1,
    low,
    big_a,
    big_b,
    resid,
    s_a,
    s_b,
    top_a,
    top_b,
    key_bias,
    sums,
    sum_expand,
    red,
    red_in,
    red_late,
    red_late_in,
    local_sem,
    send_sem,
    recv_sem,
    red_send,
    red_recv,
):
    me = lax.axis_index("seq")
    dp = lax.axis_index("dp")
    part = hidden_in.shape[1]
    rows, width = x_buf.shape
    ff = we.shape[1]
    grad_chunks = column_chunks(width)
    peers = list(range(1, group))
    members = [flip(me, j) for j in peers]
    core = me % 2
    by_core = [flip(me, 1)] + [
        flip(me, hi) - core + c for c in range(2) for hi in range(2, group, 2)
    ]
    rounds = dp_rounds(dp_size)
    dp_masks = [m for masks in rounds for m in masks]

    small = (
        bias_query,
        bias_value,
        bias_output,
        gain_attn,
        shift_attn,
        bias_contract,
        gain_ffn,
        shift_ffn,
    )
    b_q, b_v, b_o, gain1, shift1, b_c, gain2, shift2 = range(8)
    fetch = {}

    def fetch_start(name, src, dst):
        fetch[name] = pltpu.make_async_copy(src, dst, local_sem.at[len(fetch)])
        fetch[name].start()

    mine = ds(me * part, part)
    fetch_start("x", hidden_in.at[me], x_buf.at[mine])
    fetch_start("wq", w_query, wq)
    fetch_start("wk", w_key, wk)
    fetch_start("wv", w_value, wv)

    barrier = pltpu.get_barrier_semaphore()
    for j in peers:
        pl.semaphore_signal(barrier, inc=1, device_id={"seq": flip(me, j)}, device_id_type=MESH)
    for m in dp_masks:
        pl.semaphore_signal(barrier, inc=1, device_id={"dp": flip(dp, m)}, device_id_type=MESH)
    pl.semaphore_wait(barrier, len(peers) + len(dp_masks))

    def exchange(kind, src_of, dst):
        def send(peer):
            return pltpu.make_async_remote_copy(
                src_ref=src_of(peer),
                dst_ref=dst,
                send_sem=send_sem.at[kind, peer],
                recv_sem=recv_sem.at[kind, me],
                device_id={"seq": peer},
                device_id_type=MESH,
            )

        return send

    def block_of(buf):
        return lambda peer: buf.at[ds(peer * part, part)]

    def arrived(kind, dst_of, peer):
        pltpu.make_async_remote_copy(
            src_ref=dst_of(peer),
            dst_ref=dst_of(peer),
            send_sem=send_sem.at[kind, peer],
            recv_sem=recv_sem.at[kind, peer],
            device_id={"seq": peer},
            device_id_type=MESH,
        ).wait_recv()

    halves = [slice(0, width // 2), slice(width // 2, width)]
    x_kinds = (0, 3 + len(grad_chunks))
    send_x = [
        exchange(kind, lambda peer, half=half: hidden_in.at[peer, :, half], x_buf.at[mine, half])
        for kind, half in zip(x_kinds, halves)
    ]
    for send in send_x:
        send(flip(me, 1)).start()
    for c in range(2):
        for send in send_x:
            for hi in range(2, group, 2):
                send(flip(me, hi) - core + c).start()
    for i, vec in enumerate(small):
        fetch_start(("v", i), vec, vecs.at[i])
    fetch_start("be", bias_expand, vec_expand)
    fetch_start("wo", w_output, wo)
    fetch_start("we", w_expand, we)
    send_cot = exchange(1, lambda peer: cotangent.at[peer], cot_buf.at[mine])

    def cot_start(which):
        @pl.when(core == which)
        def _():
            for peer in by_core:
                send_cot(peer).start()

    fetch_start("cot", cotangent.at[me], cot_buf.at[mine])
    fetch_start("wc", w_contract, wc)

    sums[...] = jnp.zeros_like(sums)
    sum_expand[...] = jnp.zeros_like(sum_expand)
    s_ffn, s_contract, s_attn, s_output, s_query, s_value = range(6)

    scale = HEAD ** (-0.5)
    pair = 2 * part

    def qkv(base, unroll, half=None, kept=None):
        here = ds(base, pair)
        xs = x_buf[here, :] if half is None else x_buf[here, half]

        def step(i):
            cols = ds(i * 256, 256)
            q, k, v = (
                dot_nn(xs, w[:, cols] if half is None else w[half, cols]) for w in (wq, wk, wv)
            )
            if kept is not None:
                q, k, v = (p + ref[:, cols] for p, ref in zip((q, k, v), kept))
            q = ((q + vecs[b_q, :, cols]) * scale).astype(BF16)
            q_t[cols, here] = q.T
            k = k.astype(BF16)
            k_n[here, cols] = k
            k_t[cols, here] = k.T
            v = (v + vecs[b_v, :, cols]).astype(BF16)
            v_n[here, cols] = v
            v_t[cols, here] = v.T

        loop(width // 256, step, unroll)

    def qkv_first(base, half, kept):
        xs = x_buf[ds(base, pair), half]

        def step(i):
            cols = ds(i * 256, 256)
            for w, ref in zip((wq, wk, wv), kept):
                ref[:, cols] = dot_nn(xs, w[half, cols])

        loop(width // 256, step)

    length = lengths[me]
    row = lax.broadcasted_iota(jnp.int32, (rows, LANES), 0)
    lane = lax.broadcasted_iota(jnp.int32, (rows, LANES), 1)
    for j in range(2):
        key_bias[j] = jnp.where((row >= length) & (lane == HEAD * (1 - j)), NEG, 0.0).astype(BF16)

    for i in range(len(small)):
        fetch["v", i].wait()
    fetch["x"].wait()
    fetch["wq"].wait()
    fetch["wk"].wait()
    fetch["wv"].wait()
    def x_half(half):
        return lambda peer: x_buf.at[ds(peer * part, part), half]

    for kind, half in zip(x_kinds, halves):
        arrived(kind, x_half(half), flip(me, 1))
    qkv((me - core) * part, 1)
    kept = (resid.at[:pair], resid.at[pair : 2 * pair], xh1.at[:pair])
    for hi in range(2, group, 2):
        base = flip(me, hi) - core
        for c in range(2):
            arrived(x_kinds[0], x_half(halves[0]), base + c)
        qkv_first(base * part, halves[0], kept)
        for c in range(2):
            arrived(x_kinds[1], x_half(halves[1]), base + c)
        if hi == group - 2:
            cot_start(1)
        qkv(base * part, width // 256, halves[1], kept)

    score_refs, top_refs = (s_a, s_b), (top_a, top_b)

    def score(p, j):
        lanes = ds(p * LANES, LANES)
        half = lax.broadcasted_iota(jnp.int32, (rows, LANES), 1) < HEAD
        k_one = jnp.where(half if j == 0 else ~half, k_n[:, lanes], key_bias[j])
        q_one = q_t[ds(p * LANES + HEAD * j, HEAD), :]
        pad = [jnp.ones((16, rows), BF16), jnp.zeros((HEAD - 16, rows), BF16)]
        q_one = jnp.concatenate([q_one] + pad if j == 0 else pad + [q_one], 0)
        for c in range(0, rows, 256):
            cols = slice(c, c + 256)
            block = dot_nn(k_one, q_one[:, cols])
            score_refs[j][:, cols] = block
            top_refs[j][:, cols] = jnp.max(block, 0, keepdims=True)

    def exponential(h, j):
        for c in range(0, rows, 256):
            cols = slice(c, c + 256)
            probs[h, :, cols] = jnp.exp(score_refs[j][:, cols] - top_refs[j][:, cols]).astype(BF16)

    def weigh(h):
        feats = ds(h * HEAD, HEAD)
        o = dot_nn(jnp.concatenate([v_t[feats, :], jnp.ones((16, rows), BF16)], 0), probs[h])
        inv = 1.0 / o[HEAD : HEAD + 1]
        recip[pl.ds(h, 1), :] = inv
        ctx_t[feats, :] = (o[:HEAD] * inv).astype(BF16)

    def turn(p):
        lanes = ds(p * LANES, LANES)
        ctx_n[:, lanes] = ctx_t[lanes, :].T

    pairs = HEADS // 2
    for j in range(2):
        score(0, j)

    def attn_step(p, last=False):
        for j in range(2):
            exponential(2 * p + j, j)
        if not last:
            for j in range(2):
                score(p + 1, j)
        for j in range(2):
            weigh(2 * p + j)
        turn(p)

    loop(pairs - 1, attn_step, pairs - 1)
    attn_step(pairs - 1, last=True)

    cot_start(0)

    fetch["wo"].wait()

    def out_proj_step(i):
        part_rows = ds(i * 256, 256)
        ao = dot_nn(ctx_n[part_rows, :], wo[...]) + vecs[b_o]
        h = x_buf[part_rows, :].astype(F32) + ao
        center = h - jnp.mean(h, -1, keepdims=True)
        r = lax.rsqrt(jnp.mean(center * center, -1, keepdims=True) + EPSILON)
        xh = center * r
        xh1[part_rows, :] = xh
        rstd1[part_rows, :] = jnp.broadcast_to(r, (256, LANES))
        low[part_rows, :] = (xh * vecs[gain1] + vecs[shift1]).astype(BF16)

    loop(rows // 256, out_proj_step, rows // 256)

    fetch["we"].wait()
    fetch["be"].wait()

    def expand(i):
        cols = ds(i * 512, 512)
        s_a[...] = dot_nn(low[...], we[:, cols]) + vec_expand[:, cols]

    def gelu(i):
        cols = ds(i * 512, 512)
        f = s_a[...]
        t = f * (0.5**0.5)
        phi = 0.5 * lax.erf(t) + 0.5
        big_a[:, cols] = (f * phi).astype(BF16)
        bell = jnp.exp2(t * t * (-1.0 / math.log(2.0)))
        big_b[:, cols] = (phi + t * (1.0 / math.pi) ** 0.5 * bell).astype(BF16)

    expand(0)

    def expand_step(i):
        gelu(i)
        expand(i + 1)

    loop(ff // 512 - 1, expand_step, ff // 512 - 1)
    gelu(ff // 512 - 1)
    fetch["wc"].wait()

    def contract_step(i):
        cols = ds(i * 256, 256)
        n1 = xh1[:, cols] * vecs[gain1, :, cols] + vecs[shift1, :, cols]
        resid[:, cols] = n1 + dot_nn(big_a[...], wc[:, cols]) + vecs[b_c, :, cols]

    loop(width // 256, contract_step, width // 256)

    fetch["cot"].wait()
    for peer in members:
        arrived(1, block_of(cot_buf), peer)

    def norm2_step(i):
        part_rows = ds(i * 128, 128)
        h = resid[part_rows, :]
        center = h - jnp.mean(h, -1, keepdims=True)
        r = lax.rsqrt(jnp.mean(center * center, -1, keepdims=True) + EPSILON)
        xh = center * r
        ctx_n[part_rows, :] = (xh * vecs[gain2] + vecs[shift2]).astype(BF16)
        dy = cot_buf[part_rows, :].astype(F32)
        sums[s_ffn] += fold8(dy)
        e = dy * vecs[gain2]
        d = r * (e - jnp.mean(e, -1, keepdims=True) - xh * jnp.mean(e * xh, -1, keepdims=True))
        resid[part_rows, :] = d
        d_low = d.astype(BF16)
        low[part_rows, :] = d_low
        sums[s_contract] += fold8(d_low.astype(F32))

    loop(rows // 128, norm2_step, 2)

    send_out = exchange(2, block_of(ctx_n), out.at[me])
    for peer in by_core:
        send_out(peer).start()
    fetch_start("out", block_of(ctx_n)(me), out.at[me])

    def contract_back_step(i):
        cols = ds(i * 1024, 1024)
        df = (dot_nt(low[...], wc[cols, :]) * big_b[:, cols].astype(F32)).astype(BF16)
        big_b[:, cols] = df
        sum_expand[:, cols] += fold8(df.astype(F32))

    loop(ff // 1024, contract_back_step, ff // 1024)

    def expand_back_step(i):
        cols = ds(i * 256, 256)
        resid[:, cols] += dot_nt(big_b[...], we[cols, :])

    loop(width // 256, expand_back_step, width // 256)

    def norm1_step(i):
        part_rows = ds(i * 128, 128)
        dn = resid[part_rows, :]
        sums[s_attn] += fold8(dn)
        e = dn * vecs[gain1]
        xh = xh1[part_rows, :]
        r = rstd1[part_rows, :1]
        d = r * (e - jnp.mean(e, -1, keepdims=True) - xh * jnp.mean(e * xh, -1, keepdims=True))
        resid[part_rows, :] = d
        d_low = d.astype(BF16)
        low[part_rows, :] = d_low
        sums[s_output] += fold8(d_low.astype(F32))

    loop(rows // 128, norm1_step, 2)

    expand_rows = ff // width
    early = [s_ffn, s_contract, s_attn, s_output]

    partials, received = (red, red_late), (red_in, red_late_in)

    def send_partial(kind, slot, src, where):
        return pltpu.make_async_remote_copy(
            src_ref=partials[kind].at[src],
            dst_ref=received[kind].at[slot],
            send_sem=red_send.at[kind, slot],
            recv_sem=red_recv.at[kind, slot],
            device_id=where,
            device_id_type=MESH,
        )

    def round_copies(kind, which):
        if which == 0:
            return [send_partial(kind, j - 1, 0, {"seq": flip(me, j)}) for j in peers]
        first = len(peers) + sum(len(masks) for masks in rounds[: which - 1])
        return [
            send_partial(kind, first + i, which, {"dp": flip(dp, m)})
            for i, m in enumerate(rounds[which - 1])
        ]

    def reduce_start(kind, which=0):
        for copy in round_copies(kind, which):
            copy.start()

    def reduce_end(kind, which):
        for copy in round_copies(kind, which):
            copy.wait()
        first = len(peers) + sum(len(masks) for masks in rounds[: which - 1]) if which else 0
        count = len(peers) if which == 0 else len(rounds[which - 1])
        parts = [partials[kind][which]] + [received[kind][first + i] for i in range(count)]
        while len(parts) > 1:
            parts = [parts[i] + parts[i + 1] for i in range(0, len(parts), 2)]
        partials[kind][which + 1] = parts[0]
        if which < len(rounds):
            reduce_start(kind, which + 1)

    for i, which in enumerate(early):
        red[0, i : i + 1, :] = jnp.sum(sums[which], 0, keepdims=True)
    for i in range(expand_rows):
        red[0, 4 + i : 5 + i, :] = jnp.sum(
            sum_expand[:, i * width : (i + 1) * width], 0, keepdims=True
        )
    reduce_start(0)

    def ctx_back_step(i):
        feats = ds(i * 256, 256)
        v_t[feats, :] = dot_nt(wo[feats, :], low[...]).astype(BF16)

    loop(width // 256, ctx_back_step, width // 256)
    dq_n, dk_n, dv_n = (big_a.at[:, i * width : (i + 1) * width] for i in range(3))
    dscore_refs = tuple(cot_buf.at[:, i * rows : (i + 1) * rows] for i in range(2))
    turned_q, turned_k = (k_n.at[:LANES, i * rows : (i + 1) * rows] for i in range(2))

    def dscore(p, j):
        lanes = ds(p * LANES, LANES)
        feats = ds(p * LANES + HEAD * j, HEAD)
        d = v_t[feats, :].astype(F32) * recip[pl.ds(2 * p + j, 1), :]
        inner = jnp.sum(d * ctx_t[feats, :].astype(F32), 0, keepdims=True)
        d_low = d.astype(BF16)
        zeros = jnp.zeros((HEAD, rows), BF16)
        padded = jnp.concatenate([d_low, zeros] if j == 0 else [zeros, d_low], 0)
        dprobs = dot_nn(v_n[:, lanes], padded)
        dscore_refs[j][...] = (probs[2 * p + j].astype(F32) * (dprobs - inner)).astype(BF16)
        return padded

    def turn_back(p):
        lanes = ds(p * LANES, LANES)
        dq_low = turned_q[...].T
        dq_n[:, lanes] = dq_low
        dk_n[:, lanes] = turned_k[...].T
        sums[s_query, :, lanes] = fold8(dq_low.astype(F32))

    def attn_back_step(p):
        turn_back(lax.rem(p + pairs - 1, pairs))
        lanes = ds(p * LANES, LANES)
        dv = None
        for j in range(2):
            padded = dscore(p, j)
            term = dot_nn(probs[2 * p + j], padded.T)
            dv = term if dv is None else dv + term
        dv_low = dv.astype(BF16)
        dv_n[:, lanes] = dv_low
        sums[s_value, :, lanes] = fold8(dv_low.astype(F32))
        for j in range(2):
            feats, half = ds(p * LANES + HEAD * j, HEAD), slice(HEAD * j, HEAD * j + HEAD)
            dq = dot_nn(k_t[feats, :], dscore_refs[j][...]) * scale
            turned_q[half, :] = dq.astype(BF16)
            turned_k[half, :] = dot_nt(q_t[feats, :], dscore_refs[j][...]).astype(BF16)

    late = pairs - 2
    turned_q[...] = jnp.zeros_like(turned_q)
    turned_k[...] = jnp.zeros_like(turned_k)
    loop(late, attn_back_step, 2)
    reduce_end(0, 0)
    loop(2, lambda i: attn_back_step(late + i), 2)
    turn_back(pairs - 1)
    quarter = width // 4
    for i, which in enumerate((s_query, s_value)):
        for j in range(4):
            red_late[0, 4 * i + j : 4 * i + j + 1, :] = jnp.sum(
                sums[which, :, j * quarter : (j + 1) * quarter], 0, keepdims=True
            )
    reduce_start(1)

    def grad_step(base, cols):
        here = ds(base, pair)
        g = (
            resid[here, cols]
            + dot_nt(dq_n[here, :], wq[cols, :])
            + dot_nt(dk_n[here, :], wk[cols, :])
            + dot_nt(dv_n[here, :], wv[cols, :])
        )
        x_buf[here, cols] = g.astype(BF16)

    def grad_cols(cols):
        return lambda peer: x_buf.at[ds(peer * part, part), cols]

    def grad_home(cols):
        return lambda member: grad_in.at[member, :, cols]

    send_grad = [
        exchange(3 + i, grad_cols(cols), grad_home(cols)(me)) for i, cols in enumerate(grad_chunks)
    ]
    for hi in range(2, group, 2):
        base = flip(me, hi) - core
        for i, cols in enumerate(grad_chunks):
            grad_step(base * part, cols)
            for c in range(2):
                send_grad[i](base + c).start()
    reduce_end(1, 0)
    loop(width // 256, lambda i: grad_step((me - core) * part, ds(i * 256, 256)))
    for send in send_grad:
        send(flip(me, 1)).start()
    fetch_start("grad", x_buf.at[mine], grad_in.at[me])

    for which in range(1, len(rounds) + 1):
        for kind in range(2):
            reduce_end(kind, which)
    final = 1 + len(rounds)
    small_out[...] = red[final] * factor
    late_out[...] = red_late[final] * factor

    for peer in members:
        arrived(2, lambda member: out.at[member], peer)
        for i, cols in enumerate(grad_chunks):
            arrived(3 + i, grad_home(cols), peer)
    for send in send_x + [send_cot, send_out] + send_grad:
        for peer in members:
            send(peer).wait_send()
    fetch["out"].wait()
    fetch["grad"].wait()


def finish(
    early_out,
    early_grad,
    early_small,
    late_small,
    out,
    grad_in,
    g_bias_query,
    g_bias_value,
    g_bias_output,
    g_shift_attn,
    g_bias_expand,
    g_bias_contract,
    g_shift_ffn,
    sem_out,
):
    pairs = [
        (src.at[i], dst.at[i], n * early_out.shape[0] + i)
        for n, (src, dst) in enumerate(((early_out, out), (early_grad, grad_in)))
        for i in range(early_out.shape[0])
    ]
    puts = [pltpu.make_async_copy(src, dst, sem_out.at[n]) for src, dst, n in pairs]
    for put in puts:
        put.start()
    width = early_small.shape[-1]
    for i, ref in enumerate((g_shift_ffn, g_bias_contract, g_shift_attn, g_bias_output)):
        ref[...] = early_small[i : i + 1, :]
    for i in range(g_bias_expand.shape[1] // width):
        g_bias_expand[:, i * width : (i + 1) * width] = early_small[4 + i : 5 + i, :]
    for i, ref in enumerate((g_bias_query, g_bias_value)):
        for j in range(4):
            ref[:, j * width // 4 : (j + 1) * width // 4] = late_small[4 * i + j : 4 * i + j + 1, :]
    for put in puts:
        put.wait()


def local(mesh, *args):
    hidden_in, lengths = args[:2]
    group, dp_size = mesh.shape["seq"], mesh.shape["dp"]
    seqs, part, width = hidden_in.shape
    ff = args[7].shape[1]
    rows = part * group
    assert seqs == group
    assert group & (group - 1) == 0 and dp_size & (dp_size - 1) == 0
    factor = (rows * seqs // group * dp_size * group) ** (-0.5)
    rounds = dp_rounds(dp_size)
    slots = group - 1 + sum(len(masks) for masks in rounds)
    anywhere = pl.BlockSpec(memory_space=pl.ANY)
    in_specs = [anywhere] * len(args)
    in_specs[1] = pl.BlockSpec(memory_space=pltpu.SMEM)
    vmem = pl.BlockSpec(memory_space=pltpu.VMEM)
    operands = [a.reshape(1, -1) if a.ndim == 1 and i != 1 else a for i, a in enumerate(args)]
    row = jax.ShapeDtypeStruct((1, width), F32)
    outs = pl.pallas_call(
        functools.partial(kernel, group, dp_size, factor),
        out_shape=[pltpu.VMEM(hidden_in.shape, BF16)] * 2
        + [pltpu.VMEM((8, width), F32), pltpu.VMEM((8, width // 4), F32)],
        in_specs=in_specs,
        out_specs=[vmem] * 4,
        scratch_shapes=[
            pltpu.VMEM((width, width), BF16),
            pltpu.VMEM((width, width), BF16),
            pltpu.VMEM((width, width), BF16),
            pltpu.VMEM((width, width), BF16),
            pltpu.VMEM((width, ff), BF16),
            pltpu.VMEM((ff, width), BF16),
            pltpu.VMEM((8, 1, width), F32),
            pltpu.VMEM((1, ff), F32),
            pltpu.VMEM((rows, width), BF16),
            pltpu.VMEM((rows, width), BF16),
            pltpu.VMEM((width, rows), BF16),
            pltpu.VMEM((rows, width), BF16),
            pltpu.VMEM((width, rows), BF16),
            pltpu.VMEM((rows, width), BF16),
            pltpu.VMEM((width, rows), BF16),
            pltpu.VMEM((HEADS, rows, rows), BF16),
            pltpu.VMEM((HEADS, rows), F32),
            pltpu.VMEM((width, rows), BF16),
            pltpu.VMEM((rows, width), BF16),
            pltpu.VMEM((rows, width), F32),
            pltpu.VMEM((rows, LANES), F32),
            pltpu.VMEM((rows, width), BF16),
            pltpu.VMEM((rows, ff), BF16),
            pltpu.VMEM((rows, ff), BF16),
            pltpu.VMEM((rows, width), F32),
            pltpu.VMEM((rows, rows), F32),
            pltpu.VMEM((rows, rows), F32),
            pltpu.VMEM((1, rows), F32),
            pltpu.VMEM((1, rows), F32),
            pltpu.VMEM((2, rows, LANES), BF16),
            pltpu.VMEM((6, 8, width), F32),
            pltpu.VMEM((8, ff), F32),
            pltpu.VMEM((2 + len(rounds), 8, width), F32),
            pltpu.VMEM((slots, 8, width), F32),
            pltpu.VMEM((2 + len(rounds), 8, width // 4), F32),
            pltpu.VMEM((slots, 8, width // 4), F32),
            pltpu.SemaphoreType.DMA((24,)),
            pltpu.SemaphoreType.DMA((4 + len(column_chunks(width)), group)),
            pltpu.SemaphoreType.DMA((4 + len(column_chunks(width)), group)),
            pltpu.SemaphoreType.DMA((2, slots)),
            pltpu.SemaphoreType.DMA((2, slots)),
        ],
        compiler_params=pltpu.CompilerParams(
            collective_id=0, has_side_effects=True, vmem_limit_bytes=64700000
        ),
        name="layer",
    )(*operands)
    outs = [pltpu.with_memory_space_constraint(o, pltpu.VMEM) for o in outs]
    blocks = 2 * seqs
    outs = pl.pallas_call(
        finish,
        out_shape=[jax.ShapeDtypeStruct(hidden_in.shape, BF16)] * 2
        + [row] * 4
        + [jax.ShapeDtypeStruct((1, ff), F32), row, row],
        in_specs=[vmem] * 4,
        out_specs=[anywhere] * 2 + [vmem] * 7,
        scratch_shapes=[pltpu.SemaphoreType.DMA((blocks,))],
        compiler_params=pltpu.CompilerParams(vmem_limit_bytes=4 * 2**20),
        name="finish",
    )(*outs)
    return tuple(o.reshape(-1) if o.shape[0] == 1 else o for o in outs)


def solution(mesh):
    placed = (P("dp", "seq", None), P("dp")) + (P(),) * 15 + (P("dp", "seq", None),)
    return jax.shard_map(
        functools.partial(local, mesh),
        mesh=mesh,
        in_specs=placed,
        out_specs=(P("dp", "seq", None), P("dp", "seq", None), P(), P(), P(), P(), P(), P(), P()),
        check_vma=False,
    )
```

```python
import functools
import math

import jax
import jax.numpy as jnp
from jax import lax
from jax.experimental import pallas as pl
from jax.experimental.pallas import tpu as pltpu
from jax.sharding import PartitionSpec as P

HEADS = 16
HEAD = 64
NEG = -1e30
EPSILON = 1e-12
LANES = 128
MESH = pl.DeviceIdType.MESH
F32 = jnp.float32
BF16 = jnp.bfloat16


def dot_nn(left, right):
    return jnp.dot(left, right, preferred_element_type=F32)


def dot_nt(left, right):
    return lax.dot_general(left, right, (((1,), (1,)), ((), ())), preferred_element_type=F32)


def flip(index, mask):
    bit = 1
    while bit <= mask:
        if mask & bit:
            index = index + bit - 2 * bit * ((index // bit) % 2)
        bit *= 2
    return index


def ds(start, size):
    return pl.ds(start if isinstance(start, int) else pl.multiple_of(start, size), size)


def dp_rounds(size):
    rounds, low = [], 1
    while low < size:
        high = min(low * 8, size)
        rounds.append([m * low for m in range(1, high // low)])
        low = high
    return rounds


def column_chunks(width):
    edges = [0, width // 2, width]
    return [slice(a, b) for a, b in zip(edges, edges[1:])]


def fold8(value):
    rows, width = value.shape
    return jnp.sum(value.reshape(rows // 8, 8, width), 0)


def loop(count, body, unroll=1):
    def step(index, carry):
        body(index)
        return carry

    lax.fori_loop(0, count, step, 0, unroll=unroll)


def kernel(
    group,
    dp_size,
    factor,
    hidden_in,
    lengths,
    w_query,
    w_key,
    w_value,
    w_output,
    gain_attn,
    w_expand,
    w_contract,
    gain_ffn,
    bias_query,
    bias_value,
    bias_output,
    shift_attn,
    bias_expand,
    bias_contract,
    shift_ffn,
    cotangent,
    out,
    grad_in,
    small_out,
    late_out,
    wq,
    wk,
    wv,
    wo,
    we,
    wc,
    vecs,
    vec_expand,
    x_buf,
    cot_buf,
    q_t,
    k_n,
    k_t,
    v_n,
    v_t,
    probs,
    recip,
    ctx_t,
    ctx_n,
    xh1,
    rstd1,
    low,
    big_a,
    big_b,
    resid,
    s_a,
    s_b,
    top_a,
    top_b,
    key_bias,
    sums,
    sum_expand,
    red,
    red_in,
    red_late,
    red_late_in,
    local_sem,
    send_sem,
    recv_sem,
    red_send,
    red_recv,
):
    me = lax.axis_index("seq")
    dp = lax.axis_index("dp")
    part = hidden_in.shape[1]
    rows, width = x_buf.shape
    ff = we.shape[1]
    grad_chunks = column_chunks(width)
    peers = list(range(1, group))
    members = [flip(me, j) for j in peers]
    core = me % 2
    by_core = [flip(me, 1)] + [
        flip(me, hi) - core + c for c in range(2) for hi in range(2, group, 2)
    ]
    rounds = dp_rounds(dp_size)
    dp_masks = [m for masks in rounds for m in masks]

    small = (
        bias_query,
        bias_value,
        bias_output,
        gain_attn,
        shift_attn,
        bias_contract,
        gain_ffn,
        shift_ffn,
    )
    b_q, b_v, b_o, gain1, shift1, b_c, gain2, shift2 = range(8)
    fetch = {}

    def fetch_start(name, src, dst):
        fetch[name] = pltpu.make_async_copy(src, dst, local_sem.at[len(fetch)])
        fetch[name].start()

    mine = ds(me * part, part)
    fetch_start("x", hidden_in.at[me], x_buf.at[mine])
    fetch_start("wq", w_query, wq)
    fetch_start("wk", w_key, wk)
    fetch_start("wv", w_value, wv)

    barrier = pltpu.get_barrier_semaphore()
    for j in peers:
        pl.semaphore_signal(barrier, inc=1, device_id={"seq": flip(me, j)}, device_id_type=MESH)
    for m in dp_masks:
        pl.semaphore_signal(barrier, inc=1, device_id={"dp": flip(dp, m)}, device_id_type=MESH)
    pl.semaphore_wait(barrier, len(peers) + len(dp_masks))

    def exchange(kind, src_of, dst):
        def send(peer):
            return pltpu.make_async_remote_copy(
                src_ref=src_of(peer),
                dst_ref=dst,
                send_sem=send_sem.at[kind, peer],
                recv_sem=recv_sem.at[kind, me],
                device_id={"seq": peer},
                device_id_type=MESH,
            )

        return send

    def block_of(buf):
        return lambda peer: buf.at[ds(peer * part, part)]

    def arrived(kind, dst_of, peer):
        pltpu.make_async_remote_copy(
            src_ref=dst_of(peer),
            dst_ref=dst_of(peer),
            send_sem=send_sem.at[kind, peer],
            recv_sem=recv_sem.at[kind, peer],
            device_id={"seq": peer},
            device_id_type=MESH,
        ).wait_recv()

    halves = [slice(0, width // 2), slice(width // 2, width)]
    x_kinds = (0, 3 + len(grad_chunks))
    send_x = [
        exchange(kind, lambda peer, half=half: hidden_in.at[peer, :, half], x_buf.at[mine, half])
        for kind, half in zip(x_kinds, halves)
    ]
    for send in send_x:
        send(flip(me, 1)).start()
    for c in range(2):
        for send in send_x:
            for hi in range(2, group, 2):
                send(flip(me, hi) - core + c).start()
    for i, vec in enumerate(small):
        fetch_start(("v", i), vec, vecs.at[i])
    fetch_start("be", bias_expand, vec_expand)
    fetch_start("wo", w_output, wo)
    fetch_start("we", w_expand, we)
    send_cot = exchange(1, lambda peer: cotangent.at[peer], cot_buf.at[mine])

    def cot_start(which):
        @pl.when(core == which)
        def _():
            for peer in by_core:
                send_cot(peer).start()

    fetch_start("cot", cotangent.at[me], cot_buf.at[mine])
    fetch_start("wc", w_contract, wc)

    sums[...] = jnp.zeros_like(sums)
    sum_expand[...] = jnp.zeros_like(sum_expand)
    s_ffn, s_contract, s_attn, s_output, s_query, s_value = range(6)

    scale = HEAD ** (-0.5)
    pair = 2 * part

    def qkv(base, unroll, half=None, kept=None):
        here = ds(base, pair)
        xs = x_buf[here, :] if half is None else x_buf[here, half]

        def step(i):
            cols = ds(i * 256, 256)
            q, k, v = (
                dot_nn(xs, w[:, cols] if half is None else w[half, cols]) for w in (wq, wk, wv)
            )
            if kept is not None:
                q, k, v = (p + ref[:, cols] for p, ref in zip((q, k, v), kept))
            q = ((q + vecs[b_q, :, cols]) * scale).astype(BF16)
            q_t[cols, here] = q.T
            k = k.astype(BF16)
            k_n[here, cols] = k
            k_t[cols, here] = k.T
            v = (v + vecs[b_v, :, cols]).astype(BF16)
            v_n[here, cols] = v
            v_t[cols, here] = v.T

        loop(width // 256, step, unroll)

    def qkv_first(base, half, kept):
        xs = x_buf[ds(base, pair), half]

        def step(i):
            cols = ds(i * 256, 256)
            for w, ref in zip((wq, wk, wv), kept):
                ref[:, cols] = dot_nn(xs, w[half, cols])

        loop(width // 256, step)

    length = lengths[me]
    row = lax.broadcasted_iota(jnp.int32, (rows, LANES), 0)
    lane = lax.broadcasted_iota(jnp.int32, (rows, LANES), 1)
    for j in range(2):
        key_bias[j] = jnp.where((row >= length) & (lane == HEAD * (1 - j)), NEG, 0.0).astype(BF16)

    for i in range(len(small)):
        fetch["v", i].wait()
    fetch["x"].wait()
    fetch["wq"].wait()
    fetch["wk"].wait()
    fetch["wv"].wait()
    def x_half(half):
        return lambda peer: x_buf.at[ds(peer * part, part), half]

    for kind, half in zip(x_kinds, halves):
        arrived(kind, x_half(half), flip(me, 1))
    qkv((me - core) * part, 1)
    kept = (resid.at[:pair], resid.at[pair : 2 * pair], xh1.at[:pair])
    for hi in range(2, group, 2):
        base = flip(me, hi) - core
        for c in range(2):
            arrived(x_kinds[0], x_half(halves[0]), base + c)
        qkv_first(base * part, halves[0], kept)
        for c in range(2):
            arrived(x_kinds[1], x_half(halves[1]), base + c)
        if hi == group - 2:
            cot_start(1)
        qkv(base * part, width // 256, halves[1], kept)

    score_refs, top_refs = (s_a, s_b), (top_a, top_b)

    def score(p, j):
        lanes = ds(p * LANES, LANES)
        half = lax.broadcasted_iota(jnp.int32, (rows, LANES), 1) < HEAD
        k_one = jnp.where(half if j == 0 else ~half, k_n[:, lanes], key_bias[j])
        q_one = q_t[ds(p * LANES + HEAD * j, HEAD), :]
        pad = [jnp.ones((16, rows), BF16), jnp.zeros((HEAD - 16, rows), BF16)]
        q_one = jnp.concatenate([q_one] + pad if j == 0 else pad + [q_one], 0)
        for c in range(0, rows, 256):
            cols = slice(c, c + 256)
            block = dot_nn(k_one, q_one[:, cols])
            score_refs[j][:, cols] = block
            top_refs[j][:, cols] = jnp.max(block, 0, keepdims=True)

    def exponential(h, j):
        for c in range(0, rows, 256):
            cols = slice(c, c + 256)
            probs[h, :, cols] = jnp.exp(score_refs[j][:, cols] - top_refs[j][:, cols]).astype(BF16)

    def weigh(h):
        feats = ds(h * HEAD, HEAD)
        o = dot_nn(jnp.concatenate([v_t[feats, :], jnp.ones((16, rows), BF16)], 0), probs[h])
        inv = 1.0 / o[HEAD : HEAD + 1]
        recip[pl.ds(h, 1), :] = inv
        ctx_t[feats, :] = (o[:HEAD] * inv).astype(BF16)

    def turn(p):
        lanes = ds(p * LANES, LANES)
        ctx_n[:, lanes] = ctx_t[lanes, :].T

    pairs = HEADS // 2
    for j in range(2):
        score(0, j)

    def attn_step(p, last=False):
        for j in range(2):
            exponential(2 * p + j, j)
        if not last:
            for j in range(2):
                score(p + 1, j)
        for j in range(2):
            weigh(2 * p + j)
        turn(p)

    loop(pairs - 1, attn_step, pairs - 1)
    attn_step(pairs - 1, last=True)

    cot_start(0)

    fetch["wo"].wait()

    def out_proj_step(i):
        part_rows = ds(i * 256, 256)
        ao = dot_nn(ctx_n[part_rows, :], wo[...]) + vecs[b_o]
        h = x_buf[part_rows, :].astype(F32) + ao
        center = h - jnp.mean(h, -1, keepdims=True)
        r = lax.rsqrt(jnp.mean(center * center, -1, keepdims=True) + EPSILON)
        xh = center * r
        xh1[part_rows, :] = xh
        rstd1[part_rows, :] = jnp.broadcast_to(r, (256, LANES))
        low[part_rows, :] = (xh * vecs[gain1] + vecs[shift1]).astype(BF16)

    loop(rows // 256, out_proj_step, rows // 256)

    fetch["we"].wait()
    fetch["be"].wait()

    def expand(i):
        cols = ds(i * 512, 512)
        s_a[...] = dot_nn(low[...], we[:, cols]) + vec_expand[:, cols]

    def gelu(i):
        cols = ds(i * 512, 512)
        f = s_a[...]
        t = f * (0.5**0.5)
        phi = 0.5 * lax.erf(t) + 0.5
        big_a[:, cols] = (f * phi).astype(BF16)
        bell = jnp.exp2(t * t * (-1.0 / math.log(2.0)))
        big_b[:, cols] = (phi + t * (1.0 / math.pi) ** 0.5 * bell).astype(BF16)

    expand(0)

    def expand_step(i):
        gelu(i)
        expand(i + 1)

    loop(ff // 512 - 1, expand_step, ff // 512 - 1)
    gelu(ff // 512 - 1)
    fetch["wc"].wait()

    def contract_step(i):
        cols = ds(i * 256, 256)
        n1 = xh1[:, cols] * vecs[gain1, :, cols] + vecs[shift1, :, cols]
        resid[:, cols] = n1 + dot_nn(big_a[...], wc[:, cols]) + vecs[b_c, :, cols]

    loop(width // 256, contract_step, width // 256)

    fetch["cot"].wait()
    for peer in members:
        arrived(1, block_of(cot_buf), peer)

    def norm2_step(i):
        part_rows = ds(i * 128, 128)
        h = resid[part_rows, :]
        center = h - jnp.mean(h, -1, keepdims=True)
        r = lax.rsqrt(jnp.mean(center * center, -1, keepdims=True) + EPSILON)
        xh = center * r
        ctx_n[part_rows, :] = (xh * vecs[gain2] + vecs[shift2]).astype(BF16)
        dy = cot_buf[part_rows, :].astype(F32)
        sums[s_ffn] += fold8(dy)
        e = dy * vecs[gain2]
        d = r * (e - jnp.mean(e, -1, keepdims=True) - xh * jnp.mean(e * xh, -1, keepdims=True))
        resid[part_rows, :] = d
        d_low = d.astype(BF16)
        low[part_rows, :] = d_low
        sums[s_contract] += fold8(d_low.astype(F32))

    loop(rows // 128, norm2_step, 2)

    send_out = exchange(2, block_of(ctx_n), out.at[me])
    for peer in by_core:
        send_out(peer).start()
    fetch_start("out", block_of(ctx_n)(me), out.at[me])

    def contract_back_step(i):
        cols = ds(i * 1024, 1024)
        df = (dot_nt(low[...], wc[cols, :]) * big_b[:, cols].astype(F32)).astype(BF16)
        big_b[:, cols] = df
        sum_expand[:, cols] += fold8(df.astype(F32))

    loop(ff // 1024, contract_back_step, ff // 1024)

    def expand_back_step(i):
        cols = ds(i * 256, 256)
        resid[:, cols] += dot_nt(big_b[...], we[cols, :])

    loop(width // 256, expand_back_step, width // 256)

    def norm1_step(i):
        part_rows = ds(i * 128, 128)
        dn = resid[part_rows, :]
        sums[s_attn] += fold8(dn)
        e = dn * vecs[gain1]
        xh = xh1[part_rows, :]
        r = rstd1[part_rows, :1]
        d = r * (e - jnp.mean(e, -1, keepdims=True) - xh * jnp.mean(e * xh, -1, keepdims=True))
        resid[part_rows, :] = d
        d_low = d.astype(BF16)
        low[part_rows, :] = d_low
        sums[s_output] += fold8(d_low.astype(F32))

    loop(rows // 128, norm1_step, 2)

    expand_rows = ff // width
    early = [s_ffn, s_contract, s_attn, s_output]

    partials, received = (red, red_late), (red_in, red_late_in)

    def send_partial(kind, slot, src, where):
        return pltpu.make_async_remote_copy(
            src_ref=partials[kind].at[src],
            dst_ref=received[kind].at[slot],
            send_sem=red_send.at[kind, slot],
            recv_sem=red_recv.at[kind, slot],
            device_id=where,
            device_id_type=MESH,
        )

    def round_copies(kind, which):
        if which == 0:
            return [send_partial(kind, j - 1, 0, {"seq": flip(me, j)}) for j in peers]
        first = len(peers) + sum(len(masks) for masks in rounds[: which - 1])
        return [
            send_partial(kind, first + i, which, {"dp": flip(dp, m)})
            for i, m in enumerate(rounds[which - 1])
        ]

    def reduce_start(kind, which=0):
        for copy in round_copies(kind, which):
            copy.start()

    def reduce_end(kind, which):
        for copy in round_copies(kind, which):
            copy.wait()
        first = len(peers) + sum(len(masks) for masks in rounds[: which - 1]) if which else 0
        count = len(peers) if which == 0 else len(rounds[which - 1])
        parts = [partials[kind][which]] + [received[kind][first + i] for i in range(count)]
        while len(parts) > 1:
            parts = [parts[i] + parts[i + 1] for i in range(0, len(parts), 2)]
        partials[kind][which + 1] = parts[0]
        if which < len(rounds):
            reduce_start(kind, which + 1)

    for i, which in enumerate(early):
        red[0, i : i + 1, :] = jnp.sum(sums[which], 0, keepdims=True)
    for i in range(expand_rows):
        red[0, 4 + i : 5 + i, :] = jnp.sum(
            sum_expand[:, i * width : (i + 1) * width], 0, keepdims=True
        )
    reduce_start(0)

    def ctx_back_step(i):
        feats = ds(i * 256, 256)
        v_t[feats, :] = dot_nt(wo[feats, :], low[...]).astype(BF16)

    loop(width // 256, ctx_back_step, width // 256)
    dq_n, dk_n, dv_n = (big_a.at[:, i * width : (i + 1) * width] for i in range(3))
    dscore_refs = tuple(cot_buf.at[:, i * rows : (i + 1) * rows] for i in range(2))
    turned_q, turned_k = (k_n.at[:LANES, i * rows : (i + 1) * rows] for i in range(2))

    def dscore(p, j):
        lanes = ds(p * LANES, LANES)
        feats = ds(p * LANES + HEAD * j, HEAD)
        d = v_t[feats, :].astype(F32) * recip[pl.ds(2 * p + j, 1), :]
        inner = jnp.sum(d * ctx_t[feats, :].astype(F32), 0, keepdims=True)
        d_low = d.astype(BF16)
        zeros = jnp.zeros((HEAD, rows), BF16)
        padded = jnp.concatenate([d_low, zeros] if j == 0 else [zeros, d_low], 0)
        dprobs = dot_nn(v_n[:, lanes], padded)
        dscore_refs[j][...] = (probs[2 * p + j].astype(F32) * (dprobs - inner)).astype(BF16)
        return padded

    def turn_back(p):
        lanes = ds(p * LANES, LANES)
        dq_low = turned_q[...].T
        dq_n[:, lanes] = dq_low
        dk_n[:, lanes] = turned_k[...].T
        sums[s_query, :, lanes] = fold8(dq_low.astype(F32))

    def attn_back_step(p):
        turn_back(lax.rem(p + pairs - 1, pairs))
        lanes = ds(p * LANES, LANES)
        dv = None
        for j in range(2):
            padded = dscore(p, j)
            term = dot_nn(probs[2 * p + j], padded.T)
            dv = term if dv is None else dv + term
        dv_low = dv.astype(BF16)
        dv_n[:, lanes] = dv_low
        sums[s_value, :, lanes] = fold8(dv_low.astype(F32))
        for j in range(2):
            feats, half = ds(p * LANES + HEAD * j, HEAD), slice(HEAD * j, HEAD * j + HEAD)
            dq = dot_nn(k_t[feats, :], dscore_refs[j][...]) * scale
            turned_q[half, :] = dq.astype(BF16)
            turned_k[half, :] = dot_nt(q_t[feats, :], dscore_refs[j][...]).astype(BF16)

    late = pairs - 2
    turned_q[...] = jnp.zeros_like(turned_q)
    turned_k[...] = jnp.zeros_like(turned_k)
    loop(late, attn_back_step, 2)
    reduce_end(0, 0)
    loop(2, lambda i: attn_back_step(late + i), 2)
    turn_back(pairs - 1)
    quarter = width // 4
    for i, which in enumerate((s_query, s_value)):
        for j in range(4):
            red_late[0, 4 * i + j : 4 * i + j + 1, :] = jnp.sum(
                sums[which, :, j * quarter : (j + 1) * quarter], 0, keepdims=True
            )
    reduce_start(1)

    def grad_step(base, cols):
        here = ds(base, pair)
        g = (
            resid[here, cols]
            + dot_nt(dq_n[here, :], wq[cols, :])
            + dot_nt(dk_n[here, :], wk[cols, :])
            + dot_nt(dv_n[here, :], wv[cols, :])
        )
        x_buf[here, cols] = g.astype(BF16)

    def grad_cols(cols):
        return lambda peer: x_buf.at[ds(peer * part, part), cols]

    def grad_home(cols):
        return lambda member: grad_in.at[member, :, cols]

    send_grad = [
        exchange(3 + i, grad_cols(cols), grad_home(cols)(me)) for i, cols in enumerate(grad_chunks)
    ]
    for hi in range(2, group, 2):
        base = flip(me, hi) - core
        for i, cols in enumerate(grad_chunks):
            grad_step(base * part, cols)
            for c in range(2):
                send_grad[i](base + c).start()
    reduce_end(1, 0)
    loop(width // 256, lambda i: grad_step((me - core) * part, ds(i * 256, 256)))
    for send in send_grad:
        send(flip(me, 1)).start()
    fetch_start("grad", x_buf.at[mine], grad_in.at[me])

    for which in range(1, len(rounds) + 1):
        for kind in range(2):
            reduce_end(kind, which)
    final = 1 + len(rounds)
    small_out[...] = red[final] * factor
    late_out[...] = red_late[final] * factor

    for peer in members:
        arrived(2, lambda member: out.at[member], peer)
        for i, cols in enumerate(grad_chunks):
            arrived(3 + i, grad_home(cols), peer)
    for send in send_x + [send_cot, send_out] + send_grad:
        for peer in members:
            send(peer).wait_send()
    fetch["out"].wait()
    fetch["grad"].wait()


def finish(
    early_out,
    early_grad,
    early_small,
    late_small,
    out,
    grad_in,
    g_bias_query,
    g_bias_value,
    g_bias_output,
    g_shift_attn,
    g_bias_expand,
    g_bias_contract,
    g_shift_ffn,
    row_buf,
    expand_buf,
    sem_out,
    sem_small,
):
    puts = [
        pltpu.make_async_copy(src.at[i], dst.at[i], sem_out.at[n * early_out.shape[0] + i])
        for n, (src, dst) in enumerate(((early_out, out), (early_grad, grad_in)))
        for i in range(early_out.shape[0])
    ]
    for put in puts:
        put.start()
    width = early_small.shape[-1]
    rows_out = (g_shift_ffn, g_bias_contract, g_shift_attn, g_bias_output)
    late_out = (g_bias_query, g_bias_value)
    for i in range(len(rows_out)):
        row_buf[i] = early_small[i : i + 1, :]
    for i in range(len(late_out)):
        for j in range(4):
            cols = slice(j * width // 4, (j + 1) * width // 4)
            row_buf[len(rows_out) + i, :, cols] = late_small[4 * i + j : 4 * i + j + 1, :]
    for i in range(g_bias_expand.shape[1] // width):
        expand_buf[:, i * width : (i + 1) * width] = early_small[4 + i : 5 + i, :]
    moves = [
        pltpu.make_async_copy(row_buf.at[i], ref, sem_small.at[i])
        for i, ref in enumerate(rows_out + late_out)
    ]
    moves.append(pltpu.make_async_copy(expand_buf, g_bias_expand, sem_small.at[len(moves)]))
    for move in moves:
        move.start()
    for move in moves + puts:
        move.wait()


def local(mesh, *args):
    hidden_in, lengths = args[:2]
    group, dp_size = mesh.shape["seq"], mesh.shape["dp"]
    seqs, part, width = hidden_in.shape
    ff = args[7].shape[1]
    rows = part * group
    assert seqs == group
    assert group & (group - 1) == 0 and dp_size & (dp_size - 1) == 0
    factor = (rows * seqs // group * dp_size * group) ** (-0.5)
    rounds = dp_rounds(dp_size)
    slots = group - 1 + sum(len(masks) for masks in rounds)
    anywhere = pl.BlockSpec(memory_space=pl.ANY)
    in_specs = [anywhere] * len(args)
    in_specs[1] = pl.BlockSpec(memory_space=pltpu.SMEM)
    vmem = pl.BlockSpec(memory_space=pltpu.VMEM)
    operands = [a.reshape(1, -1) if a.ndim == 1 and i != 1 else a for i, a in enumerate(args)]
    row = jax.ShapeDtypeStruct((1, width), F32)
    outs = pl.pallas_call(
        functools.partial(kernel, group, dp_size, factor),
        out_shape=[pltpu.VMEM(hidden_in.shape, BF16)] * 2
        + [pltpu.VMEM((8, width), F32), pltpu.VMEM((8, width // 4), F32)],
        in_specs=in_specs,
        out_specs=[vmem] * 4,
        scratch_shapes=[
            pltpu.VMEM((width, width), BF16),
            pltpu.VMEM((width, width), BF16),
            pltpu.VMEM((width, width), BF16),
            pltpu.VMEM((width, width), BF16),
            pltpu.VMEM((width, ff), BF16),
            pltpu.VMEM((ff, width), BF16),
            pltpu.VMEM((8, 1, width), F32),
            pltpu.VMEM((1, ff), F32),
            pltpu.VMEM((rows, width), BF16),
            pltpu.VMEM((rows, width), BF16),
            pltpu.VMEM((width, rows), BF16),
            pltpu.VMEM((rows, width), BF16),
            pltpu.VMEM((width, rows), BF16),
            pltpu.VMEM((rows, width), BF16),
            pltpu.VMEM((width, rows), BF16),
            pltpu.VMEM((HEADS, rows, rows), BF16),
            pltpu.VMEM((HEADS, rows), F32),
            pltpu.VMEM((width, rows), BF16),
            pltpu.VMEM((rows, width), BF16),
            pltpu.VMEM((rows, width), F32),
            pltpu.VMEM((rows, LANES), F32),
            pltpu.VMEM((rows, width), BF16),
            pltpu.VMEM((rows, ff), BF16),
            pltpu.VMEM((rows, ff), BF16),
            pltpu.VMEM((rows, width), F32),
            pltpu.VMEM((rows, rows), F32),
            pltpu.VMEM((rows, rows), F32),
            pltpu.VMEM((1, rows), F32),
            pltpu.VMEM((1, rows), F32),
            pltpu.VMEM((2, rows, LANES), BF16),
            pltpu.VMEM((6, 8, width), F32),
            pltpu.VMEM((8, ff), F32),
            pltpu.VMEM((2 + len(rounds), 8, width), F32),
            pltpu.VMEM((slots, 8, width), F32),
            pltpu.VMEM((2 + len(rounds), 8, width // 4), F32),
            pltpu.VMEM((slots, 8, width // 4), F32),
            pltpu.SemaphoreType.DMA((24,)),
            pltpu.SemaphoreType.DMA((4 + len(column_chunks(width)), group)),
            pltpu.SemaphoreType.DMA((4 + len(column_chunks(width)), group)),
            pltpu.SemaphoreType.DMA((2, slots)),
            pltpu.SemaphoreType.DMA((2, slots)),
        ],
        compiler_params=pltpu.CompilerParams(
            collective_id=0, has_side_effects=True, vmem_limit_bytes=64700000
        ),
        name="layer",
    )(*operands)
    outs = [pltpu.with_memory_space_constraint(o, pltpu.VMEM) for o in outs]
    blocks = 2 * seqs
    outs = pl.pallas_call(
        finish,
        out_shape=[jax.ShapeDtypeStruct(hidden_in.shape, BF16)] * 2
        + [row] * 4
        + [jax.ShapeDtypeStruct((1, ff), F32), row, row],
        in_specs=[vmem] * 4,
        out_specs=[anywhere] * 9,
        scratch_shapes=[
            pltpu.VMEM((6, 1, width), F32),
            pltpu.VMEM((1, ff), F32),
            pltpu.SemaphoreType.DMA((blocks,)),
            pltpu.SemaphoreType.DMA((7,)),
        ],
        compiler_params=pltpu.CompilerParams(vmem_limit_bytes=4 * 2**20),
        name="finish",
    )(*outs)
    return tuple(o.reshape(-1) if o.shape[0] == 1 else o for o in outs)


def solution(mesh):
    placed = (P("dp", "seq", None), P("dp")) + (P(),) * 15 + (P("dp", "seq", None),)
    return jax.shard_map(
        functools.partial(local, mesh),
        mesh=mesh,
        in_specs=placed,
        out_specs=(P("dp", "seq", None), P("dp", "seq", None), P(), P(), P(), P(), P(), P(), P()),
        check_vma=False,
    )
```

```python
import functools
import math

import jax
import jax.numpy as jnp
from jax import lax
from jax.experimental import pallas as pl
from jax.experimental.pallas import tpu as pltpu
from jax.sharding import PartitionSpec as P

HEADS = 16
HEAD = 64
NEG = -1e30
EPSILON = 1e-12
LANES = 128
MESH = pl.DeviceIdType.MESH
F32 = jnp.float32
BF16 = jnp.bfloat16


def dot_nn(left, right):
    return jnp.dot(left, right, preferred_element_type=F32)


def dot_nt(left, right):
    return lax.dot_general(left, right, (((1,), (1,)), ((), ())), preferred_element_type=F32)


def flip(index, mask):
    bit = 1
    while bit <= mask:
        if mask & bit:
            index = index + bit - 2 * bit * ((index // bit) % 2)
        bit *= 2
    return index


def ds(start, size):
    return pl.ds(start if isinstance(start, int) else pl.multiple_of(start, size), size)


def dp_rounds(size):
    rounds, low = [], 1
    while low < size:
        high = min(low * 8, size)
        rounds.append([m * low for m in range(1, high // low)])
        low = high
    return rounds


def column_chunks(width):
    edges = [0, width // 2, width]
    return [slice(a, b) for a, b in zip(edges, edges[1:])]


def fold8(value):
    rows, width = value.shape
    return jnp.sum(value.reshape(rows // 8, 8, width), 0)


def loop(count, body, unroll=1):
    def step(index, carry):
        body(index)
        return carry

    lax.fori_loop(0, count, step, 0, unroll=unroll)


def kernel(
    group,
    dp_size,
    factor,
    hidden_in,
    lengths,
    w_query,
    w_key,
    w_value,
    w_output,
    gain_attn,
    w_expand,
    w_contract,
    gain_ffn,
    bias_query,
    bias_value,
    bias_output,
    shift_attn,
    bias_expand,
    bias_contract,
    shift_ffn,
    cotangent,
    out,
    grad_in,
    small_out,
    late_out,
    wq,
    wk,
    wv,
    wo,
    we,
    wc,
    vecs,
    vec_expand,
    x_buf,
    cot_buf,
    q_t,
    k_n,
    k_t,
    v_n,
    v_t,
    probs,
    recip,
    ctx_t,
    ctx_n,
    xh1,
    rstd1,
    low,
    big_a,
    big_b,
    resid,
    s_a,
    s_b,
    top_a,
    top_b,
    key_bias,
    sums,
    sum_expand,
    red,
    red_in,
    red_late,
    red_late_in,
    local_sem,
    send_sem,
    recv_sem,
    red_send,
    red_recv,
):
    me = lax.axis_index("seq")
    dp = lax.axis_index("dp")
    part = hidden_in.shape[1]
    rows, width = x_buf.shape
    ff = we.shape[1]
    grad_chunks = column_chunks(width)
    peers = list(range(1, group))
    members = [flip(me, j) for j in peers]
    core = me % 2
    by_core = [flip(me, 1)] + [
        flip(me, hi) - core + c for c in range(2) for hi in range(2, group, 2)
    ]
    rounds = dp_rounds(dp_size)
    dp_masks = [m for masks in rounds for m in masks]

    small = (
        bias_query,
        bias_value,
        bias_output,
        gain_attn,
        shift_attn,
        bias_contract,
        gain_ffn,
        shift_ffn,
    )
    b_q, b_v, b_o, gain1, shift1, b_c, gain2, shift2 = range(8)
    fetch = {}

    def fetch_start(name, src, dst):
        fetch[name] = pltpu.make_async_copy(src, dst, local_sem.at[len(fetch)])
        fetch[name].start()

    mine = ds(me * part, part)
    fetch_start("x", hidden_in.at[me], x_buf.at[mine])
    fetch_start("wq", w_query, wq)
    fetch_start("wk", w_key, wk)
    fetch_start("wv", w_value, wv)

    barrier = pltpu.get_barrier_semaphore()
    for j in peers:
        pl.semaphore_signal(barrier, inc=1, device_id={"seq": flip(me, j)}, device_id_type=MESH)
    for m in dp_masks:
        pl.semaphore_signal(barrier, inc=1, device_id={"dp": flip(dp, m)}, device_id_type=MESH)
    pl.semaphore_wait(barrier, len(peers) + len(dp_masks))

    def exchange(kind, src_of, dst):
        def send(peer):
            return pltpu.make_async_remote_copy(
                src_ref=src_of(peer),
                dst_ref=dst,
                send_sem=send_sem.at[kind, peer],
                recv_sem=recv_sem.at[kind, me],
                device_id={"seq": peer},
                device_id_type=MESH,
            )

        return send

    def block_of(buf):
        return lambda peer: buf.at[ds(peer * part, part)]

    def arrived(kind, dst_of, peer):
        pltpu.make_async_remote_copy(
            src_ref=dst_of(peer),
            dst_ref=dst_of(peer),
            send_sem=send_sem.at[kind, peer],
            recv_sem=recv_sem.at[kind, peer],
            device_id={"seq": peer},
            device_id_type=MESH,
        ).wait_recv()

    halves = [slice(0, width // 2), slice(width // 2, width)]
    x_kinds = (0, 3 + len(grad_chunks))
    send_x = [
        exchange(kind, lambda peer, half=half: hidden_in.at[peer, :, half], x_buf.at[mine, half])
        for kind, half in zip(x_kinds, halves)
    ]
    for send in send_x:
        send(flip(me, 1)).start()
    for c in range(2):
        for send in send_x:
            for hi in range(2, group, 2):
                send(flip(me, hi) - core + c).start()
    for i, vec in enumerate(small):
        fetch_start(("v", i), vec, vecs.at[i])
    fetch_start("be", bias_expand, vec_expand)
    fetch_start("wo", w_output, wo)
    fetch_start("we", w_expand, we)
    send_cot = exchange(1, lambda peer: cotangent.at[peer], cot_buf.at[mine])

    def cot_start(which):
        @pl.when(core == which)
        def _():
            for peer in by_core:
                send_cot(peer).start()

    fetch_start("cot", cotangent.at[me], cot_buf.at[mine])
    fetch_start("wc", w_contract, wc)

    sums[...] = jnp.zeros_like(sums)
    sum_expand[...] = jnp.zeros_like(sum_expand)
    s_ffn, s_contract, s_attn, s_output, s_query, s_value = range(6)

    scale = HEAD ** (-0.5)
    pair = 2 * part

    def qkv(base, unroll, half=None, kept=None):
        here = ds(base, pair)
        xs = x_buf[here, :] if half is None else x_buf[here, half]

        def step(i):
            cols = ds(i * 256, 256)
            q, k, v = (
                dot_nn(xs, w[:, cols] if half is None else w[half, cols]) for w in (wq, wk, wv)
            )
            if kept is not None:
                q, k, v = (p + ref[:, cols] for p, ref in zip((q, k, v), kept))
            q = ((q + vecs[b_q, :, cols]) * scale).astype(BF16)
            q_t[cols, here] = q.T
            k = k.astype(BF16)
            k_n[here, cols] = k
            k_t[cols, here] = k.T
            v = (v + vecs[b_v, :, cols]).astype(BF16)
            v_n[here, cols] = v
            v_t[cols, here] = v.T

        loop(width // 256, step, unroll)

    def qkv_first(base, half, kept):
        xs = x_buf[ds(base, pair), half]

        def step(i):
            cols = ds(i * 256, 256)
            for w, ref in zip((wq, wk, wv), kept):
                ref[:, cols] = dot_nn(xs, w[half, cols])

        loop(width // 256, step)

    length = lengths[me]
    row = lax.broadcasted_iota(jnp.int32, (rows, LANES), 0)
    lane = lax.broadcasted_iota(jnp.int32, (rows, LANES), 1)
    for j in range(2):
        key_bias[j] = jnp.where((row >= length) & (lane == HEAD * (1 - j)), NEG, 0.0).astype(BF16)

    for i in range(len(small)):
        fetch["v", i].wait()
    fetch["x"].wait()
    fetch["wq"].wait()
    fetch["wk"].wait()
    fetch["wv"].wait()
    def x_half(half):
        return lambda peer: x_buf.at[ds(peer * part, part), half]

    for kind, half in zip(x_kinds, halves):
        arrived(kind, x_half(half), flip(me, 1))
    qkv((me - core) * part, 1)
    kept = (resid.at[:pair], resid.at[pair : 2 * pair], xh1.at[:pair])
    for hi in range(2, group, 2):
        base = flip(me, hi) - core
        for c in range(2):
            arrived(x_kinds[0], x_half(halves[0]), base + c)
        qkv_first(base * part, halves[0], kept)
        for c in range(2):
            arrived(x_kinds[1], x_half(halves[1]), base + c)
        if hi == group - 2:
            cot_start(1)
        qkv(base * part, width // 256, halves[1], kept)

    score_refs, top_refs = (s_a, s_b), (top_a, top_b)

    def score(p, j):
        lanes = ds(p * LANES, LANES)
        half = lax.broadcasted_iota(jnp.int32, (rows, LANES), 1) < HEAD
        k_one = jnp.where(half if j == 0 else ~half, k_n[:, lanes], key_bias[j])
        q_one = q_t[ds(p * LANES + HEAD * j, HEAD), :]
        pad = [jnp.ones((16, rows), BF16), jnp.zeros((HEAD - 16, rows), BF16)]
        q_one = jnp.concatenate([q_one] + pad if j == 0 else pad + [q_one], 0)
        for c in range(0, rows, 256):
            cols = slice(c, c + 256)
            block = dot_nn(k_one, q_one[:, cols])
            score_refs[j][:, cols] = block
            top_refs[j][:, cols] = jnp.max(block, 0, keepdims=True)

    def exponential(h, j):
        for c in range(0, rows, 256):
            cols = slice(c, c + 256)
            probs[h, :, cols] = jnp.exp(score_refs[j][:, cols] - top_refs[j][:, cols]).astype(BF16)

    def weigh(h):
        feats = ds(h * HEAD, HEAD)
        o = dot_nn(jnp.concatenate([v_t[feats, :], jnp.ones((16, rows), BF16)], 0), probs[h])
        inv = 1.0 / o[HEAD : HEAD + 1]
        recip[pl.ds(h, 1), :] = inv
        ctx_t[feats, :] = (o[:HEAD] * inv).astype(BF16)

    def turn(p):
        lanes = ds(p * LANES, LANES)
        ctx_n[:, lanes] = ctx_t[lanes, :].T

    pairs = HEADS // 2
    for j in range(2):
        score(0, j)

    def attn_step(p, last=False):
        for j in range(2):
            exponential(2 * p + j, j)
        if not last:
            for j in range(2):
                score(p + 1, j)
        for j in range(2):
            weigh(2 * p + j)
        turn(p)

    loop(pairs - 1, attn_step, pairs - 1)
    attn_step(pairs - 1, last=True)

    cot_start(0)

    fetch["wo"].wait()

    def out_proj_step(i):
        part_rows = ds(i * 256, 256)
        ao = dot_nn(ctx_n[part_rows, :], wo[...]) + vecs[b_o]
        h = x_buf[part_rows, :].astype(F32) + ao
        center = h - jnp.mean(h, -1, keepdims=True)
        r = lax.rsqrt(jnp.mean(center * center, -1, keepdims=True) + EPSILON)
        xh = center * r
        xh1[part_rows, :] = xh
        rstd1[part_rows, :] = jnp.broadcast_to(r, (256, LANES))
        low[part_rows, :] = (xh * vecs[gain1] + vecs[shift1]).astype(BF16)

    loop(rows // 256, out_proj_step, rows // 256)

    fetch["we"].wait()
    fetch["be"].wait()

    def expand(i):
        cols = ds(i * 512, 512)
        s_a[...] = dot_nn(low[...], we[:, cols]) + vec_expand[:, cols]

    def gelu(i):
        cols = ds(i * 512, 512)
        f = s_a[...]
        t = f * (0.5**0.5)
        phi = 0.5 * lax.erf(t) + 0.5
        big_a[:, cols] = (f * phi).astype(BF16)
        bell = jnp.exp2(t * t * (-1.0 / math.log(2.0)))
        big_b[:, cols] = (phi + t * (1.0 / math.pi) ** 0.5 * bell).astype(BF16)

    expand(0)

    def expand_step(i):
        gelu(i)
        expand(i + 1)

    loop(ff // 512 - 1, expand_step, ff // 512 - 1)
    gelu(ff // 512 - 1)
    fetch["wc"].wait()

    def contract_step(i):
        cols = ds(i * 256, 256)
        n1 = xh1[:, cols] * vecs[gain1, :, cols] + vecs[shift1, :, cols]
        resid[:, cols] = n1 + dot_nn(big_a[...], wc[:, cols]) + vecs[b_c, :, cols]

    loop(width // 256, contract_step, width // 256)

    fetch["cot"].wait()
    for peer in members:
        arrived(1, block_of(cot_buf), peer)

    def norm2_step(i):
        part_rows = ds(i * 128, 128)
        h = resid[part_rows, :]
        center = h - jnp.mean(h, -1, keepdims=True)
        r = lax.rsqrt(jnp.mean(center * center, -1, keepdims=True) + EPSILON)
        xh = center * r
        ctx_n[part_rows, :] = (xh * vecs[gain2] + vecs[shift2]).astype(BF16)
        dy = cot_buf[part_rows, :].astype(F32)
        sums[s_ffn] += fold8(dy)
        e = dy * vecs[gain2]
        d = r * (e - jnp.mean(e, -1, keepdims=True) - xh * jnp.mean(e * xh, -1, keepdims=True))
        resid[part_rows, :] = d
        d_low = d.astype(BF16)
        low[part_rows, :] = d_low
        sums[s_contract] += fold8(d_low.astype(F32))

    loop(rows // 128, norm2_step, 2)

    send_out = exchange(2, block_of(ctx_n), out.at[me])
    for peer in by_core:
        send_out(peer).start()
    fetch_start("out", block_of(ctx_n)(me), out.at[me])

    def contract_back_step(i):
        cols = ds(i * 1024, 1024)
        df = (dot_nt(low[...], wc[cols, :]) * big_b[:, cols].astype(F32)).astype(BF16)
        big_b[:, cols] = df
        sum_expand[:, cols] += fold8(df.astype(F32))

    loop(ff // 1024, contract_back_step, ff // 1024)

    def expand_back_step(i):
        cols = ds(i * 256, 256)
        resid[:, cols] += dot_nt(big_b[...], we[cols, :])

    loop(width // 256, expand_back_step, width // 256)

    def norm1_step(i):
        part_rows = ds(i * 128, 128)
        dn = resid[part_rows, :]
        sums[s_attn] += fold8(dn)
        e = dn * vecs[gain1]
        xh = xh1[part_rows, :]
        r = rstd1[part_rows, :1]
        d = r * (e - jnp.mean(e, -1, keepdims=True) - xh * jnp.mean(e * xh, -1, keepdims=True))
        resid[part_rows, :] = d
        d_low = d.astype(BF16)
        low[part_rows, :] = d_low
        sums[s_output] += fold8(d_low.astype(F32))

    loop(rows // 128, norm1_step, 2)

    expand_rows = ff // width
    early = [s_ffn, s_contract, s_attn, s_output]

    partials, received = (red, red_late), (red_in, red_late_in)

    def send_partial(kind, slot, src, where):
        return pltpu.make_async_remote_copy(
            src_ref=partials[kind].at[src],
            dst_ref=received[kind].at[slot],
            send_sem=red_send.at[kind, slot],
            recv_sem=red_recv.at[kind, slot],
            device_id=where,
            device_id_type=MESH,
        )

    def round_copies(kind, which):
        if which == 0:
            return [send_partial(kind, j - 1, 0, {"seq": flip(me, j)}) for j in peers]
        first = len(peers) + sum(len(masks) for masks in rounds[: which - 1])
        return [
            send_partial(kind, first + i, which, {"dp": flip(dp, m)})
            for i, m in enumerate(rounds[which - 1])
        ]

    def reduce_start(kind, which=0):
        for copy in round_copies(kind, which):
            copy.start()

    def reduce_end(kind, which):
        for copy in round_copies(kind, which):
            copy.wait()
        first = len(peers) + sum(len(masks) for masks in rounds[: which - 1]) if which else 0
        count = len(peers) if which == 0 else len(rounds[which - 1])
        parts = [partials[kind][which]] + [received[kind][first + i] for i in range(count)]
        while len(parts) > 1:
            parts = [parts[i] + parts[i + 1] for i in range(0, len(parts), 2)]
        partials[kind][which + 1] = parts[0]
        if which < len(rounds):
            reduce_start(kind, which + 1)

    for i, which in enumerate(early):
        red[0, i : i + 1, :] = jnp.sum(sums[which], 0, keepdims=True)
    for i in range(expand_rows):
        red[0, 4 + i : 5 + i, :] = jnp.sum(
            sum_expand[:, i * width : (i + 1) * width], 0, keepdims=True
        )
    reduce_start(0)

    def ctx_back_step(i):
        feats = ds(i * 256, 256)
        v_t[feats, :] = dot_nt(wo[feats, :], low[...]).astype(BF16)

    loop(width // 256, ctx_back_step, width // 256)
    dq_n, dk_n, dv_n = (big_a.at[:, i * width : (i + 1) * width] for i in range(3))
    dscore_refs = tuple(cot_buf.at[:, i * rows : (i + 1) * rows] for i in range(2))
    turned_q, turned_k = (k_n.at[:LANES, i * rows : (i + 1) * rows] for i in range(2))

    def dscore(p, j):
        lanes = ds(p * LANES, LANES)
        feats = ds(p * LANES + HEAD * j, HEAD)
        d = v_t[feats, :].astype(F32) * recip[pl.ds(2 * p + j, 1), :]
        inner = jnp.sum(d * ctx_t[feats, :].astype(F32), 0, keepdims=True)
        d_low = d.astype(BF16)
        zeros = jnp.zeros((HEAD, rows), BF16)
        padded = jnp.concatenate([d_low, zeros] if j == 0 else [zeros, d_low], 0)
        dprobs = dot_nn(v_n[:, lanes], padded)
        dscore_refs[j][...] = (probs[2 * p + j].astype(F32) * (dprobs - inner)).astype(BF16)
        return padded

    def turn_back(p):
        lanes = ds(p * LANES, LANES)
        dq_low = turned_q[...].T
        dq_n[:, lanes] = dq_low
        dk_n[:, lanes] = turned_k[...].T
        sums[s_query, :, lanes] = fold8(dq_low.astype(F32))

    def attn_back_step(p):
        turn_back(lax.rem(p + pairs - 1, pairs))
        lanes = ds(p * LANES, LANES)
        dv = None
        for j in range(2):
            padded = dscore(p, j)
            term = dot_nn(probs[2 * p + j], padded.T)
            dv = term if dv is None else dv + term
        dv_low = dv.astype(BF16)
        dv_n[:, lanes] = dv_low
        sums[s_value, :, lanes] = fold8(dv_low.astype(F32))
        for j in range(2):
            feats, half = ds(p * LANES + HEAD * j, HEAD), slice(HEAD * j, HEAD * j + HEAD)
            dq = dot_nn(k_t[feats, :], dscore_refs[j][...]) * scale
            turned_q[half, :] = dq.astype(BF16)
            turned_k[half, :] = dot_nt(q_t[feats, :], dscore_refs[j][...]).astype(BF16)

    late = pairs - 2
    turned_q[...] = jnp.zeros_like(turned_q)
    turned_k[...] = jnp.zeros_like(turned_k)
    loop(late, attn_back_step, 3)
    reduce_end(0, 0)
    loop(2, lambda i: attn_back_step(late + i), 2)
    turn_back(pairs - 1)
    quarter = width // 4
    for i, which in enumerate((s_query, s_value)):
        for j in range(4):
            red_late[0, 4 * i + j : 4 * i + j + 1, :] = jnp.sum(
                sums[which, :, j * quarter : (j + 1) * quarter], 0, keepdims=True
            )
    reduce_start(1)

    def grad_step(base, cols):
        here = ds(base, pair)
        g = (
            resid[here, cols]
            + dot_nt(dq_n[here, :], wq[cols, :])
            + dot_nt(dk_n[here, :], wk[cols, :])
            + dot_nt(dv_n[here, :], wv[cols, :])
        )
        x_buf[here, cols] = g.astype(BF16)

    def grad_cols(cols):
        return lambda peer: x_buf.at[ds(peer * part, part), cols]

    def grad_home(cols):
        return lambda member: grad_in.at[member, :, cols]

    send_grad = [
        exchange(3 + i, grad_cols(cols), grad_home(cols)(me)) for i, cols in enumerate(grad_chunks)
    ]
    for hi in range(2, group, 2):
        base = flip(me, hi) - core
        for i, cols in enumerate(grad_chunks):
            grad_step(base * part, cols)
            for c in range(2):
                send_grad[i](base + c).start()
    reduce_end(1, 0)
    loop(width // 256, lambda i: grad_step((me - core) * part, ds(i * 256, 256)))
    for send in send_grad:
        send(flip(me, 1)).start()
    fetch_start("grad", x_buf.at[mine], grad_in.at[me])

    for which in range(1, len(rounds) + 1):
        for kind in range(2):
            reduce_end(kind, which)
    final = 1 + len(rounds)
    small_out[...] = red[final] * factor
    late_out[...] = red_late[final] * factor

    for peer in members:
        arrived(2, lambda member: out.at[member], peer)
        for i, cols in enumerate(grad_chunks):
            arrived(3 + i, grad_home(cols), peer)
    for send in send_x + [send_cot, send_out] + send_grad:
        for peer in members:
            send(peer).wait_send()
    fetch["out"].wait()
    fetch["grad"].wait()


def finish(
    early_out,
    early_grad,
    early_small,
    late_small,
    out,
    grad_in,
    g_bias_query,
    g_bias_value,
    g_bias_output,
    g_shift_attn,
    g_bias_expand,
    g_bias_contract,
    g_shift_ffn,
    row_buf,
    expand_buf,
    sem_out,
    sem_small,
):
    puts = [
        pltpu.make_async_copy(src.at[i], dst.at[i], sem_out.at[n * early_out.shape[0] + i])
        for n, (src, dst) in enumerate(((early_out, out), (early_grad, grad_in)))
        for i in range(early_out.shape[0])
    ]
    for put in puts:
        put.start()
    width = early_small.shape[-1]
    rows_out = (g_shift_ffn, g_bias_contract, g_shift_attn, g_bias_output)
    late_out = (g_bias_query, g_bias_value)
    for i in range(len(rows_out)):
        row_buf[i] = early_small[i : i + 1, :]
    for i in range(len(late_out)):
        for j in range(4):
            cols = slice(j * width // 4, (j + 1) * width // 4)
            row_buf[len(rows_out) + i, :, cols] = late_small[4 * i + j : 4 * i + j + 1, :]
    for i in range(g_bias_expand.shape[1] // width):
        expand_buf[:, i * width : (i + 1) * width] = early_small[4 + i : 5 + i, :]
    moves = [
        pltpu.make_async_copy(row_buf.at[i], ref, sem_small.at[i])
        for i, ref in enumerate(rows_out + late_out)
    ]
    moves.append(pltpu.make_async_copy(expand_buf, g_bias_expand, sem_small.at[len(moves)]))
    for move in moves:
        move.start()
    for move in moves + puts:
        move.wait()


def local(mesh, *args):
    hidden_in, lengths = args[:2]
    group, dp_size = mesh.shape["seq"], mesh.shape["dp"]
    seqs, part, width = hidden_in.shape
    ff = args[7].shape[1]
    rows = part * group
    assert seqs == group
    assert group & (group - 1) == 0 and dp_size & (dp_size - 1) == 0
    factor = (rows * seqs // group * dp_size * group) ** (-0.5)
    rounds = dp_rounds(dp_size)
    slots = group - 1 + sum(len(masks) for masks in rounds)
    anywhere = pl.BlockSpec(memory_space=pl.ANY)
    in_specs = [anywhere] * len(args)
    in_specs[1] = pl.BlockSpec(memory_space=pltpu.SMEM)
    vmem = pl.BlockSpec(memory_space=pltpu.VMEM)
    operands = [a.reshape(1, -1) if a.ndim == 1 and i != 1 else a for i, a in enumerate(args)]
    row = jax.ShapeDtypeStruct((1, width), F32)
    outs = pl.pallas_call(
        functools.partial(kernel, group, dp_size, factor),
        out_shape=[pltpu.VMEM(hidden_in.shape, BF16)] * 2
        + [pltpu.VMEM((8, width), F32), pltpu.VMEM((8, width // 4), F32)],
        in_specs=in_specs,
        out_specs=[vmem] * 4,
        scratch_shapes=[
            pltpu.VMEM((width, width), BF16),
            pltpu.VMEM((width, width), BF16),
            pltpu.VMEM((width, width), BF16),
            pltpu.VMEM((width, width), BF16),
            pltpu.VMEM((width, ff), BF16),
            pltpu.VMEM((ff, width), BF16),
            pltpu.VMEM((8, 1, width), F32),
            pltpu.VMEM((1, ff), F32),
            pltpu.VMEM((rows, width), BF16),
            pltpu.VMEM((rows, width), BF16),
            pltpu.VMEM((width, rows), BF16),
            pltpu.VMEM((rows, width), BF16),
            pltpu.VMEM((width, rows), BF16),
            pltpu.VMEM((rows, width), BF16),
            pltpu.VMEM((width, rows), BF16),
            pltpu.VMEM((HEADS, rows, rows), BF16),
            pltpu.VMEM((HEADS, rows), F32),
            pltpu.VMEM((width, rows), BF16),
            pltpu.VMEM((rows, width), BF16),
            pltpu.VMEM((rows, width), F32),
            pltpu.VMEM((rows, LANES), F32),
            pltpu.VMEM((rows, width), BF16),
            pltpu.VMEM((rows, ff), BF16),
            pltpu.VMEM((rows, ff), BF16),
            pltpu.VMEM((rows, width), F32),
            pltpu.VMEM((rows, rows), F32),
            pltpu.VMEM((rows, rows), F32),
            pltpu.VMEM((1, rows), F32),
            pltpu.VMEM((1, rows), F32),
            pltpu.VMEM((2, rows, LANES), BF16),
            pltpu.VMEM((6, 8, width), F32),
            pltpu.VMEM((8, ff), F32),
            pltpu.VMEM((2 + len(rounds), 8, width), F32),
            pltpu.VMEM((slots, 8, width), F32),
            pltpu.VMEM((2 + len(rounds), 8, width // 4), F32),
            pltpu.VMEM((slots, 8, width // 4), F32),
            pltpu.SemaphoreType.DMA((24,)),
            pltpu.SemaphoreType.DMA((4 + len(column_chunks(width)), group)),
            pltpu.SemaphoreType.DMA((4 + len(column_chunks(width)), group)),
            pltpu.SemaphoreType.DMA((2, slots)),
            pltpu.SemaphoreType.DMA((2, slots)),
        ],
        compiler_params=pltpu.CompilerParams(
            collective_id=0, has_side_effects=True, vmem_limit_bytes=64700000
        ),
        name="layer",
    )(*operands)
    outs = [pltpu.with_memory_space_constraint(o, pltpu.VMEM) for o in outs]
    blocks = 2 * seqs
    outs = pl.pallas_call(
        finish,
        out_shape=[jax.ShapeDtypeStruct(hidden_in.shape, BF16)] * 2
        + [row] * 4
        + [jax.ShapeDtypeStruct((1, ff), F32), row, row],
        in_specs=[vmem] * 4,
        out_specs=[anywhere] * 9,
        scratch_shapes=[
            pltpu.VMEM((6, 1, width), F32),
            pltpu.VMEM((1, ff), F32),
            pltpu.SemaphoreType.DMA((blocks,)),
            pltpu.SemaphoreType.DMA((7,)),
        ],
        compiler_params=pltpu.CompilerParams(vmem_limit_bytes=4 * 2**20),
        name="finish",
    )(*outs)
    return tuple(o.reshape(-1) if o.shape[0] == 1 else o for o in outs)


def solution(mesh):
    placed = (P("dp", "seq", None), P("dp")) + (P(),) * 15 + (P("dp", "seq", None),)
    return jax.shard_map(
        functools.partial(local, mesh),
        mesh=mesh,
        in_specs=placed,
        out_specs=(P("dp", "seq", None), P("dp", "seq", None), P(), P(), P(), P(), P(), P(), P()),
        check_vma=False,
    )
```
